256 devices in a mesh: dp: 64 (over y, z, core), tp: 4 (over x).
Axes of the slice: x: 4, y: 4, z: 8, core: 2. Of those that a mesh axis runs over, the one named last changes fastest.
Arguments:
- hidden: bfloat16 [128, 4096], P('dp'), may hold values from -6 to 6
- attention_norm_gain: bfloat16 [4096], replicated, may hold values from 0.5 to 1.5
- query_key_value_weight: bfloat16 [4096, 4, 1280], P('dp', 'tp'), may hold values from -0.09375 to 0.09375
- key_value_cache: bfloat16 [128, 2048, 4, 256], P('dp', None, 'tp'), may hold values from -6 to 6
- cache_fill_lengths: int32 [128], P('dp'), may hold values from 2 to 2048
- output_weight_frozen: bfloat16 [4, 1024, 4096], P('tp', None, 'dp'), may hold values from -0.09375 to 0.09375
- adapter_down_transposed: bfloat16 [64, 4, 1024], P(None, 'tp', 'dp'), may hold values from -0.09375 to 0.09375
- adapter_up_matrix: bfloat16 [64, 4, 1024], P(None, 'tp', 'dp'), may hold values from -0.75 to 0.75
- attention_rows: bfloat16 [32768, 4096], P('dp', 'tp'), may hold values from -6 to 6
- upstream: bfloat16 [32768, 4096], P('dp', 'tp'), may hold values from -6 to 6
- rewards: float32 [128], P('dp'), may hold values from 0 to 2
- prompt_group_index: int32 [128], P('dp'), may hold values from 0 to 31, as said below
- completion_live_lengths: int32 [128], P('dp'), may hold values from 1 to 256
Outputs:
- decoded: float32 [128, 4096], P('dp')
- adapted_output_rows: float32 [32768, 4096], P('dp', 'tp')
- grad_lora_a_t: float32 [64, 4, 1024], P(None, 'tp', 'dp')
- grad_lora_b: float32 [64, 4, 1024], P(None, 'tp', 'dp')
The draws below stay inside these ranges and needn't reach their ends.
Inputs may be any that keep to these rules, and one draw needn't show every extreme that they name: `prompt_group_index`: each prompt holds exactly 4 rollouts.
All inputs are finite; a program needn't handle non-finite values.
Results may differ from the reference program's by a relative error of at most 0.0041.
Values may be sent and summed in bfloat16 or wider, within the bound.
No kernel may reach another device: no remote copies, remote signals or barrier semaphores. Data moves between devices by JAX's collectives and lax.ppermute only.
A program may use at most 128 MiB of HBM per device.

```python
import math
import jax
import jax.numpy as jnp
from jax import lax

MODEL_WIDTH = 4096
HD = 128
HEADS_TP = 8
ADAPTER_RANK = 64
CTX = 2048
GROUP = 4
COMP = 256
ROLLOUTS = 128
GROUP_QUERY_DIMS = 1024
QKV_TP = 1280
SHARD_WIDTH = 1024
ROWS = 32768
N_TP = 4


def draw_prompt_group_index(key, part):
    order = jax.random.permutation(key, ROLLOUTS)
    return (order // GROUP).astype(jnp.int32)


def draw_query_key_value_weight(key, part):
    noise_key = jax.random.fold_in(key, 101)
    weight = jax.random.truncated_normal(noise_key, -6.0, 6.0, (MODEL_WIDTH, N_TP, QKV_TP), jnp.float32) / math.sqrt(MODEL_WIDTH)
    return weight.astype(jnp.bfloat16)


def draw_key_value_cache(key, part):
    cache = jax.random.truncated_normal(jax.random.fold_in(key, 202), -6.0, 6.0, (ROLLOUTS, CTX, N_TP, 2 * HD), jnp.float32)
    return cache.astype(jnp.bfloat16)


def set_ends(entries, rng, low, high):
    place = [jax.random.randint(jax.random.fold_in(rng, axis), (), 0, length) for axis, length in enumerate(entries.shape)]
    main_axis = entries.shape.index(max(entries.shape))
    neighbour = place[:main_axis] + [(place[main_axis] + 1) % entries.shape[main_axis]] + place[main_axis + 1:]
    return entries.at[tuple(place)].set(low).at[tuple(neighbour)].set(high)


def shard_levels(key, extent, cuts, least, high):
    def one(dim, shards_of):
        steps = jax.random.uniform(jax.random.fold_in(jax.random.fold_in(key, 6), dim), (shards_of,), jnp.float32, least / len(cuts), high / len(cuts))
        return jnp.repeat(jnp.exp(steps), extent[dim] // shards_of).reshape((-1,) + (1,) * (len(extent) - dim - 1))

    level = one(*cuts[0])
    for cut in cuts[1:]:
        level = level * one(*cut)
    return level


def gaussian(stream_key, shape, spread, bound, cuts=(), held_as=jnp.bfloat16):
    level = shard_levels(stream_key, shape, cuts, -0.22, 0.18) if cuts else 1.0
    array = jax.random.normal(stream_key, shape, jnp.float32) * spread * level
    return jnp.minimum(jnp.maximum(array, -bound), bound).astype(held_as)


def setup_inputs(seed: int = 0) -> dict:
    seeds = jax.random.split(jax.random.key(seed), 14)
    hidden = gaussian(seeds[0], (ROLLOUTS, MODEL_WIDTH), 1.0, 6.0, ((0, 64),))
    attention_norm_gain = jnp.clip(1.0 + 0.1 * jax.random.normal(seeds[1], (MODEL_WIDTH,), jnp.float32), 0.5, 1.5).astype(jnp.bfloat16)
    query_key_value_weight = draw_query_key_value_weight(jax.random.fold_in(seeds[13], 71), 0)
    key_value_cache = draw_key_value_cache(jax.random.fold_in(seeds[13], 71), 0)
    cache_fill_lengths = set_ends(jax.random.randint(seeds[4], (ROLLOUTS,), 2, CTX + 1), jax.random.fold_in(seeds[4], 1), 2, CTX).astype(jnp.int32)
    output_weight_frozen = gaussian(seeds[5], (N_TP, GROUP_QUERY_DIMS, MODEL_WIDTH), (GROUP_QUERY_DIMS * N_TP) ** -0.5, 0.09375, ((0, 4), (2, 64)))
    adapter_down_transposed = gaussian(seeds[6], (ADAPTER_RANK, N_TP, GROUP_QUERY_DIMS), (GROUP_QUERY_DIMS * N_TP) ** -0.5, 0.09375, ((1, 4), (2, 64)))
    adapter_up_matrix = gaussian(seeds[7], (ADAPTER_RANK, N_TP, SHARD_WIDTH), ADAPTER_RANK ** -0.5, 0.75, ((1, 4), (2, 64)))
    attention_rows = gaussian(seeds[8], (ROWS, GROUP_QUERY_DIMS * N_TP), 1.0, 6.0, ((0, 64), (1, 4)))
    upstream = gaussian(seeds[9], (ROWS, MODEL_WIDTH), 1.0, 6.0, ((0, 64), (1, 4)))
    rewards = jnp.clip(2.0 * jax.random.uniform(seeds[10], (ROLLOUTS,), jnp.float32) ** shard_levels(seeds[10], (ROLLOUTS,), ((0, 64),), -0.2, 0.2), 0.0, 2.0)
    prompt_group_index = draw_prompt_group_index(jax.random.fold_in(seeds[13], 71), 0)
    completion_live_lengths = set_ends(jax.random.randint(seeds[12], (ROLLOUTS,), 1, COMP + 1), jax.random.fold_in(seeds[12], 1), 1, COMP).astype(jnp.int32)
    return {"hidden": hidden, "attention_norm_gain": attention_norm_gain, "query_key_value_weight": query_key_value_weight, "key_value_cache": key_value_cache, "cache_fill_lengths": cache_fill_lengths, "output_weight_frozen": output_weight_frozen, "adapter_down_transposed": adapter_down_transposed, "adapter_up_matrix": adapter_up_matrix, "attention_rows": attention_rows, "upstream": upstream, "rewards": rewards, "prompt_group_index": prompt_group_index, "completion_live_lengths": completion_live_lengths}


adapter_scale = 2.0

def rms_norm(decode_state, gain):
    scale = lax.rsqrt(lax.optimization_barrier(jnp.mean(decode_state * decode_state, axis=-1, keepdims=True)) + 1e-05)
    return decode_state * scale * gain.astype(jnp.float32)

def one_rollout(packed):
    query, cache, length, new_keys, new_values = packed
    head = query.shape[-1]
    slots = cache.shape[0]
    factor = 1.0 / math.sqrt(head)
    q32 = query.astype(jnp.float32)
    keys = cache[:, :, :head].astype(jnp.float32)
    values = cache[:, :, head:].astype(jnp.float32)
    scores = jnp.einsum('thd,ctd->thc', q32, keys, precision=lax.Precision.HIGHEST) * factor
    valid = jnp.arange(slots) < length
    scores = jnp.where(valid[None, None, :], scores, -1e+30)
    extra = jnp.einsum('thd,etd->the', q32, new_keys.astype(jnp.float32), precision=lax.Precision.HIGHEST) * factor
    joined = jnp.concatenate([scores, extra], axis=-1)
    top = lax.optimization_barrier(jnp.max(joined, axis=-1, keepdims=True))
    expo = jnp.exp(joined - top)
    probs = (expo / lax.optimization_barrier(jnp.sum(expo, axis=-1, keepdims=True))).astype(jnp.bfloat16).astype(jnp.float32)
    out = jnp.einsum('thc,ctd->thd', probs[..., :slots], values, precision=lax.Precision.HIGHEST)
    out = out + jnp.einsum('the,etd->thd', probs[..., slots:], new_values.astype(jnp.float32), precision=lax.Precision.HIGHEST)
    return out.astype(jnp.bfloat16)

def reference(hidden, attention_norm_gain, query_key_value_weight, key_value_cache, cache_fill_lengths, output_weight_frozen, adapter_down_transposed, adapter_up_matrix, attention_rows, upstream, rewards, prompt_group_index, completion_live_lengths):
    rollouts = hidden.shape[0]
    w_qkv = query_key_value_weight.reshape(MODEL_WIDTH, N_TP * QKV_TP).astype(jnp.float32)
    w_out = output_weight_frozen.reshape(N_TP * GROUP_QUERY_DIMS, MODEL_WIDTH)
    down_matrix_full = adapter_down_transposed.reshape(ADAPTER_RANK, N_TP * GROUP_QUERY_DIMS)
    up_matrix_full = adapter_up_matrix.reshape(ADAPTER_RANK, MODEL_WIDTH)
    decode_state = hidden.astype(jnp.float32)
    keys_new = []
    values_new = []
    for step in range(2):
        normed = rms_norm(decode_state, attention_norm_gain)
        qkv = jnp.dot(normed, w_qkv, precision=lax.Precision.HIGHEST)
        qkv = qkv.reshape(rollouts, N_TP, QKV_TP)
        query = qkv[:, :, :GROUP_QUERY_DIMS].reshape(rollouts, N_TP, HEADS_TP, HD)
        keys_new.append(qkv[:, :, GROUP_QUERY_DIMS:GROUP_QUERY_DIMS + HD])
        values_new.append(qkv[:, :, GROUP_QUERY_DIMS + HD:])
        stacked_k = jnp.stack(keys_new, axis=1)
        stacked_v = jnp.stack(values_new, axis=1)
        attended = lax.map(one_rollout, (query, key_value_cache, cache_fill_lengths, stacked_k, stacked_v))
        attended = attended.reshape(rollouts, N_TP * GROUP_QUERY_DIMS)
        frozen_output = jnp.dot(attended, w_out, preferred_element_type=jnp.float32)
        low_rank_decode = jnp.dot(attended, down_matrix_full.T, preferred_element_type=jnp.float32)
        decode_state = decode_state + frozen_output + adapter_scale * jnp.dot(low_rank_decode, up_matrix_full.astype(jnp.float32), precision=lax.Precision.HIGHEST)
    decoded = decode_state
    groups = rollouts // GROUP
    onehot = (prompt_group_index[:, None] == jnp.arange(groups, dtype=jnp.int32)[None, :]).astype(jnp.float32)
    totals = lax.optimization_barrier(jnp.sum(onehot * rewards[:, None], axis=0))
    squares = lax.optimization_barrier(jnp.sum(onehot * (rewards * rewards)[:, None], axis=0))
    mean = totals / GROUP
    std = jnp.sqrt(jnp.maximum(squares / GROUP - mean * mean, 0.09))
    advantage = (rewards - lax.optimization_barrier(jnp.sum(onehot * mean[None, :], axis=1))) / lax.optimization_barrier(jnp.sum(onehot * std[None, :], axis=1))
    per_roll = advantage / completion_live_lengths.astype(jnp.float32)
    rows = attention_rows.shape[0]
    slot = jnp.arange(rows, dtype=jnp.int32) % COMP
    limit = jnp.repeat(completion_live_lengths, COMP)
    row_w = jnp.where(slot < limit, jnp.repeat(per_roll, COMP), 0.0)
    low_rank_rows = jnp.dot(attention_rows, down_matrix_full.T, preferred_element_type=jnp.float32).astype(jnp.bfloat16)
    frozen_output_rows = jnp.dot(attention_rows, w_out, preferred_element_type=jnp.float32)
    adapted_output_rows = frozen_output_rows + adapter_scale * jnp.dot(low_rank_rows, up_matrix_full, preferred_element_type=jnp.float32)
    advantage_weighted = (row_w[:, None] * upstream.astype(jnp.float32)).astype(jnp.bfloat16)
    backward_result = jnp.dot(advantage_weighted, up_matrix_full.T, preferred_element_type=jnp.float32).astype(jnp.bfloat16)
    down_gradient = adapter_scale * lax.dot_general(backward_result, attention_rows, (((0,), (0,)), ((), ())), preferred_element_type=jnp.float32)
    up_gradient = adapter_scale * lax.dot_general(low_rank_rows, advantage_weighted, (((0,), (0,)), ((), ())), preferred_element_type=jnp.float32)
    return (decoded, adapted_output_rows, down_gradient.reshape(ADAPTER_RANK, N_TP, GROUP_QUERY_DIMS), up_gradient.reshape(ADAPTER_RANK, N_TP, MODEL_WIDTH // N_TP))
```

```python
import math

import jax
import jax.numpy as jnp
from jax import lax
from jax.experimental import pallas as pl
from jax.experimental.pallas import tpu as pltpu
from jax.sharding import Mesh
from jax.sharding import PartitionSpec as P

HD = 128
HEADS_TP = 8
GROUP = 4
COMP = 256
QUERY = HEADS_TP * HD

adapter_scale = 2.0
f32 = jnp.float32
bf16 = jnp.bfloat16
CHIPS = ("y", "z")
DP = ("y", "z", "c")
HIGH = lax.Precision.HIGHEST


def nt_dot(a, b, precision=None):
    return lax.dot_general(
        a, b, (((1,), (1,)), ((), ())), preferred_element_type=f32, precision=precision
    )


def tn_dot(a, b):
    return lax.dot_general(a, b, (((0,), (0,)), ((), ())), preferred_element_type=f32)


def swapped(x):
    return lax.ppermute(x, "c", [(0, 1), (1, 0)])


def in_core_order(own, other, axis):
    first = lax.axis_index("c") == 0
    return jnp.where(
        first,
        jnp.concatenate([own, other], axis=axis),
        jnp.concatenate([other, own], axis=axis),
    )


def shift(x, by, n):
    return lax.ppermute(x, "t", [(i, (i + by) % n) for i in range(n)])


def exchange(x, axes):
    return lax.all_to_all(x, axes, split_axis=0, concat_axis=0, tiled=True)


def to_all(x, axes):
    return exchange(jnp.broadcast_to(x, (lax.axis_size(axes), *x.shape)), axes)


def summed_over_t(x):
    n = lax.axis_size("t")
    out = x
    for by in range(1, n):
        out = out + shift(x, by, n)
    return out


def attend(query, cache, lengths, new_keys, new_values):
    head = query.shape[-1]
    slots = cache.shape[1]
    factor = 1.0 / math.sqrt(head)
    keys = cache[:, :, :head].astype(f32)
    values = cache[:, :, head:]
    scores = jnp.einsum("bhd,bcd->bhc", query, keys, precision=HIGH) * factor
    valid = jnp.arange(slots, dtype=jnp.int32)[None, None, :] < lengths[:, None, None]
    scores = jnp.where(valid, scores, -1e30)
    extra = jnp.einsum("bhd,bed->bhe", query, new_keys, precision=HIGH) * factor
    joined = jnp.concatenate([scores, extra], axis=-1)
    top = jnp.max(joined, axis=-1, keepdims=True)
    expo = jnp.exp(joined - top)
    probs = (expo / jnp.sum(expo, axis=-1, keepdims=True)).astype(bf16)
    out = jnp.einsum("bhc,bcd->bhd", probs[..., :slots], values, preferred_element_type=f32)
    out = out + jnp.einsum(
        "bhe,bed->bhd", probs[..., slots:].astype(f32), new_values, precision=HIGH
    )
    return out.astype(bf16).reshape(query.shape[0], -1)


def rows_kernel(n, where_ref, own, left, right, far_a, far_b, w_ref, low, b_ref, out):
    half = far_a.shape[0]
    acc = adapter_scale * nt_dot(low[...], b_ref[...])
    acc = acc + nt_dot(own[...], w_ref[where_ref[0]])
    acc = acc + nt_dot(left[...], w_ref[where_ref[1]])
    acc = acc + nt_dot(right[...], w_ref[where_ref[3]])
    out[...] = acc
    far = w_ref[where_ref[2]]
    out[:half, :] += nt_dot(far_a[...], far)
    out[half:, :] += nt_dot(far_b[...], far)


def output_rows(where, own, left, right, far_a, far_b, w, low, b):
    n, width, depth = w.shape
    rows = own.shape[0]
    tile = 256
    whole = lambda a: pl.BlockSpec(a.shape, lambda j, s: (0, 0))
    return pl.pallas_call(
        lambda *refs: rows_kernel(n, *refs),
        out_shape=jax.ShapeDtypeStruct((rows, width), f32),
        grid_spec=pltpu.PrefetchScalarGridSpec(
            num_scalar_prefetch=1,
            grid=(width // tile,),
            in_specs=[
                whole(own),
                whole(left),
                whole(right),
                whole(far_a),
                whole(far_b),
                pl.BlockSpec((n, tile, depth), lambda j, s: (0, j, 0)),
                whole(low),
                pl.BlockSpec((tile, b.shape[1]), lambda j, s: (j, 0)),
            ],
            out_specs=pl.BlockSpec((rows, tile), lambda j, s: (0, j)),
        ),
        compiler_params=pltpu.CompilerParams(vmem_limit_bytes=40 << 20),
        cost_estimate=pl.CostEstimate(
            flops=2 * rows * width * depth * n,
            bytes_accessed=2 * (n * width * depth + n * rows * depth) + 4 * rows * width,
            transcendentals=0,
        ),
    )(where, own, left, right, far_a, far_b, w, low, b)


def shards(
    hidden,
    attention_norm_gain,
    query_key_value_weight,
    key_value_cache,
    cache_fill_lengths,
    output_weight_frozen,
    adapter_down_transposed,
    adapter_up_matrix,
    attention_rows,
    upstream,
    rewards,
    prompt_group_index,
    completion_live_lengths,
):
    nt = lax.axis_size("t")
    chips = lax.axis_size(CHIPS)
    t = lax.axis_index("t")
    y = lax.axis_index("y")
    z = lax.axis_index("z")
    m = lax.axis_index(CHIPS)
    rolls, width = hidden.shape
    shard_width = width // nt
    rank = adapter_up_matrix.shape[0]
    cols = width // chips
    cache = key_value_cache[:, :, 0, :]

    w_cols = output_weight_frozen[0].T
    ny = lax.axis_size("y")
    turned = lax.ppermute(
        w_cols, ("y", "t"), [(a * nt + b, b * nt + a) for a in range(ny) for b in range(nt)]
    )
    w_block = lax.all_gather(turned, DP, axis=0, tiled=True)
    w_block = w_block.reshape(nt, shard_width, w_cols.shape[1])

    half = attention_rows.shape[0] // 2
    left = shift(attention_rows, 1, nt)
    right = shift(attention_rows, nt - 1, nt)
    far_a = shift(left[:half], 1, nt)
    far_b = shift(right[half:], nt - 1, nt)

    w_rows = query_key_value_weight[:, 0, :]
    w_rows = in_core_order(w_rows, swapped(w_rows), 0).astype(f32)
    w_pair = in_core_order(w_cols, swapped(w_cols), 0)

    pieces = jnp.concatenate(
        [adapter_down_transposed[:, 0, :].T, adapter_up_matrix[:, 0, :].T], axis=1
    )
    high = lax.reduce_precision(rewards, 8, 7)
    mid = lax.reduce_precision(rewards - high, 8, 7)
    low_part = rewards - high - mid
    stats = jnp.concatenate([high, mid, low_part, prompt_group_index.astype(f32)]).astype(bf16)
    tail = jnp.pad(stats[None, :], ((0, 5), (0, 128 - stats.shape[0])))
    depth = pieces.shape[0]
    hid = hidden.reshape(rolls, chips, cols).transpose(1, 0, 2)
    message = jnp.concatenate(
        [
            jnp.broadcast_to(pieces, (chips, *pieces.shape)),
            hid,
            jnp.broadcast_to(tail, (chips, *tail.shape)),
        ],
        axis=1,
    )
    arrived = exchange(message, CHIPS)
    state = arrived[:, depth : depth + rolls, :].reshape(chips * rolls, cols).astype(f32)
    common = jnp.concatenate([arrived[:, :depth], arrived[:, depth + rolls :]], axis=1)
    common_other = swapped(common)
    own_pieces, other_pieces = common[:, None, :depth], common_other[:, None, :depth]
    both = in_core_order(own_pieces, other_pieces, 1).reshape(-1, 2 * rank)
    a_t = both[:, :rank]
    b_t = both[:, rank:]

    everyone = jnp.concatenate([common[:, depth], common_other[:, depth]], axis=0).astype(f32)
    values = (
        everyone[:, :rolls] + everyone[:, rolls : 2 * rolls] + everyone[:, 2 * rolls : 3 * rolls]
    )
    prompts = everyone[:, 3 * rolls : 4 * rolls]
    mine = (
        prompt_group_index.astype(f32)[:, None, None] == prompts[None, :, :]
    ).astype(f32)
    totals = jnp.sum(mine * values[None], axis=(1, 2))
    squares = jnp.sum(mine * (values * values)[None], axis=(1, 2))
    mean = totals / GROUP
    std = jnp.sqrt(jnp.maximum(squares / GROUP - mean * mean, 0.09))
    per_roll = (rewards - mean) / std / completion_live_lengths.astype(f32)
    rows = attention_rows.shape[0]
    index = lax.broadcasted_iota(jnp.int32, (rows, 1), 0)
    weight = jnp.zeros((rows, 1), f32)
    for r in range(rolls):
        slot = index - r * COMP
        inside = (slot >= 0) & (slot < COMP) & (slot < completion_live_lengths[r])
        weight = jnp.where(inside, per_roll[r], weight)
    weighted = (weight * upstream.astype(f32)).astype(bf16)

    low_part = jnp.dot(attention_rows, a_t, preferred_element_type=f32)
    back_part = jnp.dot(weighted, b_t, preferred_element_type=f32)
    b_slice = lax.dynamic_slice_in_dim(b_t, z * cols, cols, 0).astype(f32)
    b_slice = jnp.pad(b_slice, ((0, 0), (0, rank)))
    part = jnp.concatenate([low_part, back_part], axis=1)
    part = jnp.concatenate([part, b_slice], axis=0)
    by_shift = [part] + [shift(part, by, nt) for by in range(1, nt)]
    low_back = sum(p[:rows] for p in by_shift).astype(bf16)
    from_y = lax.rem(t - y + nt, nt)
    b_cols = by_shift[0][rows:, :rank]
    for by in range(1, nt):
        b_cols = jnp.where(from_y == by, by_shift[by][rows:, :rank], b_cols)
    low_rows = low_back[:, :rank]
    back_rows = low_back[:, rank:]
    grads = adapter_scale * jnp.concatenate(
        [tn_dot(back_rows, attention_rows), tn_dot(low_rows, weighted)], axis=0
    )

    gain = lax.dynamic_slice_in_dim(attention_norm_gain, m * cols, cols, 0).astype(f32)
    owned = hidden.astype(f32)
    keys_new = []
    values_new = []
    for step in range(2):
        partial_value = jnp.dot(state * gain[None, :], w_rows, precision=HIGH)
        partial_value = partial_value.reshape(chips, rolls, -1)
        if step:
            partial_value = jnp.concatenate(
                [partial_value, state.reshape(chips, rolls, cols)], axis=2
            )
        came = exchange(partial_value, CHIPS)
        qkv = came[:, :, : w_rows.shape[1]].sum(axis=0)
        if step:
            owned = came[:, :, w_rows.shape[1] :].transpose(1, 0, 2).reshape(rolls, width)
        scale = lax.rsqrt(jnp.mean(owned * owned, axis=-1, keepdims=True) + 1e-05)
        qkv = qkv * scale
        query = qkv[:, :QUERY].reshape(rolls, HEADS_TP, HD)
        keys_new.append(qkv[:, QUERY : QUERY + HD])
        values_new.append(qkv[:, QUERY + HD :])
        attended = attend(
            query,
            cache,
            cache_fill_lengths,
            jnp.stack(keys_new, axis=1),
            jnp.stack(values_new, axis=1),
        )
        if step == 0:
            everyones = to_all(attended, CHIPS).reshape(chips * rolls, -1)
            share = jnp.concatenate(
                [nt_dot(everyones, w_pair), jnp.dot(everyones, a_t, preferred_element_type=f32)],
                axis=1,
            )
            share = summed_over_t(share)
            state = (
                state
                + share[:, :cols]
                + adapter_scale * nt_dot(share[:, cols:], b_cols, precision=HIGH)
            )
        else:
            low_decode = jnp.dot(attended, a_t, preferred_element_type=f32)
            groups = to_all(jnp.concatenate([attended.astype(f32), low_decode], axis=1), "t")
            low_decode = groups[:, :, shard_width:].sum(axis=0)
            heads = groups[:, :, :shard_width].astype(bf16)
            update = adapter_scale * nt_dot(low_decode, b_t.astype(f32), precision=HIGH)
            for g in range(nt):
                update = update + nt_dot(heads[g], w_block[g])
            own_cols = lax.dynamic_slice_in_dim(owned, t * shard_width, shard_width, 1) + update
            decoded = to_all(own_cols, "t").transpose(1, 0, 2).reshape(rolls, width)

    tiles = grads.reshape(2 * rank, chips, 2, depth).transpose(2, 1, 0, 3)
    c = lax.axis_index("c")
    kept = lax.dynamic_index_in_dim(tiles, c, 0, keepdims=False)
    given = lax.dynamic_index_in_dim(tiles, 1 - c, 0, keepdims=False)
    kept = kept + swapped(given)
    kept = kept.reshape(chips, -1, 128)
    summed = exchange(kept, CHIPS).sum(axis=0).reshape(2 * rank, depth)

    where = lax.rem(t - jnp.arange(nt, dtype=jnp.int32) + nt, nt)
    adapted = output_rows(
        where, attention_rows, left, right, far_a, far_b, w_block, low_rows, b_t
    )
    return (decoded, adapted, summed[:rank, None, :], summed[rank:, None, :])


def solution(mesh):
    split = Mesh(mesh.devices.reshape(4, 8, 2, 4), ("y", "z", "c", "t"))
    placed = (
        P(DP, None),
        P(),
        P(DP, "t", None),
        P(DP, None, "t", None),
        P(DP),
        P("t", None, DP),
        P(None, "t", DP),
        P(None, "t", DP),
        P(DP, "t"),
        P(DP, "t"),
        P(DP),
        P(DP),
        P(DP),
    )
    return jax.shard_map(
        shards,
        mesh=split,
        in_specs=placed,
        out_specs=(P(DP, None), P(DP, "t"), P(None, "t", DP), P(None, "t", DP)),
        check_vma=False,
    )
```

```python
import math

import jax
import jax.numpy as jnp
from jax import lax
from jax.experimental import pallas as pl
from jax.experimental.pallas import tpu as pltpu
from jax.sharding import Mesh
from jax.sharding import PartitionSpec as P

HD = 128
HEADS_TP = 8
GROUP = 4
COMP = 256
RANK = 64
LANES = 128
ROLLS = 2
CHIP_COUNT = 32
PIECE = 16
FIRST_ROWS = 24
QKV_ROWS = 24
KEY_ROW = ROLLS * HEADS_TP
STATE_ROW = KEY_ROW + 2 * ROLLS

adapter_scale = 2.0
f32 = jnp.float32
bf16 = jnp.bfloat16
CHIPS = ("y", "z")
DP = ("y", "z", "c")
HIGH = lax.Precision.HIGHEST
VMEM = pl.BlockSpec(memory_space=pltpu.VMEM)
SMEM = pl.BlockSpec(memory_space=pltpu.SMEM)


def nn_dot(a, b):
    return jnp.dot(a, b, preferred_element_type=f32)


def nt_dot(a, b, precision=None):
    return lax.dot_general(
        a, b, (((1,), (1,)), ((), ())), preferred_element_type=f32, precision=precision
    )


def tn_dot(a, b):
    return lax.dot_general(a, b, (((0,), (0,)), ((), ())), preferred_element_type=f32)


def swapped(x):
    return lax.ppermute(x, "c", [(0, 1), (1, 0)])


def shift(x, by, n):
    return lax.ppermute(x, "t", [(i, (i + by) % n) for i in range(n)])


def shifts(x, n):
    return [x] + [shift(x, by, n) for by in range(1, n)]


def exchange(x, axes):
    return lax.all_to_all(x, axes, split_axis=0, concat_axis=0, tiled=True)


def to_all(x, axes):
    return exchange(jnp.broadcast_to(x, (lax.axis_size(axes), *x.shape)), axes)


def together(*xs):
    return lax.optimization_barrier(xs)


def lane_iota(shape):
    return lax.broadcasted_iota(jnp.int32, shape, len(shape) - 1)


def call(kernel, out, specs, args, scratch=(), flops=0, vmem=32):
    moved = sum(a.size * a.dtype.itemsize for a in args)
    outs = out if isinstance(out, tuple) else (out,)
    moved += sum(math.prod(o.shape) * o.dtype.itemsize for o in outs)
    return pl.pallas_call(
        kernel,
        out_shape=out,
        in_specs=specs,
        out_specs=tuple(VMEM for _ in outs) if isinstance(out, tuple) else VMEM,
        scratch_shapes=list(scratch),
        compiler_params=pltpu.CompilerParams(vmem_limit_bytes=vmem << 20),
        cost_estimate=pl.CostEstimate(flops=flops, bytes_accessed=moved, transcendentals=0),
    )(*args)


def shape(*dims, dtype=f32):
    return jax.ShapeDtypeStruct(dims, dtype)


def message_kernel(rewards, prompts, a_ref, b_ref, hidden, out):
    pieces = jnp.concatenate([a_ref[...], b_ref[...]], axis=1)
    out[:, :PIECE, :] = jnp.broadcast_to(pieces, (CHIP_COUNT, PIECE, LANES))
    lane = lane_iota((1, LANES))
    value = jnp.where(lane == 0, rewards[0], jnp.where(lane == 1, rewards[1], 0.0))
    prompt = jnp.where(lane == 0, prompts[0], jnp.where(lane == 1, prompts[1], 0)).astype(f32)
    high = value.astype(bf16).astype(f32)
    mid = (value - high).astype(bf16).astype(f32)
    low = value - high - mid
    tail = jnp.concatenate([high, mid, low, prompt, jnp.zeros((2, LANES), f32)], axis=0)
    for m in range(CHIP_COUNT):
        cut = hidden[:, m * LANES : (m + 1) * LANES].astype(f32)
        out[m, PIECE:, :] = jnp.concatenate([cut, tail], axis=0).astype(bf16)


def spread_qkv(state, gain, first, w_own, w_other, out):
    w_even = jnp.where(first, w_own[...], w_other[...])
    w_odd = jnp.where(first, w_other[...], w_own[...])
    w = jnp.concatenate([w_even, w_odd], axis=0)
    x = state * gain
    x1 = x.astype(bf16)
    rest = x - x1.astype(f32)
    x2 = rest.astype(bf16)
    x3 = (rest - x2.astype(f32)).astype(bf16)
    count = x.shape[0]
    parts = nn_dot(jnp.concatenate([x1, x2, x3], axis=0), w)
    qkv = parts[:count] + parts[count : 2 * count] + parts[2 * count :]

    def put(row, block):
        out[pl.ds(row, CHIP_COUNT, stride=QKV_ROWS), :] = block

    for b in range(ROLLS):
        mine = qkv[b * CHIP_COUNT : (b + 1) * CHIP_COUNT]
        for h in range(HEADS_TP):
            put(b * HEADS_TP + h, mine[:, h * HD : (h + 1) * HD])
        put(KEY_ROW + 2 * b, mine[:, HEADS_TP * HD : (HEADS_TP + 1) * HD])
        put(KEY_ROW + 2 * b + 1, mine[:, (HEADS_TP + 1) * HD :])
        put(STATE_ROW + b, state[b * CHIP_COUNT : (b + 1) * CHIP_COUNT])
    for row in range(STATE_ROW + ROLLS, QKV_ROWS):
        put(row, jnp.zeros((CHIP_COUNT, LANES), f32))


def qkv_first_kernel(place, arrived, gain, w_own, w_other, out, state_out, held):
    held[...] = arrived[...].astype(f32).reshape(CHIP_COUNT * FIRST_ROWS, LANES)
    state = jnp.concatenate(
        [held[pl.ds(PIECE + b, CHIP_COUNT, stride=FIRST_ROWS), :] for b in range(ROLLS)], axis=0
    )
    state_out[...] = state
    spread_qkv(state, gain[...], place[0] == 0, w_own, w_other, out)


def qkv_later_kernel(place, state, gain, w_own, w_other, b_cols, s0, s1, s2, s3, out):
    share = s0[...] + s1[...] + s2[...] + s3[...]
    low = share[:, LANES:]
    now = (
        state[...]
        + share[:, :LANES]
        + adapter_scale * nt_dot(low, b_cols[...], precision=HIGH)
    )
    spread_qkv(now, gain[...], place[0] == 0, w_own, w_other, out)


def attend_kernel(last, lengths, came, cache, before, ab, attended, kv_out, owned_out, held):
    sums = jnp.sum(came[...].reshape(CHIP_COUNT, QKV_ROWS, LANES), axis=0)
    factor = 1.0 / math.sqrt(HD)
    width = CHIP_COUNT * LANES
    rows = []
    lows = []
    kvs = []
    for b in range(ROLLS):
        owned = came[pl.ds(STATE_ROW + b, CHIP_COUNT, stride=QKV_ROWS), :]
        owned_out[b * CHIP_COUNT : (b + 1) * CHIP_COUNT, :] = owned
        total = jnp.sum(jnp.sum(owned * owned, axis=0, keepdims=True), axis=1, keepdims=True)
        scale = lax.rsqrt(total * (1.0 / width) + 1e-05)
        query = sums[b * HEADS_TP : (b + 1) * HEADS_TP] * scale
        fresh = sums[KEY_ROW + 2 * b : KEY_ROW + 2 * b + 2] * scale
        kvs.append(fresh)
        q1 = query.astype(bf16)
        rest = query - q1.astype(f32)
        q2 = rest.astype(bf16)
        q3 = (rest - q2.astype(f32)).astype(bf16)
        keys = cache[b, :, :HD]
        parts = nt_dot(jnp.concatenate([q1, q2, q3], axis=0), keys)
        scores = (parts[:HEADS_TP] + parts[HEADS_TP : 2 * HEADS_TP] + parts[2 * HEADS_TP :]) * factor
        scores = jnp.where(lane_iota(scores.shape) < lengths[b], scores, -1e30)
        newest = [(fresh[0:1], fresh[1:2])]
        if last:
            newest = [(before[2 * b : 2 * b + 1], before[2 * b + 1 : 2 * b + 2])] + newest
        extra = [jnp.sum(query * k, axis=1, keepdims=True) * factor for k, _ in newest]
        top = jnp.max(scores, axis=1, keepdims=True)
        for e in extra:
            top = jnp.maximum(top, e)
        expo = jnp.exp(scores - top)
        total = jnp.sum(expo, axis=1, keepdims=True)
        more = [jnp.exp(e - top) for e in extra]
        for e in more:
            total = total + e
        out = nn_dot((expo / total).astype(bf16), cache[b, :, HD:])
        for e, (_, v) in zip(more, newest):
            out = out + (e / total).astype(bf16).astype(f32) * v
        out = out.astype(bf16)
        rows.append(out)
        if last:
            flat = out.astype(f32)
            lows.append(
                jnp.concatenate([flat[h : h + 1] for h in range(HEADS_TP)], axis=1)
            )
    both = jnp.concatenate([r.astype(f32) for r in rows], axis=0)
    if last:
        low = jnp.concatenate(lows + [jnp.zeros((8 - ROLLS, HEADS_TP * HD), f32)], axis=0)
        low = nn_dot(low.astype(bf16), ab[...])
        attended[...] = jnp.concatenate([both, low], axis=0)
    else:
        attended[...] = both.astype(bf16)
    kv_out[...] = jnp.concatenate(kvs + [jnp.zeros((8 - 2 * ROLLS, LANES), f32)], axis=0)


def attend(last, lengths, came, cache, before, ab):
    att = shape(24, LANES) if last else shape(ROLLS * HEADS_TP, LANES, dtype=bf16)
    return call(
        lambda *refs: attend_kernel(last, *refs),
        (att, shape(8, LANES), shape(ROLLS * CHIP_COUNT, LANES)),
        [SMEM, VMEM, VMEM, VMEM, VMEM],
        (lengths, came, cache, before, ab),
        scratch=[pltpu.VMEM((8, LANES), f32)],
        flops=2 * 32 * 2 * cache.shape[0] * cache.shape[1] * HD,
    )


def close_kernel(place, came, w_own, w_other, ab, out, held):
    rows = ROLLS * HEADS_TP
    held[...] = came[...].astype(f32).reshape(CHIP_COUNT * rows, LANES)
    blocks = []
    for b in range(ROLLS):
        heads = [
            held[pl.ds(b * HEADS_TP + h, CHIP_COUNT, stride=rows), :] for h in range(HEADS_TP)
        ]
        blocks.append(jnp.concatenate(heads, axis=1))
    everyone = jnp.concatenate(blocks, axis=0).astype(bf16)
    first = place[0] == 0
    w_even = jnp.where(first, w_own[...], w_other[...])
    w_odd = jnp.where(first, w_other[...], w_own[...])
    w = jnp.concatenate([w_even, w_odd], axis=0)
    out[:, :LANES] = nt_dot(everyone, w)
    out[:, LANES:] = nn_dot(everyone, ab[...])


def adapter_kernel(
    place, rewards, prompts, live, own, other, rows, upstream, weighted_out, ab_out, part
):
    first = place[0] == 0
    even = jnp.where(first, own[...], other[...])
    odd = jnp.where(first, other[...], own[...])
    ab_out[:, :PIECE, :] = even[:, :PIECE]
    ab_out[:, PIECE:, :] = odd[:, :PIECE]
    lane = lane_iota((CHIP_COUNT, LANES))
    seen = []
    for side in (own, other):
        tail = side[:, PIECE:, :].astype(f32)
        seen.append((tail[:, 2, :] + tail[:, 3, :] + tail[:, 4, :], tail[:, 5, :]))
    count = rows.shape[0]
    index = lax.broadcasted_iota(jnp.int32, (count, 1), 0)
    weight = jnp.zeros((count, 1), f32)
    for b in range(ROLLS):
        total = jnp.zeros((1, 1), f32)
        squares = jnp.zeros((1, 1), f32)
        for value, prompt in seen:
            hit = (prompt == prompts[b].astype(f32)) & (lane < ROLLS)
            value = jnp.where(hit, value, 0.0)
            total = total + jnp.sum(jnp.sum(value, axis=0, keepdims=True), axis=1, keepdims=True)
            value = value * value
            squares = squares + jnp.sum(
                jnp.sum(value, axis=0, keepdims=True), axis=1, keepdims=True
            )
        mean = total / GROUP
        std = jnp.sqrt(jnp.maximum(squares / GROUP - mean * mean, 0.09))
        per_roll = (rewards[b] - mean) / std / live[b].astype(f32)
        slot = index - b * COMP
        inside = (slot >= 0) & (slot < COMP) & (slot < live[b])
        weight = jnp.where(inside, per_roll, weight)
    weighted = (weight * upstream[...].astype(f32)).astype(bf16)
    weighted_out[...] = weighted
    ab = ab_out[...].reshape(2 * CHIP_COUNT * PIECE, LANES)
    low = nn_dot(rows[...], ab)
    back = nn_dot(weighted, ab)
    part[:count, :] = jnp.where(lane_iota((count, LANES)) < RANK, low, back)
    z = place[2]
    each = LANES // (2 * PIECE)
    piece = ab_out[pl.ds(z * each, each), :, :].reshape(LANES, LANES).astype(f32)
    piece = pltpu.roll(piece, RANK, 1)
    part[count:, :] = jnp.where(lane_iota((LANES, LANES)) < RANK, piece, 0.0)


def gradient_kernel(
    place, p0, p1, p2, p3, rows, weighted, low_back, b_cols, kept, given
):
    count = rows.shape[0]
    total = p0[:count, :] + p1[:count, :] + p2[:count, :] + p3[:count, :]
    low_back[...] = total.astype(bf16)
    turned = pltpu.roll(total, RANK, 1).astype(bf16)
    from_y = place[3]
    piece = p0[count:, :]
    for by, p in ((1, p1), (2, p2), (3, p3)):
        piece = jnp.where(from_y == by, p[count:, :], piece)
    b_cols[...] = piece
    a_side = tn_dot(rows[...], turned)
    b_side = tn_dot(weighted[...], turned)
    both = adapter_scale * jnp.where(lane_iota(a_side.shape) < RANK, a_side, b_side)
    both = both.reshape(CHIP_COUNT, 2 * PIECE, LANES)
    even, odd = both[:, :PIECE], both[:, PIECE:]
    first = place[0] == 0
    kept[...] = jnp.where(first, even, odd)
    given[...] = jnp.where(first, odd, even)


def rows_kernel(
    where_ref, own, left, right, far_a, far_b, w_ref, low, b_ref, s0, s1, s2, s3, owned, out, cols
):
    half = far_a.shape[0]
    b_tile = b_ref[...]
    mine = lane_iota(b_tile.shape) >= RANK
    b_tile = jnp.where(mine, b_tile, jnp.zeros_like(b_tile))
    b_turned = pltpu.roll(b_tile.astype(f32), RANK, 1)
    acc = adapter_scale * nt_dot(low[...], b_turned.astype(bf16))
    acc = acc + nt_dot(own[...], w_ref[where_ref[0]])
    acc = acc + nt_dot(left[...], w_ref[where_ref[1]])
    acc = acc + nt_dot(right[...], w_ref[where_ref[3]])
    out[...] = acc
    far = w_ref[where_ref[2]]
    out[:half, :] += nt_dot(far_a[...], far)
    out[half:, :] += nt_dot(far_b[...], far)
    top = ROLLS * HEADS_TP
    low_sum = s0[top:, :] + s1[top:, :] + s2[top:, :] + s3[top:, :]
    got = adapter_scale * nt_dot(low_sum, b_turned, precision=HIGH)
    for k, s in enumerate((s0, s1, s2, s3)):
        flat = [
            jnp.concatenate(
                [s[b * HEADS_TP + h : b * HEADS_TP + h + 1, :] for h in range(HEADS_TP)], axis=1
            )
            for b in range(ROLLS)
        ]
        flat.append(jnp.zeros((8 - ROLLS, HEADS_TP * HD), f32))
        heads = jnp.concatenate(flat, axis=0).astype(bf16)
        got = got + nt_dot(heads, w_ref[where_ref[k]])
    cols[...] = got[:ROLLS, :] + owned[...]


def output_rows(where, own, left, right, far_a, far_b, w, low, b, sent, owned):
    n, width, depth = w.shape
    rows = own.shape[0]
    tile = 256
    tiles = width // tile
    whole = lambda a: pl.BlockSpec(a.shape, lambda j, s: (0, 0))
    return pl.pallas_call(
        rows_kernel,
        out_shape=(shape(rows, width), shape(ROLLS, width)),
        grid_spec=pltpu.PrefetchScalarGridSpec(
            num_scalar_prefetch=1,
            grid=(tiles,),
            in_specs=[
                whole(own),
                whole(left),
                whole(right),
                whole(far_a),
                whole(far_b),
                pl.BlockSpec((n, tile, depth), lambda j, s: (0, j, 0)),
                whole(low),
                pl.BlockSpec((tile, b.shape[1]), lambda j, s: (j, 0)),
                *(whole(s) for s in sent),
                pl.BlockSpec((ROLLS, tile), lambda j, s: (0, s[0] * tiles + j)),
            ],
            out_specs=(
                pl.BlockSpec((rows, tile), lambda j, s: (0, j)),
                pl.BlockSpec((ROLLS, tile), lambda j, s: (0, j)),
            ),
        ),
        compiler_params=pltpu.CompilerParams(vmem_limit_bytes=40 << 20),
        cost_estimate=pl.CostEstimate(
            flops=2 * rows * width * depth * n,
            bytes_accessed=2 * (n * width * depth + n * rows * depth) + 4 * rows * width,
            transcendentals=0,
        ),
    )(where, own, left, right, far_a, far_b, w, low, b, *sent, owned)


def shards(
    hidden,
    attention_norm_gain,
    query_key_value_weight,
    key_value_cache,
    cache_fill_lengths,
    output_weight_frozen,
    adapter_down_transposed,
    adapter_up_matrix,
    attention_rows,
    upstream,
    rewards,
    prompt_group_index,
    completion_live_lengths,
):
    nt = lax.axis_size("t")
    t = lax.axis_index("t")
    y = lax.axis_index("y")
    z = lax.axis_index("z")
    c = lax.axis_index("c")
    m = lax.axis_index(CHIPS)
    width = hidden.shape[1]
    shard_width = width // nt
    cache = key_value_cache[:, :, 0, :]
    place = jnp.stack([c, y, z, lax.rem(t - y + nt, nt)]).astype(jnp.int32)
    where = lax.rem(t - jnp.arange(nt, dtype=jnp.int32) + nt, nt)

    message = call(
        message_kernel,
        shape(CHIP_COUNT, FIRST_ROWS, LANES, dtype=bf16),
        [SMEM, SMEM, VMEM, VMEM, VMEM],
        (
            rewards,
            prompt_group_index,
            adapter_down_transposed[:, 0, :].T,
            adapter_up_matrix[:, 0, :].T,
            hidden,
        ),
    )

    w_cols = output_weight_frozen[0].T
    ny = lax.axis_size("y")
    turned = lax.ppermute(
        w_cols, ("y", "t"), [(a * nt + b, b * nt + a) for a in range(ny) for b in range(nt)]
    )
    w_block = lax.all_gather(turned, DP, axis=0, tiled=True)
    w_block = w_block.reshape(nt, shard_width, w_cols.shape[1])

    left = shift(attention_rows, 1, nt)
    right = shift(attention_rows, nt - 1, nt)
    w_rows = query_key_value_weight[:, 0, :]
    w_rows_other = swapped(w_rows)
    w_cols_other = swapped(w_cols)

    arrived = exchange(message, CHIPS)
    gain = lax.dynamic_slice_in_dim(attention_norm_gain, m * LANES, LANES, 0).astype(f32)[None, :]
    sent, state = call(
        qkv_first_kernel,
        (shape(CHIP_COUNT * QKV_ROWS, LANES), shape(ROLLS * CHIP_COUNT, LANES)),
        [SMEM] + [VMEM] * 4,
        (place, arrived, gain, w_rows, w_rows_other),
        scratch=[pltpu.VMEM((CHIP_COUNT * FIRST_ROWS, LANES), f32)],
    )
    arrived_other = swapped(arrived)
    sent, arrived, arrived_other = together(sent, arrived, arrived_other)
    came = exchange(sent.reshape(CHIP_COUNT, QKV_ROWS, LANES), CHIPS)

    rows = attention_rows.shape[0]
    weighted, ab, part = call(
        adapter_kernel,
        (
            shape(rows, shard_width, dtype=bf16),
            shape(CHIP_COUNT, 2 * PIECE, LANES, dtype=bf16),
            shape(rows + LANES, LANES),
        ),
        [SMEM] * 4 + [VMEM] * 4,
        (
            place,
            rewards,
            prompt_group_index,
            completion_live_lengths,
            arrived,
            arrived_other,
            attention_rows,
            upstream,
        ),
        flops=4 * rows * shard_width * LANES,
    )
    ab = ab.reshape(shard_width, LANES)
    parts = shifts(part, nt)

    nothing = jnp.zeros((8, LANES), f32)
    attended, kv, _ = attend(
        False, cache_fill_lengths, came.reshape(-1, LANES), cache, nothing, ab
    )
    attended, *parts = together(attended, *parts)
    everyone = to_all(attended, CHIPS)

    low_back, b_cols, kept, given = call(
        gradient_kernel,
        (
            shape(rows, LANES, dtype=bf16),
            shape(LANES, LANES),
            shape(CHIP_COUNT, PIECE, LANES),
            shape(CHIP_COUNT, PIECE, LANES),
        ),
        [SMEM] + [VMEM] * 6,
        (place, *parts, attention_rows, weighted),
        flops=4 * rows * shard_width * LANES,
    )

    share = call(
        close_kernel,
        shape(ROLLS * CHIP_COUNT, 2 * LANES),
        [SMEM] + [VMEM] * 4,
        (place, everyone, w_cols, w_cols_other, ab),
        scratch=[pltpu.VMEM((CHIP_COUNT * ROLLS * HEADS_TP, LANES), f32)],
    )
    share, given, kept = together(share, given, kept)
    shares = shifts(share, nt)
    kept = kept + swapped(given)
    summed = exchange(kept, CHIPS)

    sent = call(
        qkv_later_kernel,
        shape(CHIP_COUNT * QKV_ROWS, LANES),
        [SMEM] + [VMEM] * 9,
        (place, state, gain, w_rows, w_rows_other, b_cols, *shares),
    )
    sent, left, right = together(sent, left, right)
    came = exchange(sent.reshape(CHIP_COUNT, QKV_ROWS, LANES), CHIPS)
    half = rows // 2
    far_a = shift(left[:half], 1, nt)
    far_b = shift(right[half:], nt - 1, nt)
    summed = summed.sum(axis=0)

    attended, _, owned = attend(True, cache_fill_lengths, came.reshape(-1, LANES), cache, kv, ab)
    adapted, own_cols = output_rows(
        where,
        attention_rows,
        left,
        right,
        far_a,
        far_b,
        w_block,
        low_back,
        ab,
        shifts(attended, nt),
        owned.reshape(ROLLS, width),
    )
    decoded = to_all(own_cols, "t").transpose(1, 0, 2).reshape(ROLLS, width)
    grad_a = summed[:, :RANK].T[:, None, :]
    grad_b = summed[:, RANK:].T[:, None, :]
    return (decoded, adapted, grad_a, grad_b)


def solution(mesh):
    split = Mesh(mesh.devices.reshape(4, 8, 2, 4), ("y", "z", "c", "t"))
    placed = (
        P(DP, None),
        P(),
        P(DP, "t", None),
        P(DP, None, "t", None),
        P(DP),
        P("t", None, DP),
        P(None, "t", DP),
        P(None, "t", DP),
        P(DP, "t"),
        P(DP, "t"),
        P(DP),
        P(DP),
        P(DP),
    )
    return jax.shard_map(
        shards,
        mesh=split,
        in_specs=placed,
        out_specs=(P(DP, None), P(DP, "t"), P(None, "t", DP), P(None, "t", DP)),
        check_vma=False,
    )
```

```python
import math

import jax
import jax.numpy as jnp
from jax import lax
from jax.experimental import pallas as pl
from jax.experimental.pallas import tpu as pltpu
from jax.sharding import Mesh
from jax.sharding import PartitionSpec as P

HD = 128
HEADS_TP = 8
GROUP = 4
COMP = 256
RANK = 64
LANES = 128
ROLLS = 2
CHIP_COUNT = 32
PIECE = 16
FIRST_ROWS = 24
QKV_ROWS = 24
KEY_ROW = ROLLS * HEADS_TP
STATE_ROW = KEY_ROW + 2 * ROLLS

adapter_scale = 2.0
f32 = jnp.float32
bf16 = jnp.bfloat16
CHIPS = ("y", "z")
DP = ("y", "z", "c")
HIGH = lax.Precision.HIGHEST
VMEM = pl.BlockSpec()
SMEM = pl.BlockSpec(memory_space=pltpu.SMEM)


def nn_dot(a, b):
    return jnp.dot(a, b, preferred_element_type=f32)


def nt_dot(a, b, precision=None):
    return lax.dot_general(
        a, b, (((1,), (1,)), ((), ())), preferred_element_type=f32, precision=precision
    )


def tn_dot(a, b):
    return lax.dot_general(a, b, (((0,), (0,)), ((), ())), preferred_element_type=f32)


def swapped(x):
    return lax.ppermute(x, "c", [(0, 1), (1, 0)])


def shift(x, by, n):
    return lax.ppermute(x, "t", [(i, (i + by) % n) for i in range(n)])


def shifts(x, n):
    return [x] + [shift(x, by, n) for by in range(1, n)]


def exchange(x, axes):
    return lax.all_to_all(x, axes, split_axis=0, concat_axis=0, tiled=True)


def to_all(x, axes):
    return exchange(jnp.broadcast_to(x, (lax.axis_size(axes), *x.shape)), axes)


def together(*xs):
    return lax.optimization_barrier(xs)


def lane_iota(shape):
    return lax.broadcasted_iota(jnp.int32, shape, len(shape) - 1)


def call(kernel, out, specs, args, scratch=(), flops=0, vmem=32):
    moved = sum(a.size * a.dtype.itemsize for a in args)
    outs = out if isinstance(out, tuple) else (out,)
    moved += sum(math.prod(o.shape) * o.dtype.itemsize for o in outs)
    return pl.pallas_call(
        kernel,
        out_shape=out,
        in_specs=specs,
        out_specs=tuple(VMEM for _ in outs) if isinstance(out, tuple) else VMEM,
        scratch_shapes=list(scratch),
        compiler_params=pltpu.CompilerParams(vmem_limit_bytes=vmem << 20),
        cost_estimate=pl.CostEstimate(flops=flops, bytes_accessed=moved, transcendentals=0),
    )(*args)


def shape(*dims, dtype=f32):
    return jax.ShapeDtypeStruct(dims, dtype)


def message_kernel(rewards, prompts, a_ref, b_ref, hidden, out):
    pieces = jnp.concatenate([a_ref[...], b_ref[...]], axis=1)
    out[:, :PIECE, :] = jnp.broadcast_to(pieces, (CHIP_COUNT, PIECE, LANES))
    lane = lane_iota((1, LANES))
    value = jnp.where(lane == 0, rewards[0], jnp.where(lane == 1, rewards[1], 0.0))
    prompt = jnp.where(lane == 0, prompts[0], jnp.where(lane == 1, prompts[1], 0)).astype(f32)
    high = value.astype(bf16).astype(f32)
    mid = (value - high).astype(bf16).astype(f32)
    low = value - high - mid
    tail = jnp.concatenate([high, mid, low, prompt, jnp.zeros((2, LANES), f32)], axis=0)
    for m in range(CHIP_COUNT):
        cut = hidden[:, m * LANES : (m + 1) * LANES].astype(f32)
        out[m, PIECE:, :] = jnp.concatenate([cut, tail], axis=0).astype(bf16)


def spread_qkv(state, gain, first, w_own, w_other, out):
    w_even = jnp.where(first, w_own[...], w_other[...])
    w_odd = jnp.where(first, w_other[...], w_own[...])
    w = jnp.concatenate([w_even, w_odd], axis=0)
    x = state * gain
    x1 = x.astype(bf16)
    rest = x - x1.astype(f32)
    x2 = rest.astype(bf16)
    x3 = (rest - x2.astype(f32)).astype(bf16)
    count = x.shape[0]
    parts = nn_dot(jnp.concatenate([x1, x2, x3], axis=0), w)
    qkv = parts[:count] + parts[count : 2 * count] + parts[2 * count :]

    def put(row, block):
        out[pl.ds(row, CHIP_COUNT, stride=QKV_ROWS), :] = block

    for b in range(ROLLS):
        mine = qkv[b * CHIP_COUNT : (b + 1) * CHIP_COUNT]
        for h in range(HEADS_TP):
            put(b * HEADS_TP + h, mine[:, h * HD : (h + 1) * HD])
        put(KEY_ROW + 2 * b, mine[:, HEADS_TP * HD : (HEADS_TP + 1) * HD])
        put(KEY_ROW + 2 * b + 1, mine[:, (HEADS_TP + 1) * HD :])
        put(STATE_ROW + b, state[b * CHIP_COUNT : (b + 1) * CHIP_COUNT])
    for row in range(STATE_ROW + ROLLS, QKV_ROWS):
        put(row, jnp.zeros((CHIP_COUNT, LANES), f32))


def qkv_first_kernel(place, arrived, gain, w_own, w_other, out, state_out, held):
    held[...] = arrived[...].astype(f32).reshape(CHIP_COUNT * FIRST_ROWS, LANES)
    state = jnp.concatenate(
        [held[pl.ds(PIECE + b, CHIP_COUNT, stride=FIRST_ROWS), :] for b in range(ROLLS)], axis=0
    )
    state_out[...] = state
    spread_qkv(state, gain[...], place[0] == 0, w_own, w_other, out)


def qkv_later_kernel(place, state, gain, w_own, w_other, b_cols, s0, s1, s2, s3, out):
    share = s0[...] + s1[...] + s2[...] + s3[...]
    low = share[:, LANES:]
    now = (
        state[...]
        + share[:, :LANES]
        + adapter_scale * nt_dot(low, b_cols[...], precision=HIGH)
    )
    spread_qkv(now, gain[...], place[0] == 0, w_own, w_other, out)


def attend_kernel(last, lengths, came, cache, before, ab, attended, kv_out, owned_out, held):
    sums = jnp.sum(came[...].reshape(CHIP_COUNT, QKV_ROWS, LANES), axis=0)
    factor = 1.0 / math.sqrt(HD)
    width = CHIP_COUNT * LANES
    rows = []
    lows = []
    kvs = []
    for b in range(ROLLS):
        owned = came[pl.ds(STATE_ROW + b, CHIP_COUNT, stride=QKV_ROWS), :]
        owned_out[b * CHIP_COUNT : (b + 1) * CHIP_COUNT, :] = owned
        total = jnp.sum(jnp.sum(owned * owned, axis=0, keepdims=True), axis=1, keepdims=True)
        scale = lax.rsqrt(total * (1.0 / width) + 1e-05)
        query = sums[b * HEADS_TP : (b + 1) * HEADS_TP] * scale
        fresh = sums[KEY_ROW + 2 * b : KEY_ROW + 2 * b + 2] * scale
        kvs.append(fresh)
        q1 = query.astype(bf16)
        rest = query - q1.astype(f32)
        q2 = rest.astype(bf16)
        q3 = (rest - q2.astype(f32)).astype(bf16)
        keys = cache[b, :, :HD]
        parts = nt_dot(jnp.concatenate([q1, q2, q3], axis=0), keys)
        scores = (parts[:HEADS_TP] + parts[HEADS_TP : 2 * HEADS_TP] + parts[2 * HEADS_TP :]) * factor
        scores = jnp.where(lane_iota(scores.shape) < lengths[b], scores, -1e30)
        newest = [(fresh[0:1], fresh[1:2])]
        if last:
            newest = [(before[2 * b : 2 * b + 1], before[2 * b + 1 : 2 * b + 2])] + newest
        extra = [jnp.sum(query * k, axis=1, keepdims=True) * factor for k, _ in newest]
        top = jnp.max(scores, axis=1, keepdims=True)
        for e in extra:
            top = jnp.maximum(top, e)
        expo = jnp.exp(scores - top)
        total = jnp.sum(expo, axis=1, keepdims=True)
        more = [jnp.exp(e - top) for e in extra]
        for e in more:
            total = total + e
        out = nn_dot((expo / total).astype(bf16), cache[b, :, HD:])
        for e, (_, v) in zip(more, newest):
            out = out + (e / total).astype(bf16).astype(f32) * v
        out = out.astype(bf16)
        rows.append(out)
        if last:
            flat = out.astype(f32)
            lows.append(
                jnp.concatenate([flat[h : h + 1] for h in range(HEADS_TP)], axis=1)
            )
    both = jnp.concatenate([r.astype(f32) for r in rows], axis=0)
    if last:
        low = jnp.concatenate(lows + [jnp.zeros((8 - ROLLS, HEADS_TP * HD), f32)], axis=0)
        low = nn_dot(low.astype(bf16), ab[...])
        attended[...] = jnp.concatenate([both, low], axis=0)
    else:
        attended[...] = both.astype(bf16)
    kv_out[...] = jnp.concatenate(kvs + [jnp.zeros((8 - 2 * ROLLS, LANES), f32)], axis=0)


def attend(last, lengths, came, cache, before, ab):
    att = shape(24, LANES) if last else shape(ROLLS * HEADS_TP, LANES, dtype=bf16)
    return call(
        lambda *refs: attend_kernel(last, *refs),
        (att, shape(8, LANES), shape(ROLLS * CHIP_COUNT, LANES)),
        [SMEM, VMEM, VMEM, VMEM, VMEM],
        (lengths, came, cache, before, ab),
        scratch=[pltpu.VMEM((8, LANES), f32)],
        flops=2 * 32 * 2 * cache.shape[0] * cache.shape[1] * HD,
    )


def close_kernel(place, came, w_own, w_other, ab, out, held):
    rows = ROLLS * HEADS_TP
    held[...] = came[...].astype(f32).reshape(CHIP_COUNT * rows, LANES)
    blocks = []
    for b in range(ROLLS):
        heads = [
            held[pl.ds(b * HEADS_TP + h, CHIP_COUNT, stride=rows), :] for h in range(HEADS_TP)
        ]
        blocks.append(jnp.concatenate(heads, axis=1))
    everyone = jnp.concatenate(blocks, axis=0).astype(bf16)
    first = place[0] == 0
    w_even = jnp.where(first, w_own[...], w_other[...])
    w_odd = jnp.where(first, w_other[...], w_own[...])
    w = jnp.concatenate([w_even, w_odd], axis=0)
    out[:, :LANES] = nt_dot(everyone, w)
    out[:, LANES:] = nn_dot(everyone, ab[...])


def adapter_kernel(
    place, rewards, prompts, live, own, other, rows, upstream, weighted_out, ab_out, part
):
    first = place[0] == 0
    even = jnp.where(first, own[...], other[...])
    odd = jnp.where(first, other[...], own[...])
    ab_out[:, :PIECE, :] = even[:, :PIECE]
    ab_out[:, PIECE:, :] = odd[:, :PIECE]
    lane = lane_iota((CHIP_COUNT, LANES))
    seen = []
    for side in (own, other):
        tail = side[:, PIECE:, :].astype(f32)
        seen.append((tail[:, 2, :] + tail[:, 3, :] + tail[:, 4, :], tail[:, 5, :]))
    count = rows.shape[0]
    index = lax.broadcasted_iota(jnp.int32, (count, 1), 0)
    weight = jnp.zeros((count, 1), f32)
    for b in range(ROLLS):
        total = jnp.zeros((1, 1), f32)
        squares = jnp.zeros((1, 1), f32)
        for value, prompt in seen:
            hit = (prompt == prompts[b].astype(f32)) & (lane < ROLLS)
            value = jnp.where(hit, value, 0.0)
            total = total + jnp.sum(jnp.sum(value, axis=0, keepdims=True), axis=1, keepdims=True)
            value = value * value
            squares = squares + jnp.sum(
                jnp.sum(value, axis=0, keepdims=True), axis=1, keepdims=True
            )
        mean = total / GROUP
        std = jnp.sqrt(jnp.maximum(squares / GROUP - mean * mean, 0.09))
        per_roll = (rewards[b] - mean) / std / live[b].astype(f32)
        slot = index - b * COMP
        inside = (slot >= 0) & (slot < COMP) & (slot < live[b])
        weight = jnp.where(inside, per_roll, weight)
    weighted = (weight * upstream[...].astype(f32)).astype(bf16)
    weighted_out[...] = weighted
    ab = ab_out[...].reshape(2 * CHIP_COUNT * PIECE, LANES)
    low = nn_dot(rows[...], ab)
    back = nn_dot(weighted, ab)
    part[:count, :] = jnp.where(lane_iota((count, LANES)) < RANK, low, back)
    z = place[2]
    each = LANES // (2 * PIECE)
    piece = ab_out[pl.ds(z * each, each), :, :].reshape(LANES, LANES).astype(f32)
    piece = pltpu.roll(piece, RANK, 1)
    part[count:, :] = jnp.where(lane_iota((LANES, LANES)) < RANK, piece, 0.0)


def gradient_kernel(
    place, p0, p1, p2, p3, rows, weighted, low_back, b_cols, kept, given
):
    count = rows.shape[0]
    total = p0[:count, :] + p1[:count, :] + p2[:count, :] + p3[:count, :]
    low_back[...] = total.astype(bf16)
    turned = pltpu.roll(total, RANK, 1).astype(bf16)
    from_y = place[3]
    piece = p0[count:, :]
    for by, p in ((1, p1), (2, p2), (3, p3)):
        piece = jnp.where(from_y == by, p[count:, :], piece)
    b_cols[...] = piece
    a_side = tn_dot(rows[...], turned)
    b_side = tn_dot(weighted[...], turned)
    both = adapter_scale * jnp.where(lane_iota(a_side.shape) < RANK, a_side, b_side)
    both = both.reshape(CHIP_COUNT, 2 * PIECE, LANES)
    even, odd = both[:, :PIECE], both[:, PIECE:]
    first = place[0] == 0
    kept[...] = jnp.where(first, even, odd)
    given[...] = jnp.where(first, odd, even)


def rows_kernel(
    where_ref, own, left, right, far_a, far_b, w_ref, low, b_ref, s0, s1, s2, s3, owned, out, cols, x
):
    rows = own.shape[0]
    half = far_a.shape[0]
    sent = (s0, s1, s2, s3)

    @pl.when(pl.program_id(0) == 0)
    def _():
        x[0, :rows, :] = own[...]
        x[1, :rows, :] = left[...]
        x[2, :half, :] = far_a[...]
        x[2, half:rows, :] = far_b[...]
        x[3, :rows, :] = right[...]
        for k, s in enumerate(sent):
            flat = [
                jnp.concatenate(
                    [s[b * HEADS_TP + h : b * HEADS_TP + h + 1, :] for h in range(HEADS_TP)],
                    axis=1,
                )
                for b in range(ROLLS)
            ]
            flat.append(jnp.zeros((16 - ROLLS, HEADS_TP * HD), f32))
            x[k, rows:, :] = jnp.concatenate(flat, axis=0).astype(bf16)

    b_tile = b_ref[...]
    mine = lane_iota(b_tile.shape) >= RANK
    b_tile = jnp.where(mine, b_tile, jnp.zeros_like(b_tile))
    b_turned = pltpu.roll(b_tile.astype(f32), RANK, 1)
    acc = nt_dot(x[0], w_ref[where_ref[0]])
    for k in range(1, len(sent)):
        acc = acc + nt_dot(x[k], w_ref[where_ref[k]])
    out[...] = acc[:rows] + adapter_scale * nt_dot(low[...], b_turned.astype(bf16))
    top = ROLLS * HEADS_TP
    low_sum = s0[top:, :] + s1[top:, :] + s2[top:, :] + s3[top:, :]
    got = adapter_scale * nt_dot(low_sum, b_turned, precision=HIGH)
    got = got[:ROLLS, :] + acc[rows : rows + ROLLS] + owned[...]
    cols[...] = jnp.broadcast_to(got, cols.shape)


def output_rows(where, own, left, right, far_a, far_b, w, low, b, sent, owned):
    n, width, depth = w.shape
    rows = own.shape[0]
    tile = 256
    tiles = width // tile
    whole = lambda a: pl.BlockSpec(a.shape, lambda j, s: (0, 0))
    return pl.pallas_call(
        rows_kernel,
        out_shape=(shape(rows, width), shape(n, ROLLS, width)),
        grid_spec=pltpu.PrefetchScalarGridSpec(
            num_scalar_prefetch=1,
            grid=(tiles,),
            in_specs=[
                whole(own),
                whole(left),
                whole(right),
                whole(far_a),
                whole(far_b),
                pl.BlockSpec((n, tile, depth), lambda j, s: (0, j, 0)),
                whole(low),
                pl.BlockSpec((tile, b.shape[1]), lambda j, s: (j, 0)),
                *(whole(s) for s in sent),
                pl.BlockSpec((ROLLS, tile), lambda j, s: (0, s[0] * tiles + j)),
            ],
            out_specs=(
                pl.BlockSpec((rows, tile), lambda j, s: (0, j)),
                pl.BlockSpec((n, ROLLS, tile), lambda j, s: (0, 0, j)),
            ),
            scratch_shapes=[pltpu.VMEM((n, rows + 16, depth), bf16)],
        ),
        compiler_params=pltpu.CompilerParams(vmem_limit_bytes=40 << 20),
        cost_estimate=pl.CostEstimate(
            flops=2 * rows * width * depth * n,
            bytes_accessed=2 * (n * width * depth + n * rows * depth) + 4 * rows * width,
            transcendentals=0,
        ),
    )(where, own, left, right, far_a, far_b, w, low, b, *sent, owned)


def shards(
    hidden,
    attention_norm_gain,
    query_key_value_weight,
    key_value_cache,
    cache_fill_lengths,
    output_weight_frozen,
    adapter_down_transposed,
    adapter_up_matrix,
    attention_rows,
    upstream,
    rewards,
    prompt_group_index,
    completion_live_lengths,
):
    nt = lax.axis_size("t")
    t = lax.axis_index("t")
    y = lax.axis_index("y")
    z = lax.axis_index("z")
    c = lax.axis_index("c")
    m = lax.axis_index(CHIPS)
    width = hidden.shape[1]
    shard_width = width // nt
    cache = key_value_cache[:, :, 0, :]
    place = jnp.stack([c, y, z, lax.rem(t - y + nt, nt)]).astype(jnp.int32)
    where = lax.rem(t - jnp.arange(nt, dtype=jnp.int32) + nt, nt)

    message = call(
        message_kernel,
        shape(CHIP_COUNT, FIRST_ROWS, LANES, dtype=bf16),
        [SMEM, SMEM, VMEM, VMEM, VMEM],
        (
            rewards,
            prompt_group_index,
            adapter_down_transposed[:, 0, :].T,
            adapter_up_matrix[:, 0, :].T,
            hidden,
        ),
    )

    w_rows = query_key_value_weight[:, 0, :]
    w_rows_other = swapped(w_rows)
    w_cols = output_weight_frozen[0].T
    w_cols_other = swapped(w_cols)

    ny = lax.axis_size("y")
    turned = lax.ppermute(
        w_cols, ("y", "t"), [(a * nt + b, b * nt + a) for a in range(ny) for b in range(nt)]
    )
    turned, message = together(turned, message)
    w_block = lax.all_gather(turned, DP, axis=0, tiled=True)
    w_block = w_block.reshape(nt, shard_width, w_cols.shape[1])

    left = shift(attention_rows, 1, nt)
    right = shift(attention_rows, nt - 1, nt)

    arrived = exchange(message, CHIPS)
    gain = lax.dynamic_slice_in_dim(attention_norm_gain, m * LANES, LANES, 0).astype(f32)[None, :]
    sent, state = call(
        qkv_first_kernel,
        (shape(CHIP_COUNT * QKV_ROWS, LANES), shape(ROLLS * CHIP_COUNT, LANES)),
        [SMEM] + [VMEM] * 4,
        (place, arrived, gain, w_rows, w_rows_other),
        scratch=[pltpu.VMEM((CHIP_COUNT * FIRST_ROWS, LANES), f32)],
    )
    arrived_other = swapped(arrived)
    sent, arrived, arrived_other, left, right = together(
        sent, arrived, arrived_other, left, right
    )
    came = exchange(sent.reshape(CHIP_COUNT, QKV_ROWS, LANES), CHIPS)

    rows = attention_rows.shape[0]
    weighted, ab, part = call(
        adapter_kernel,
        (
            shape(rows, shard_width, dtype=bf16),
            shape(CHIP_COUNT, 2 * PIECE, LANES, dtype=bf16),
            shape(rows + LANES, LANES),
        ),
        [SMEM] * 4 + [VMEM] * 4,
        (
            place,
            rewards,
            prompt_group_index,
            completion_live_lengths,
            arrived,
            arrived_other,
            attention_rows,
            upstream,
        ),
        flops=4 * rows * shard_width * LANES,
    )
    ab = ab.reshape(shard_width, LANES)
    parts = shifts(part, nt)

    nothing = jnp.zeros((8, LANES), f32)
    attended, kv, _ = attend(
        False, cache_fill_lengths, came.reshape(-1, LANES), cache, nothing, ab
    )
    attended, weighted, left, right = together(attended, weighted, left, right)
    half = rows // 2
    far_a = shift(left[:half], 1, nt)
    far_b = shift(right[half:], nt - 1, nt)
    everyone = to_all(attended, CHIPS)

    low_back, b_cols, kept, given = call(
        gradient_kernel,
        (
            shape(rows, LANES, dtype=bf16),
            shape(LANES, LANES),
            shape(CHIP_COUNT, PIECE, LANES),
            shape(CHIP_COUNT, PIECE, LANES),
        ),
        [SMEM] + [VMEM] * 6,
        (place, *parts, attention_rows, weighted),
        flops=4 * rows * shard_width * LANES,
    )

    share = call(
        close_kernel,
        shape(ROLLS * CHIP_COUNT, 2 * LANES),
        [SMEM] + [VMEM] * 4,
        (place, everyone, w_cols, w_cols_other, ab),
        scratch=[pltpu.VMEM((CHIP_COUNT * ROLLS * HEADS_TP, LANES), f32)],
    )
    share, given, kept = together(share, given, kept)
    shares = shifts(share, nt)
    kept = kept + swapped(given)

    sent = call(
        qkv_later_kernel,
        shape(CHIP_COUNT * QKV_ROWS, LANES),
        [SMEM] + [VMEM] * 9,
        (place, state, gain, w_rows, w_rows_other, b_cols, *shares),
    )
    came = exchange(sent.reshape(CHIP_COUNT, QKV_ROWS, LANES), CHIPS)

    attended, _, owned = attend(True, cache_fill_lengths, came.reshape(-1, LANES), cache, kv, ab)
    attended, kept = together(attended, kept)
    summed = exchange(kept, CHIPS)
    adapted, own_cols = output_rows(
        where,
        attention_rows,
        left,
        right,
        far_a,
        far_b,
        w_block,
        low_back,
        ab,
        shifts(attended, nt),
        owned.reshape(ROLLS, width),
    )
    own_cols, summed = together(own_cols, summed)
    summed = summed.sum(axis=0)
    decoded = exchange(own_cols, "t").transpose(1, 0, 2).reshape(ROLLS, width)
    grad_a = summed[:, :RANK].T[:, None, :]
    grad_b = summed[:, RANK:].T[:, None, :]
    return (decoded, adapted, grad_a, grad_b)


def solution(mesh):
    split = Mesh(mesh.devices.reshape(4, 8, 2, 4), ("y", "z", "c", "t"))
    placed = (
        P(DP, None),
        P(),
        P(DP, "t", None),
        P(DP, None, "t", None),
        P(DP),
        P("t", None, DP),
        P(None, "t", DP),
        P(None, "t", DP),
        P(DP, "t"),
        P(DP, "t"),
        P(DP),
        P(DP),
        P(DP),
    )
    return jax.shard_map(
        shards,
        mesh=split,
        in_specs=placed,
        out_specs=(P(DP, None), P(DP, "t"), P(None, "t", DP), P(None, "t", DP)),
        check_vma=False,
    )
```

```python
import math

import jax
import jax.numpy as jnp
from jax import lax
from jax.experimental import pallas as pl
from jax.experimental.pallas import tpu as pltpu
from jax.sharding import Mesh
from jax.sharding import PartitionSpec as P

HD = 128
HEADS_TP = 8
GROUP = 4
COMP = 256
RANK = 64
LANES = 128
ROLLS = 2
CHIP_COUNT = 32
PIECE = 16
FIRST_ROWS = 24
QKV_ROWS = 24
KEY_ROW = ROLLS * HEADS_TP
STATE_ROW = KEY_ROW + 2 * ROLLS
GRANT = 56
SMALL_GRANT = 24
MID_GRANT = 60
DECODE_HINT = 1

adapter_scale = 2.0
f32 = jnp.float32
bf16 = jnp.bfloat16
CHIPS = ("y", "z")
DP = ("y", "z", "c")
HIGH = lax.Precision.HIGHEST
HBM = pltpu.HBM
SMEM = pltpu.SMEM
ANY = pl.ANY


def nn_dot(a, b):
    return jnp.dot(a, b, preferred_element_type=f32)


def nt_dot(a, b, precision=None):
    return lax.dot_general(
        a, b, (((1,), (1,)), ((), ())), preferred_element_type=f32, precision=precision
    )


def tn_dot(a, b):
    return lax.dot_general(a, b, (((0,), (0,)), ((), ())), preferred_element_type=f32)


def swapped(x):
    return lax.ppermute(x, "c", [(0, 1), (1, 0)])


def shift(x, by, n):
    return lax.ppermute(x, "t", [(i, (i + by) % n) for i in range(n)])


def shifts(x, n):
    return [x] + [shift(x, by, n) for by in range(1, n)]


def exchange(x, axes):
    return lax.all_to_all(x, axes, split_axis=0, concat_axis=0, tiled=True)


def to_all(x, axes):
    return exchange(jnp.broadcast_to(x, (lax.axis_size(axes), *x.shape)), axes)


def together(*xs):
    return lax.optimization_barrier(xs)


def lane_iota(shape):
    return lax.broadcasted_iota(jnp.int32, shape, len(shape) - 1)


def call(kernel, out, specs, args, scratch=(), flops=0, grant=GRANT):
    moved = sum(a.size * a.dtype.itemsize for a in args)
    outs = out if isinstance(out, tuple) else (out,)
    moved += sum(math.prod(o.shape) * o.dtype.itemsize for o in outs)
    in_hbm = [i for i, kind in enumerate(specs) if kind != SMEM]
    n_in, n_out = len(specs), len(outs)
    buffers = [pltpu.VMEM(args[i].shape, args[i].dtype) for i in in_hbm]
    buffers += [pltpu.VMEM(o.shape, o.dtype) for o in outs]

    def body(*refs):
        ins, results, rest = refs[:n_in], refs[n_in : n_in + n_out], refs[n_in + n_out :]
        held, rest = rest[: len(buffers)], rest[len(buffers) :]
        sem, rest = rest[0], rest[1:]
        copies = [
            pltpu.make_async_copy(ins[i], held[k], sem.at[k]) for k, i in enumerate(in_hbm)
        ]
        for copy in copies:
            copy.start()
        for copy in copies:
            copy.wait()
        given = list(ins)
        for k, i in enumerate(in_hbm):
            given[i] = held[k]
        made = held[len(in_hbm) :]
        kernel(*given, *made, *rest)
        copies = [
            pltpu.make_async_copy(made[k], results[k], sem.at[len(in_hbm) + k])
            for k in range(n_out)
        ]
        for copy in copies:
            copy.start()
        for copy in copies:
            copy.wait()

    hbm = pl.BlockSpec(memory_space=HBM)
    return pl.pallas_call(
        body,
        out_shape=out,
        in_specs=[pl.BlockSpec(memory_space=kind) for kind in specs],
        out_specs=tuple(hbm for _ in outs) if isinstance(out, tuple) else hbm,
        scratch_shapes=[*buffers, pltpu.SemaphoreType.DMA((len(buffers),)), *scratch],
        compiler_params=pltpu.CompilerParams(vmem_limit_bytes=grant << 20),
        cost_estimate=pl.CostEstimate(
            flops=flops, bytes_accessed=moved, transcendentals=0
        ),
    )(*args)


def shape(*dims, dtype=f32):
    return jax.ShapeDtypeStruct(dims, dtype)


def message_kernel(rewards, prompts, a_ref, b_ref, hidden, out):
    pieces = jnp.concatenate([a_ref[...], b_ref[...]], axis=1)
    out[:, :PIECE, :] = jnp.broadcast_to(pieces, (CHIP_COUNT, PIECE, LANES))
    lane = lane_iota((1, LANES))
    value = jnp.where(lane == 0, rewards[0], jnp.where(lane == 1, rewards[1], 0.0))
    prompt = jnp.where(lane == 0, prompts[0], jnp.where(lane == 1, prompts[1], 0)).astype(f32)
    high = value.astype(bf16).astype(f32)
    mid = (value - high).astype(bf16).astype(f32)
    low = value - high - mid
    tail = jnp.concatenate([high, mid, low, prompt, jnp.zeros((2, LANES), f32)], axis=0)
    for m in range(CHIP_COUNT):
        cut = hidden[:, m * LANES : (m + 1) * LANES].astype(f32)
        out[m, PIECE:, :] = jnp.concatenate([cut, tail], axis=0).astype(bf16)


def spread_qkv(state, gain, first, w_own, w_other, out):
    w_even = jnp.where(first, w_own[...], w_other[...])
    w_odd = jnp.where(first, w_other[...], w_own[...])
    w = jnp.concatenate([w_even, w_odd], axis=0)
    x = state * gain
    x1 = x.astype(bf16)
    rest = x - x1.astype(f32)
    x2 = rest.astype(bf16)
    x3 = (rest - x2.astype(f32)).astype(bf16)
    count = x.shape[0]
    parts = nn_dot(jnp.concatenate([x1, x2, x3], axis=0), w)
    qkv = parts[:count] + parts[count : 2 * count] + parts[2 * count :]

    def put(row, block):
        out[pl.ds(row, CHIP_COUNT, stride=QKV_ROWS), :] = block

    for b in range(ROLLS):
        mine = qkv[b * CHIP_COUNT : (b + 1) * CHIP_COUNT]
        for h in range(HEADS_TP):
            put(b * HEADS_TP + h, mine[:, h * HD : (h + 1) * HD])
        put(KEY_ROW + 2 * b, mine[:, HEADS_TP * HD : (HEADS_TP + 1) * HD])
        put(KEY_ROW + 2 * b + 1, mine[:, (HEADS_TP + 1) * HD :])
        put(STATE_ROW + b, state[b * CHIP_COUNT : (b + 1) * CHIP_COUNT])
    for row in range(STATE_ROW + ROLLS, QKV_ROWS):
        put(row, jnp.zeros((CHIP_COUNT, LANES), f32))


def gain_of(place, gain):
    start = pl.multiple_of(place[4] * LANES, LANES)
    return gain[:, pl.ds(start, LANES)].astype(f32)


def qkv_first_kernel(place, arrived, gain, w_own, w_other, out, state_out, held):
    held[...] = arrived[...].astype(f32).reshape(CHIP_COUNT * FIRST_ROWS, LANES)
    state = jnp.concatenate(
        [held[pl.ds(PIECE + b, CHIP_COUNT, stride=FIRST_ROWS), :] for b in range(ROLLS)], axis=0
    )
    state_out[...] = state
    spread_qkv(state, gain_of(place, gain), place[0] == 0, w_own, w_other, out)


def qkv_later_kernel(place, state, gain, w_own, w_other, b_cols, s0, s1, s2, s3, out):
    share = s0[...] + s1[...] + s2[...] + s3[...]
    low = share[:, LANES:]
    now = (
        state[...]
        + share[:, :LANES]
        + adapter_scale * nt_dot(low, b_cols[...], precision=HIGH)
    )
    spread_qkv(now, gain_of(place, gain), place[0] == 0, w_own, w_other, out)


def attend_kernel(last, lengths, came, cache, before, ab, attended, kv_out, owned_out, held):
    sums = jnp.sum(came[...].reshape(CHIP_COUNT, QKV_ROWS, LANES), axis=0)
    factor = 1.0 / math.sqrt(HD)
    width = CHIP_COUNT * LANES
    rows = []
    lows = []
    kvs = []
    for b in range(ROLLS):
        owned = came[pl.ds(STATE_ROW + b, CHIP_COUNT, stride=QKV_ROWS), :]
        owned_out[b * CHIP_COUNT : (b + 1) * CHIP_COUNT, :] = owned
        total = jnp.sum(jnp.sum(owned * owned, axis=0, keepdims=True), axis=1, keepdims=True)
        scale = lax.rsqrt(total * (1.0 / width) + 1e-05)
        query = sums[b * HEADS_TP : (b + 1) * HEADS_TP] * scale
        fresh = sums[KEY_ROW + 2 * b : KEY_ROW + 2 * b + 2] * scale
        kvs.append(fresh)
        q1 = query.astype(bf16)
        rest = query - q1.astype(f32)
        q2 = rest.astype(bf16)
        q3 = (rest - q2.astype(f32)).astype(bf16)
        keys = cache[b, :, :HD]
        parts = nt_dot(jnp.concatenate([q1, q2, q3], axis=0), keys)
        scores = (parts[:HEADS_TP] + parts[HEADS_TP : 2 * HEADS_TP] + parts[2 * HEADS_TP :]) * factor
        scores = jnp.where(lane_iota(scores.shape) < lengths[b], scores, -1e30)
        newest = [(fresh[0:1], fresh[1:2])]
        if last:
            newest = [(before[2 * b : 2 * b + 1], before[2 * b + 1 : 2 * b + 2])] + newest
        extra = [jnp.sum(query * k, axis=1, keepdims=True) * factor for k, _ in newest]
        top = jnp.max(scores, axis=1, keepdims=True)
        for e in extra:
            top = jnp.maximum(top, e)
        expo = jnp.exp(scores - top)
        total = jnp.sum(expo, axis=1, keepdims=True)
        more = [jnp.exp(e - top) for e in extra]
        for e in more:
            total = total + e
        out = nn_dot((expo / total).astype(bf16), cache[b, :, HD:])
        for e, (_, v) in zip(more, newest):
            out = out + (e / total).astype(bf16).astype(f32) * v
        out = out.astype(bf16)
        rows.append(out)
        if last:
            flat = out.astype(f32)
            lows.append(
                jnp.concatenate([flat[h : h + 1] for h in range(HEADS_TP)], axis=1)
            )
    both = jnp.concatenate([r.astype(f32) for r in rows], axis=0)
    if last:
        low = jnp.concatenate(lows + [jnp.zeros((8 - ROLLS, HEADS_TP * HD), f32)], axis=0)
        low = nn_dot(low.astype(bf16), ab[...])
        attended[...] = jnp.concatenate([both, low], axis=0)
    else:
        attended[...] = jnp.broadcast_to(both.astype(bf16), attended.shape)
    kv_out[...] = jnp.concatenate(kvs + [jnp.zeros((8 - 2 * ROLLS, LANES), f32)], axis=0)


def attend(last, lengths, came, cache, before, ab):
    att = (
        shape(24, LANES)
        if last
        else shape(CHIP_COUNT, ROLLS * HEADS_TP, LANES, dtype=bf16)
    )
    return call(
        lambda *refs: attend_kernel(last, *refs),
        (att, shape(8, LANES), shape(ROLLS * CHIP_COUNT, LANES)),
        [SMEM, ANY, HBM, HBM, HBM],
        (lengths, came, cache, before, ab),
        scratch=[pltpu.VMEM((8, LANES), f32)],
        flops=2 * 32 * 2 * cache.shape[0] * cache.shape[1] * HD,
    )


def close_kernel(place, came, w_own, w_other, ab, out, held):
    rows = ROLLS * HEADS_TP
    held[...] = came[...].astype(f32).reshape(CHIP_COUNT * rows, LANES)
    blocks = []
    for b in range(ROLLS):
        heads = [
            held[pl.ds(b * HEADS_TP + h, CHIP_COUNT, stride=rows), :] for h in range(HEADS_TP)
        ]
        blocks.append(jnp.concatenate(heads, axis=1))
    everyone = jnp.concatenate(blocks, axis=0).astype(bf16)
    first = place[0] == 0
    w_even = jnp.where(first, w_own[...], w_other[...])
    w_odd = jnp.where(first, w_other[...], w_own[...])
    w = jnp.concatenate([w_even, w_odd], axis=0)
    out[:, :LANES] = nt_dot(everyone, w)
    out[:, LANES:] = nn_dot(everyone, ab[...])


def adapter_kernel(
    place, rewards, prompts, live, own, other, rows, upstream, weighted_out, ab_out, part
):
    first = place[0] == 0
    even = jnp.where(first, own[...], other[...])
    odd = jnp.where(first, other[...], own[...])
    ab_out[:, :PIECE, :] = even[:, :PIECE]
    ab_out[:, PIECE:, :] = odd[:, :PIECE]
    lane = lane_iota((CHIP_COUNT, LANES))
    seen = []
    for side in (own, other):
        tail = side[:, PIECE:, :].astype(f32)
        seen.append((tail[:, 2, :] + tail[:, 3, :] + tail[:, 4, :], tail[:, 5, :]))
    count = rows.shape[0]
    index = lax.broadcasted_iota(jnp.int32, (count, 1), 0)
    weight = jnp.zeros((count, 1), f32)
    for b in range(ROLLS):
        total = jnp.zeros((1, 1), f32)
        squares = jnp.zeros((1, 1), f32)
        for value, prompt in seen:
            hit = (prompt == prompts[b].astype(f32)) & (lane < ROLLS)
            value = jnp.where(hit, value, 0.0)
            total = total + jnp.sum(jnp.sum(value, axis=0, keepdims=True), axis=1, keepdims=True)
            value = value * value
            squares = squares + jnp.sum(
                jnp.sum(value, axis=0, keepdims=True), axis=1, keepdims=True
            )
        mean = total / GROUP
        std = jnp.sqrt(jnp.maximum(squares / GROUP - mean * mean, 0.09))
        per_roll = (rewards[b] - mean) / std / live[b].astype(f32)
        slot = index - b * COMP
        inside = (slot >= 0) & (slot < COMP) & (slot < live[b])
        weight = jnp.where(inside, per_roll, weight)
    weighted = (weight * upstream[...].astype(f32)).astype(bf16)
    weighted_out[...] = weighted
    ab = ab_out[...].reshape(2 * CHIP_COUNT * PIECE, LANES)
    low = nn_dot(rows[...], ab)
    back = nn_dot(weighted, ab)
    part[:count, :] = jnp.where(lane_iota((count, LANES)) < RANK, low, back)
    z = place[2]
    each = LANES // (2 * PIECE)
    piece = ab_out[pl.ds(z * each, each), :, :].reshape(LANES, LANES).astype(f32)
    piece = pltpu.roll(piece, RANK, 1)
    part[count:, :] = jnp.where(lane_iota((LANES, LANES)) < RANK, piece, 0.0)


def gradient_kernel(
    place, p0, p1, p2, p3, rows, weighted, low_back, b_cols, kept, given
):
    count = rows.shape[0]
    total = p0[:count, :] + p1[:count, :] + p2[:count, :] + p3[:count, :]
    low_back[...] = total.astype(bf16)
    turned = pltpu.roll(total, RANK, 1).astype(bf16)
    from_y = place[3]
    piece = p0[count:, :]
    for by, p in ((1, p1), (2, p2), (3, p3)):
        piece = jnp.where(from_y == by, p[count:, :], piece)
    b_cols[...] = piece
    a_side = tn_dot(rows[...], turned)
    b_side = tn_dot(weighted[...], turned)
    both = adapter_scale * jnp.where(lane_iota(a_side.shape) < RANK, a_side, b_side)
    both = both.reshape(CHIP_COUNT, 2 * PIECE, LANES)
    even, odd = both[:, :PIECE], both[:, PIECE:]
    first = place[0] == 0
    kept[...] = jnp.where(first, even, odd)
    given[...] = jnp.where(first, odd, even)


def turned_up(b_ref):
    b = b_ref[...]
    b = jnp.where(lane_iota(b.shape) >= RANK, b, jnp.zeros_like(b))
    return pltpu.roll(b.astype(f32), RANK, 1)


def rows_kernel(where_ref, own, left, right, far_a, far_b, w_ref, low, b_ref, out):
    half = far_a.shape[0]
    acc = nt_dot(own[...], w_ref[where_ref[0]])
    acc = acc + nt_dot(left[...], w_ref[where_ref[1]])
    acc = acc + nt_dot(right[...], w_ref[where_ref[3]])
    far = jnp.concatenate([far_a[...], far_b[...]], axis=0)
    acc = acc + nt_dot(far, w_ref[where_ref[2]])
    out[...] = acc + adapter_scale * nt_dot(low[...], turned_up(b_ref).astype(bf16))


def output_rows(where, own, left, right, far_a, far_b, w, low, b):
    n, width, depth = w.shape
    rows = own.shape[0]
    tile = 256
    whole = lambda a: pl.BlockSpec(a.shape, lambda j, s: (0, 0))
    return pl.pallas_call(
        rows_kernel,
        out_shape=shape(rows, width),
        grid_spec=pltpu.PrefetchScalarGridSpec(
            num_scalar_prefetch=1,
            grid=(width // tile,),
            in_specs=[
                whole(own),
                whole(left),
                whole(right),
                whole(far_a),
                whole(far_b),
                pl.BlockSpec((n, tile, depth), lambda j, s: (0, j, 0)),
                whole(low),
                pl.BlockSpec((tile, b.shape[1]), lambda j, s: (j, 0)),
            ],
            out_specs=pl.BlockSpec((rows, tile), lambda j, s: (0, j)),
        ),
        compiler_params=pltpu.CompilerParams(vmem_limit_bytes=GRANT << 20),
        cost_estimate=pl.CostEstimate(
            flops=2 * rows * width * depth * n,
            bytes_accessed=2 * (n * width * depth + n * rows * depth) + 4 * rows * width,
            transcendentals=0,
        ),
    )(where, own, left, right, far_a, far_b, w, low, b)


def decode_kernel(where_ref, p0, p1, p2, p3, w_ref, b_ref, owned, out, heads, held, sem):
    k = pl.program_id(1)

    @pl.when((pl.program_id(0) == 0) & (k == 0))
    def _():
        copies = [
            pltpu.make_async_copy(p, held.at[i], sem.at[i]) for i, p in enumerate((p0, p1, p2, p3))
        ]
        for copy in copies:
            copy.start()
        for copy in copies:
            copy.wait()
        for i in range(len(copies)):
            s = held[i]
            flat = [
                jnp.concatenate(
                    [s[b * HEADS_TP + h : b * HEADS_TP + h + 1] for h in range(HEADS_TP)],
                    axis=1,
                )
                for b in range(ROLLS)
            ]
            flat.append(jnp.zeros((16 - ROLLS, HEADS_TP * HD), f32))
            heads[i] = jnp.concatenate(flat, axis=0).astype(bf16)

    got = nt_dot(heads[k], w_ref[0])[:8]

    @pl.when(k == 0)
    def _():
        top = ROLLS * HEADS_TP
        low = held[0, top:, :] + held[1, top:, :] + held[2, top:, :] + held[3, top:, :]
        start = adapter_scale * nt_dot(low, turned_up(b_ref), precision=HIGH)
        base = jnp.concatenate([owned[...], jnp.zeros((8 - ROLLS, owned.shape[1]), f32)], axis=0)
        out[...] = base + start + got

    @pl.when(k > 0)
    def _():
        out[...] += got


def decode_columns(where, sent, w, b, owned):
    n, width, depth = w.shape
    tile = 512
    tiles = width // tile
    whole = lambda a: pl.BlockSpec(a.shape, lambda j, k, s: (0, 0))
    return pl.pallas_call(
        decode_kernel,
        out_shape=shape(8, width),
        grid_spec=pltpu.PrefetchScalarGridSpec(
            num_scalar_prefetch=1,
            grid=(tiles, n),
            in_specs=[
                *(pl.BlockSpec(memory_space=ANY) for s in sent),
                pl.BlockSpec((1, tile, depth), lambda j, k, s: (s[k], j, 0)),
                pl.BlockSpec((tile, b.shape[1]), lambda j, k, s: (j, 0)),
                pl.BlockSpec((ROLLS, tile), lambda j, k, s: (0, s[0] * tiles + j)),
            ],
            out_specs=pl.BlockSpec((8, tile), lambda j, k, s: (0, j)),
            scratch_shapes=[
                pltpu.VMEM((n, 16, depth), bf16),
                pltpu.VMEM((n, *sent[0].shape), f32),
                pltpu.SemaphoreType.DMA((n,)),
            ],
        ),
        compiler_params=pltpu.CompilerParams(vmem_limit_bytes=MID_GRANT << 20),
        cost_estimate=pl.CostEstimate(
            flops=2 * 16 * width * depth * n,
            bytes_accessed=DECODE_HINT * 2 * n * width * depth,
            transcendentals=0,
        ),
    )(where, *sent, w, b, owned)


def place_kernel(where_ref, c0, c1, c2, c3, out):
    width = c0.shape[1]
    for k, part in enumerate((c0, c1, c2, c3)):
        start = pl.multiple_of(where_ref[k] * width, width)
        out[:, pl.ds(start, width)] = part[:ROLLS, :]


def shards(
    hidden,
    attention_norm_gain,
    query_key_value_weight,
    key_value_cache,
    cache_fill_lengths,
    output_weight_frozen,
    adapter_down_transposed,
    adapter_up_matrix,
    attention_rows,
    upstream,
    rewards,
    prompt_group_index,
    completion_live_lengths,
):
    nt = lax.axis_size("t")
    t = lax.axis_index("t")
    y = lax.axis_index("y")
    z = lax.axis_index("z")
    c = lax.axis_index("c")
    m = lax.axis_index(CHIPS)
    width = hidden.shape[1]
    shard_width = width // nt
    cache = key_value_cache[:, :, 0, :]
    place = jnp.stack([c, y, z, lax.rem(t - y + nt, nt), m]).astype(jnp.int32)
    where = lax.rem(t - jnp.arange(nt, dtype=jnp.int32) + nt, nt)

    message = call(
        message_kernel,
        shape(CHIP_COUNT, FIRST_ROWS, LANES, dtype=bf16),
        [SMEM, SMEM, HBM, HBM, HBM],
        (
            rewards,
            prompt_group_index,
            adapter_down_transposed[:, 0, :].T,
            adapter_up_matrix[:, 0, :].T,
            hidden,
        ),
    )

    w_rows = query_key_value_weight[:, 0, :]
    w_rows_other = swapped(w_rows)
    w_cols = output_weight_frozen[0].T
    w_cols_other = swapped(w_cols)

    ny = lax.axis_size("y")
    turned = lax.ppermute(
        w_cols, ("y", "t"), [(a * nt + b, b * nt + a) for a in range(ny) for b in range(nt)]
    )
    turned, message, place, where = together(turned, message, place, where)
    w_block = lax.all_gather(turned, DP, axis=0, tiled=True)
    w_block = w_block.reshape(nt, shard_width, w_cols.shape[1])

    left = shift(attention_rows, 1, nt)
    right = shift(attention_rows, nt - 1, nt)

    arrived = exchange(message, CHIPS)
    gain = attention_norm_gain[None, :]
    sent, state = call(
        qkv_first_kernel,
        (shape(CHIP_COUNT * QKV_ROWS, LANES), shape(ROLLS * CHIP_COUNT, LANES)),
        [SMEM, ANY, HBM, HBM, ANY],
        (place, arrived, gain, w_rows, w_rows_other),
        scratch=[pltpu.VMEM((CHIP_COUNT * FIRST_ROWS, LANES), f32)],
    )
    arrived_other = swapped(arrived)
    sent, arrived, arrived_other, left, right = together(
        sent, arrived, arrived_other, left, right
    )
    came = exchange(sent.reshape(CHIP_COUNT, QKV_ROWS, LANES), CHIPS)
    half = attention_rows.shape[0] // 2
    far_a = shift(left[:half], 1, nt)
    far_b = shift(right[half:], nt - 1, nt)

    rows = attention_rows.shape[0]
    weighted, ab, part = call(
        adapter_kernel,
        (
            shape(rows, shard_width, dtype=bf16),
            shape(CHIP_COUNT, 2 * PIECE, LANES, dtype=bf16),
            shape(rows + LANES, LANES),
        ),
        [SMEM] * 4 + [ANY, ANY, HBM, HBM],
        (
            place,
            rewards,
            prompt_group_index,
            completion_live_lengths,
            arrived,
            arrived_other,
            attention_rows,
            upstream,
        ),
        flops=4 * rows * shard_width * LANES,
    )
    ab = ab.reshape(shard_width, LANES)
    parts = shifts(part, nt)

    nothing = jnp.zeros((8, LANES), f32)
    attended, kv, _ = attend(
        False, cache_fill_lengths, came.reshape(-1, LANES), cache, nothing, ab
    )
    attended, weighted, far_a, far_b = together(attended, weighted, far_a, far_b)
    everyone = exchange(attended, CHIPS)

    low_back, b_cols, kept, given = call(
        gradient_kernel,
        (
            shape(rows, LANES, dtype=bf16),
            shape(LANES, LANES),
            shape(CHIP_COUNT, PIECE, LANES),
            shape(CHIP_COUNT, PIECE, LANES),
        ),
        [SMEM] + [ANY] * 4 + [HBM] * 2,
        (place, *parts, attention_rows, weighted),
        flops=4 * rows * shard_width * LANES,
    )

    share = call(
        close_kernel,
        shape(ROLLS * CHIP_COUNT, 2 * LANES),
        [SMEM, ANY, HBM, ANY, HBM],
        (place, everyone, w_cols, w_cols_other, ab),
        scratch=[pltpu.VMEM((CHIP_COUNT * ROLLS * HEADS_TP, LANES), f32)],
    )
    shares = shifts(share, nt)

    sent = call(
        qkv_later_kernel,
        shape(CHIP_COUNT * QKV_ROWS, LANES),
        [SMEM, HBM, HBM, HBM, ANY, HBM] + [ANY] * 4,
        (place, state, gain, w_rows, w_rows_other, b_cols, *shares),
    )
    sent, low_back, given = together(sent, low_back, given)
    kept = kept + swapped(given)
    came = exchange(sent.reshape(CHIP_COUNT, QKV_ROWS, LANES), CHIPS)

    adapted = output_rows(
        where, attention_rows, left, right, far_a, far_b, w_block, low_back, ab
    )

    came, adapted = together(came, adapted)

    attended, _, owned = attend(True, cache_fill_lengths, came.reshape(-1, LANES), cache, kv, ab)
    attended, kept = together(attended, kept)
    summed = exchange(kept, CHIPS)
    cols = decode_columns(where, shifts(attended, nt), w_block, ab, owned.reshape(ROLLS, width))
    arriving = shifts(cols, nt)
    arriving[1], summed = together(arriving[1], summed)
    summed = summed.sum(axis=0)
    decoded = call(
        place_kernel,
        shape(ROLLS, width),
        [SMEM] + [ANY] * nt,
        (where, *arriving),
        grant=SMALL_GRANT,
    )
    grad_a = summed[:, :RANK].T[:, None, :]
    grad_b = summed[:, RANK:].T[:, None, :]
    return (decoded, adapted, grad_a, grad_b)


def solution(mesh):
    split = Mesh(mesh.devices.reshape(4, 8, 2, 4), ("y", "z", "c", "t"))
    placed = (
        P(DP, None),
        P(),
        P(DP, "t", None),
        P(DP, None, "t", None),
        P(DP),
        P("t", None, DP),
        P(None, "t", DP),
        P(None, "t", DP),
        P(DP, "t"),
        P(DP, "t"),
        P(DP),
        P(DP),
        P(DP),
    )
    return jax.shard_map(
        shards,
        mesh=split,
        in_specs=placed,
        out_specs=(P(DP, None), P(DP, "t"), P(None, "t", DP), P(None, "t", DP)),
        check_vma=False,
    )
```

```python
import math

import jax
import jax.numpy as jnp
from jax import lax
from jax.experimental import pallas as pl
from jax.experimental.pallas import tpu as pltpu
from jax.sharding import Mesh
from jax.sharding import PartitionSpec as P

HD = 128
HEADS_TP = 8
GROUP = 4
COMP = 256
RANK = 64
LANES = 128
ROLLS = 2
CHIP_COUNT = 32
PIECE = 16
FIRST_ROWS = 24
QKV_ROWS = 24
KEY_ROW = ROLLS * HEADS_TP
STATE_ROW = KEY_ROW + 2 * ROLLS
GRANT = 56
SMALL_GRANT = 24
MID_GRANT = 60
DECODE_HINT = 128

adapter_scale = 2.0
f32 = jnp.float32
bf16 = jnp.bfloat16
CHIPS = ("y", "z")
DP = ("y", "z", "c")
HIGH = lax.Precision.HIGHEST
SMEM = pltpu.SMEM
VMEM = None


def nn_dot(a, b):
    return jnp.dot(a, b, preferred_element_type=f32)


def nt_dot(a, b, precision=None):
    return lax.dot_general(
        a, b, (((1,), (1,)), ((), ())), preferred_element_type=f32, precision=precision
    )


def tn_dot(a, b):
    return lax.dot_general(a, b, (((0,), (0,)), ((), ())), preferred_element_type=f32)


def swapped(x):
    return lax.ppermute(x, "c", [(0, 1), (1, 0)])


def shift(x, by, n):
    return lax.ppermute(x, "t", [(i, (i + by) % n) for i in range(n)])


def shifts(x, n):
    return [x] + [shift(x, by, n) for by in range(1, n)]


def exchange(x, axes):
    return lax.all_to_all(x, axes, split_axis=0, concat_axis=0, tiled=True)


def to_all(x, axes):
    return exchange(jnp.broadcast_to(x, (lax.axis_size(axes), *x.shape)), axes)


def together(*xs):
    return lax.optimization_barrier(xs)


def lane_iota(shape):
    return lax.broadcasted_iota(jnp.int32, shape, len(shape) - 1)


def call(kernel, out, specs, args, scratch=(), flops=0, grant=SMALL_GRANT):
    moved = sum(a.size * a.dtype.itemsize for a in args)
    outs = out if isinstance(out, tuple) else (out,)
    moved += sum(math.prod(o.shape) * o.dtype.itemsize for o in outs)
    whole = pl.BlockSpec()
    return pl.pallas_call(
        kernel,
        out_shape=out,
        in_specs=[pl.BlockSpec(memory_space=k) if k == SMEM else whole for k in specs],
        out_specs=tuple(whole for _ in outs) if isinstance(out, tuple) else whole,
        scratch_shapes=list(scratch),
        compiler_params=pltpu.CompilerParams(vmem_limit_bytes=grant << 20),
        cost_estimate=pl.CostEstimate(flops=flops, bytes_accessed=moved, transcendentals=0),
    )(*args)


def shape(*dims, dtype=f32):
    return jax.ShapeDtypeStruct(dims, dtype)


def message_kernel(rewards, prompts, a_ref, b_ref, hidden, out):
    pieces = jnp.concatenate([a_ref[...], b_ref[...]], axis=1)
    out[:, :PIECE, :] = jnp.broadcast_to(pieces, (CHIP_COUNT, PIECE, LANES))
    lane = lane_iota((1, LANES))
    value = jnp.where(lane == 0, rewards[0], jnp.where(lane == 1, rewards[1], 0.0))
    prompt = jnp.where(lane == 0, prompts[0], jnp.where(lane == 1, prompts[1], 0)).astype(f32)
    high = value.astype(bf16).astype(f32)
    mid = (value - high).astype(bf16).astype(f32)
    low = value - high - mid
    tail = jnp.concatenate([high, mid, low, prompt, jnp.zeros((2, LANES), f32)], axis=0)
    for m in range(CHIP_COUNT):
        cut = hidden[:, m * LANES : (m + 1) * LANES].astype(f32)
        out[m, PIECE:, :] = jnp.concatenate([cut, tail], axis=0).astype(bf16)


def spread_qkv(state, gain, first, w_own, w_other, out):
    w_even = jnp.where(first, w_own[...], w_other[...])
    w_odd = jnp.where(first, w_other[...], w_own[...])
    w = jnp.concatenate([w_even, w_odd], axis=0)
    x = state * gain
    x1 = x.astype(bf16)
    rest = x - x1.astype(f32)
    x2 = rest.astype(bf16)
    x3 = (rest - x2.astype(f32)).astype(bf16)
    count = x.shape[0]
    parts = nn_dot(jnp.concatenate([x1, x2, x3], axis=0), w)
    qkv = parts[:count] + parts[count : 2 * count] + parts[2 * count :]

    def put(row, block):
        out[pl.ds(row, CHIP_COUNT, stride=QKV_ROWS), :] = block

    for b in range(ROLLS):
        mine = qkv[b * CHIP_COUNT : (b + 1) * CHIP_COUNT]
        for h in range(HEADS_TP):
            put(b * HEADS_TP + h, mine[:, h * HD : (h + 1) * HD])
        put(KEY_ROW + 2 * b, mine[:, HEADS_TP * HD : (HEADS_TP + 1) * HD])
        put(KEY_ROW + 2 * b + 1, mine[:, (HEADS_TP + 1) * HD :])
        put(STATE_ROW + b, state[b * CHIP_COUNT : (b + 1) * CHIP_COUNT])
    for row in range(STATE_ROW + ROLLS, QKV_ROWS):
        put(row, jnp.zeros((CHIP_COUNT, LANES), f32))


def first_core():
    return lax.axis_index("c") == 0


def gain_of(gain):
    m = lax.axis_index("y") * lax.axis_size("z") + lax.axis_index("z")
    start = pl.multiple_of(m * LANES, LANES)
    return gain[:, pl.ds(start, LANES)].astype(f32)


def qkv_first_kernel(arrived, gain, w_own, w_other, out, state_out, held):
    held[...] = arrived[...].astype(f32).reshape(CHIP_COUNT * FIRST_ROWS, LANES)
    state = jnp.concatenate(
        [held[pl.ds(PIECE + b, CHIP_COUNT, stride=FIRST_ROWS), :] for b in range(ROLLS)], axis=0
    )
    state_out[...] = state
    spread_qkv(state, gain_of(gain), first_core(), w_own, w_other, out)


def qkv_later_kernel(state, gain, w_own, w_other, b_cols, s0, s1, s2, s3, out):
    share = s0[...] + s1[...] + s2[...] + s3[...]
    low = share[:, LANES:]
    now = (
        state[...]
        + share[:, :LANES]
        + adapter_scale * nt_dot(low, b_cols[...], precision=HIGH)
    )
    spread_qkv(now, gain_of(gain), first_core(), w_own, w_other, out)


def attend_kernel(last, lengths, came, cache, before, ab, attended, kv_out, owned_out, held):
    sums = jnp.sum(came[...].reshape(CHIP_COUNT, QKV_ROWS, LANES), axis=0)
    factor = 1.0 / math.sqrt(HD)
    width = CHIP_COUNT * LANES
    rows = []
    lows = []
    kvs = []
    for b in range(ROLLS):
        owned = came[pl.ds(STATE_ROW + b, CHIP_COUNT, stride=QKV_ROWS), :]
        owned_out[b * CHIP_COUNT : (b + 1) * CHIP_COUNT, :] = owned
        total = jnp.sum(jnp.sum(owned * owned, axis=0, keepdims=True), axis=1, keepdims=True)
        scale = lax.rsqrt(total * (1.0 / width) + 1e-05)
        query = sums[b * HEADS_TP : (b + 1) * HEADS_TP] * scale
        fresh = sums[KEY_ROW + 2 * b : KEY_ROW + 2 * b + 2] * scale
        kvs.append(fresh)
        q1 = query.astype(bf16)
        rest = query - q1.astype(f32)
        q2 = rest.astype(bf16)
        q3 = (rest - q2.astype(f32)).astype(bf16)
        keys = cache[b, :, :HD]
        parts = nt_dot(jnp.concatenate([q1, q2, q3], axis=0), keys)
        scores = (parts[:HEADS_TP] + parts[HEADS_TP : 2 * HEADS_TP] + parts[2 * HEADS_TP :]) * factor
        scores = jnp.where(lane_iota(scores.shape) < lengths[b], scores, -1e30)
        newest = [(fresh[0:1], fresh[1:2])]
        if last:
            newest = [(before[2 * b : 2 * b + 1], before[2 * b + 1 : 2 * b + 2])] + newest
        extra = [jnp.sum(query * k, axis=1, keepdims=True) * factor for k, _ in newest]
        top = jnp.max(scores, axis=1, keepdims=True)
        for e in extra:
            top = jnp.maximum(top, e)
        expo = jnp.exp(scores - top)
        total = jnp.sum(expo, axis=1, keepdims=True)
        more = [jnp.exp(e - top) for e in extra]
        for e in more:
            total = total + e
        out = nn_dot((expo / total).astype(bf16), cache[b, :, HD:])
        for e, (_, v) in zip(more, newest):
            out = out + (e / total).astype(bf16).astype(f32) * v
        out = out.astype(bf16)
        rows.append(out)
        if last:
            flat = out.astype(f32)
            lows.append(
                jnp.concatenate([flat[h : h + 1] for h in range(HEADS_TP)], axis=1)
            )
    both = jnp.concatenate([r.astype(f32) for r in rows], axis=0)
    if last:
        low = jnp.concatenate(lows + [jnp.zeros((8 - ROLLS, HEADS_TP * HD), f32)], axis=0)
        low = nn_dot(low.astype(bf16), ab[...])
        attended[...] = jnp.concatenate([both, low], axis=0)
    else:
        attended[...] = jnp.broadcast_to(both.astype(bf16), attended.shape)
    kv_out[...] = jnp.concatenate(kvs + [jnp.zeros((8 - 2 * ROLLS, LANES), f32)], axis=0)


def attend(last, lengths, came, cache, before, ab):
    att = (
        shape(24, LANES)
        if last
        else shape(CHIP_COUNT, ROLLS * HEADS_TP, LANES, dtype=bf16)
    )
    return call(
        lambda *refs: attend_kernel(last, *refs),
        (att, shape(8, LANES), shape(ROLLS * CHIP_COUNT, LANES)),
        [SMEM, VMEM, VMEM, VMEM, VMEM],
        (lengths, came, cache, before, ab),
        scratch=[pltpu.VMEM((8, LANES), f32)],
        flops=2 * 32 * 2 * cache.shape[0] * cache.shape[1] * HD,
    )


def close_kernel(came, w_own, w_other, ab, out, held):
    rows = ROLLS * HEADS_TP
    held[...] = came[...].astype(f32).reshape(CHIP_COUNT * rows, LANES)
    blocks = []
    for b in range(ROLLS):
        heads = [
            held[pl.ds(b * HEADS_TP + h, CHIP_COUNT, stride=rows), :] for h in range(HEADS_TP)
        ]
        blocks.append(jnp.concatenate(heads, axis=1))
    everyone = jnp.concatenate(blocks, axis=0).astype(bf16)
    first = first_core()
    w_even = jnp.where(first, w_own[...], w_other[...])
    w_odd = jnp.where(first, w_other[...], w_own[...])
    w = jnp.concatenate([w_even, w_odd], axis=0)
    out[:, :LANES] = nt_dot(everyone, w)
    out[:, LANES:] = nn_dot(everyone, ab[...])


def adapter_kernel(
    rewards, prompts, live, own, other, rows, upstream, weighted_out, ab_out, part
):
    first = first_core()
    even = jnp.where(first, own[...], other[...])
    odd = jnp.where(first, other[...], own[...])
    ab_out[:, :PIECE, :] = even[:, :PIECE]
    ab_out[:, PIECE:, :] = odd[:, :PIECE]
    lane = lane_iota((CHIP_COUNT, LANES))
    seen = []
    for side in (own, other):
        tail = side[:, PIECE:, :].astype(f32)
        seen.append((tail[:, 2, :] + tail[:, 3, :] + tail[:, 4, :], tail[:, 5, :]))
    count = rows.shape[0]
    index = lax.broadcasted_iota(jnp.int32, (count, 1), 0)
    weight = jnp.zeros((count, 1), f32)
    for b in range(ROLLS):
        total = jnp.zeros((1, 1), f32)
        squares = jnp.zeros((1, 1), f32)
        for value, prompt in seen:
            hit = (prompt == prompts[b].astype(f32)) & (lane < ROLLS)
            value = jnp.where(hit, value, 0.0)
            total = total + jnp.sum(jnp.sum(value, axis=0, keepdims=True), axis=1, keepdims=True)
            value = value * value
            squares = squares + jnp.sum(
                jnp.sum(value, axis=0, keepdims=True), axis=1, keepdims=True
            )
        mean = total / GROUP
        std = jnp.sqrt(jnp.maximum(squares / GROUP - mean * mean, 0.09))
        per_roll = (rewards[b] - mean) / std / live[b].astype(f32)
        slot = index - b * COMP
        inside = (slot >= 0) & (slot < COMP) & (slot < live[b])
        weight = jnp.where(inside, per_roll, weight)
    weighted = (weight * upstream[...].astype(f32)).astype(bf16)
    weighted_out[...] = weighted
    ab = ab_out[...].reshape(2 * CHIP_COUNT * PIECE, LANES)
    low = nn_dot(rows[...], ab)
    back = nn_dot(weighted, ab)
    part[:count, :] = jnp.where(lane_iota((count, LANES)) < RANK, low, back)
    z = lax.axis_index("z")
    each = LANES // (2 * PIECE)
    piece = ab_out[pl.ds(z * each, each), :, :].reshape(LANES, LANES).astype(f32)
    piece = pltpu.roll(piece, RANK, 1)
    part[count:, :] = jnp.where(lane_iota((LANES, LANES)) < RANK, piece, 0.0)


def gradient_kernel(
    p0, p1, p2, p3, rows, weighted, low_back, b_cols, kept, given
):
    count = rows.shape[0]
    total = p0[:count, :] + p1[:count, :] + p2[:count, :] + p3[:count, :]
    low_back[...] = total.astype(bf16)
    turned = pltpu.roll(total, RANK, 1).astype(bf16)
    nt = lax.axis_size("t")
    from_y = lax.rem(lax.axis_index("t") - lax.axis_index("y") + nt, nt)
    piece = p0[count:, :]
    for by, p in ((1, p1), (2, p2), (3, p3)):
        piece = jnp.where(from_y == by, p[count:, :], piece)
    b_cols[...] = piece
    a_side = tn_dot(rows[...], turned)
    b_side = tn_dot(weighted[...], turned)
    both = adapter_scale * jnp.where(lane_iota(a_side.shape) < RANK, a_side, b_side)
    both = both.reshape(CHIP_COUNT, 2 * PIECE, LANES)
    even, odd = both[:, :PIECE], both[:, PIECE:]
    first = first_core()
    kept[...] = jnp.where(first, even, odd)
    given[...] = jnp.where(first, odd, even)


def turned_up(b_ref):
    b = b_ref[...]
    b = jnp.where(lane_iota(b.shape) >= RANK, b, jnp.zeros_like(b))
    return pltpu.roll(b.astype(f32), RANK, 1)


def rows_kernel(where_ref, own, left, right, far_a, far_b, w_ref, low, b_ref, out):
    half = far_a.shape[0]
    acc = nt_dot(own[...], w_ref[where_ref[0]])
    acc = acc + nt_dot(left[...], w_ref[where_ref[1]])
    acc = acc + nt_dot(right[...], w_ref[where_ref[3]])
    far = jnp.concatenate([far_a[...], far_b[...]], axis=0)
    acc = acc + nt_dot(far, w_ref[where_ref[2]])
    out[...] = acc + adapter_scale * nt_dot(low[...], turned_up(b_ref).astype(bf16))


def output_rows(where, own, left, right, far_a, far_b, w, low, b):
    n, width, depth = w.shape
    rows = own.shape[0]
    tile = 256
    whole = lambda a: pl.BlockSpec(a.shape, lambda j, s: (0, 0))
    return pl.pallas_call(
        rows_kernel,
        out_shape=shape(rows, width),
        grid_spec=pltpu.PrefetchScalarGridSpec(
            num_scalar_prefetch=1,
            grid=(width // tile,),
            in_specs=[
                whole(own),
                whole(left),
                whole(right),
                whole(far_a),
                whole(far_b),
                pl.BlockSpec((n, tile, depth), lambda j, s: (0, j, 0)),
                whole(low),
                pl.BlockSpec((tile, b.shape[1]), lambda j, s: (j, 0)),
            ],
            out_specs=pl.BlockSpec((rows, tile), lambda j, s: (0, j)),
        ),
        compiler_params=pltpu.CompilerParams(vmem_limit_bytes=GRANT << 20),
        cost_estimate=pl.CostEstimate(
            flops=2 * rows * width * depth * n,
            bytes_accessed=2 * (n * width * depth + n * rows * depth) + 4 * rows * width,
            transcendentals=0,
        ),
    )(where, own, left, right, far_a, far_b, w, low, b)


def decode_kernel(where_ref, s0, s1, s2, s3, w_ref, b_ref, owned, out, heads, acc):
    sent = (s0, s1, s2, s3)
    k = pl.program_id(0)

    @pl.when(k == 0)
    def _():
        for i, s in enumerate(sent):
            flat = [
                jnp.concatenate(
                    [s[b * HEADS_TP + h : b * HEADS_TP + h + 1, :] for h in range(HEADS_TP)],
                    axis=1,
                )
                for b in range(ROLLS)
            ]
            flat.append(jnp.zeros((16 - ROLLS, HEADS_TP * HD), f32))
            heads[i] = jnp.concatenate(flat, axis=0).astype(bf16)
        acc[...] = jnp.zeros_like(acc)

    acc[...] += nt_dot(w_ref[0], heads[k])

    @pl.when(k == pl.num_programs(0) - 1)
    def _():
        top = ROLLS * HEADS_TP
        low = s0[top:, :] + s1[top:, :] + s2[top:, :] + s3[top:, :]
        got = acc[...].T[:8] + adapter_scale * nt_dot(low, turned_up(b_ref), precision=HIGH)
        out[...] = got
        out[:ROLLS, :] += owned[...]


def decode_columns(where, sent, w, b, owned):
    n, width, depth = w.shape
    whole = lambda a: pl.BlockSpec(a.shape, lambda k, s: (0, 0))
    return pl.pallas_call(
        decode_kernel,
        out_shape=shape(8, width),
        grid_spec=pltpu.PrefetchScalarGridSpec(
            num_scalar_prefetch=1,
            grid=(n,),
            in_specs=[
                *(whole(s) for s in sent),
                pl.BlockSpec((1, width, depth), lambda k, s: (s[k], 0, 0)),
                whole(b),
                pl.BlockSpec((ROLLS, width), lambda k, s: (0, s[0])),
            ],
            out_specs=pl.BlockSpec((8, width), lambda k, s: (0, 0)),
            scratch_shapes=[
                pltpu.VMEM((n, 16, depth), bf16),
                pltpu.VMEM((width, 16), f32),
            ],
        ),
        compiler_params=pltpu.CompilerParams(vmem_limit_bytes=MID_GRANT << 20),
        cost_estimate=pl.CostEstimate(
            flops=DECODE_HINT * 2 * 16 * width * depth * n,
            bytes_accessed=2 * n * width * depth,
            transcendentals=0,
        ),
    )(where, *sent, w, b, owned)


def place_kernel(c0, c1, c2, c3, out):
    width = c0.shape[1]
    nt = lax.axis_size("t")
    for k, part in enumerate((c0, c1, c2, c3)):
        block = lax.rem(lax.axis_index("t") - k + nt, nt)
        start = pl.multiple_of(block * width, width)
        out[:, pl.ds(start, width)] = part[:ROLLS, :]


def shards(
    hidden,
    attention_norm_gain,
    query_key_value_weight,
    key_value_cache,
    cache_fill_lengths,
    output_weight_frozen,
    adapter_down_transposed,
    adapter_up_matrix,
    attention_rows,
    upstream,
    rewards,
    prompt_group_index,
    completion_live_lengths,
):
    nt = lax.axis_size("t")
    t = lax.axis_index("t")
    width = hidden.shape[1]
    shard_width = width // nt
    cache = key_value_cache[:, :, 0, :]
    where = lax.rem(t - jnp.arange(nt, dtype=jnp.int32) + nt, nt)

    message = call(
        message_kernel,
        shape(CHIP_COUNT, FIRST_ROWS, LANES, dtype=bf16),
        [SMEM, SMEM, VMEM, VMEM, VMEM],
        (
            rewards,
            prompt_group_index,
            adapter_down_transposed[:, 0, :].T,
            adapter_up_matrix[:, 0, :].T,
            hidden,
        ),
    )

    w_rows = query_key_value_weight[:, 0, :]
    w_rows_other = swapped(w_rows)
    w_cols = output_weight_frozen[0].T
    w_cols_other = swapped(w_cols)

    ny = lax.axis_size("y")
    turned = lax.ppermute(
        w_cols, ("y", "t"), [(a * nt + b, b * nt + a) for a in range(ny) for b in range(nt)]
    )
    turned, message, where = together(turned, message, where)
    w_block = lax.all_gather(turned, DP, axis=0, tiled=True)
    w_block = w_block.reshape(nt, shard_width, w_cols.shape[1])


    left = shift(attention_rows, 1, nt)
    right = shift(attention_rows, nt - 1, nt)
    arrived = exchange(message, CHIPS)
    gain = attention_norm_gain[None, :]
    sent, state = call(
        qkv_first_kernel,
        (shape(CHIP_COUNT * QKV_ROWS, LANES), shape(ROLLS * CHIP_COUNT, LANES)),
        [VMEM] * 4,
        (arrived, gain, w_rows, w_rows_other),
        scratch=[pltpu.VMEM((CHIP_COUNT * FIRST_ROWS, LANES), f32)],
    )
    arrived_other = swapped(arrived)
    sent, arrived, arrived_other, left, right = together(
        sent, arrived, arrived_other, left, right
    )
    came = exchange(sent.reshape(CHIP_COUNT, QKV_ROWS, LANES), CHIPS)
    half = attention_rows.shape[0] // 2
    came, left_half, right_half = together(came, left[:half], right[half:])

    rows = attention_rows.shape[0]
    weighted, ab, part = call(
        adapter_kernel,
        (
            shape(rows, shard_width, dtype=bf16),
            shape(CHIP_COUNT, 2 * PIECE, LANES, dtype=bf16),
            shape(rows + LANES, LANES),
        ),
        [SMEM] * 3 + [VMEM] * 4,
        (
            rewards,
            prompt_group_index,
            completion_live_lengths,
            arrived,
            arrived_other,
            attention_rows,
            upstream,
        ),
        flops=4 * rows * shard_width * LANES,
    )
    ab = ab.reshape(shard_width, LANES)
    parts = shifts(part, nt)

    nothing = jnp.zeros((8, LANES), f32)
    attended, kv, _ = attend(
        False, cache_fill_lengths, came.reshape(-1, LANES), cache, nothing, ab
    )
    attended, weighted = together(attended, weighted)
    everyone = exchange(attended, CHIPS)

    low_back, b_cols, kept, given = call(
        gradient_kernel,
        (
            shape(rows, LANES, dtype=bf16),
            shape(LANES, LANES),
            shape(CHIP_COUNT, PIECE, LANES),
            shape(CHIP_COUNT, PIECE, LANES),
        ),
        [VMEM] * 6,
        (*parts, attention_rows, weighted),
        flops=4 * rows * shard_width * LANES,
    )

    everyone, b_cols = together(everyone, b_cols)

    share = call(
        close_kernel,
        shape(ROLLS * CHIP_COUNT, 2 * LANES),
        [VMEM] * 4,
        (everyone, w_cols, w_cols_other, ab),
        scratch=[pltpu.VMEM((CHIP_COUNT * ROLLS * HEADS_TP, LANES), f32)],
    )
    shares = shifts(share, nt)

    sent = call(
        qkv_later_kernel,
        shape(CHIP_COUNT * QKV_ROWS, LANES),
        [VMEM] * 9,
        (state, gain, w_rows, w_rows_other, b_cols, *shares),
    )
    sent, low_back, given = together(sent, low_back, given)
    given, left_half, right_half = together(swapped(given), left_half, right_half)
    kept = kept + given
    far_a = shift(left_half, 1, nt)
    far_b = shift(right_half, nt - 1, nt)
    came = exchange(sent.reshape(CHIP_COUNT, QKV_ROWS, LANES), CHIPS)

    adapted = output_rows(
        where, attention_rows, left, right, far_a, far_b, w_block, low_back, ab
    )

    came, adapted = together(came, adapted)

    attended, _, owned = attend(True, cache_fill_lengths, came.reshape(-1, LANES), cache, kv, ab)
    attended, kept = together(attended, kept)
    summed = exchange(kept, CHIPS)
    cols = decode_columns(where, shifts(attended, nt), w_block, ab, owned.reshape(ROLLS, width))
    arriving = shifts(cols, nt)
    arriving[1], summed = together(arriving[1], summed)
    summed = summed.sum(axis=0)
    decoded = call(
        place_kernel,
        shape(ROLLS, width),
        [VMEM] * nt,
        tuple(arriving),
        grant=SMALL_GRANT,
    )
    grad_a = summed[:, :RANK].T[:, None, :]
    grad_b = summed[:, RANK:].T[:, None, :]
    return (decoded, adapted, grad_a, grad_b)


def solution(mesh):
    split = Mesh(mesh.devices.reshape(4, 8, 2, 4), ("y", "z", "c", "t"))
    placed = (
        P(DP, None),
        P(),
        P(DP, "t", None),
        P(DP, None, "t", None),
        P(DP),
        P("t", None, DP),
        P(None, "t", DP),
        P(None, "t", DP),
        P(DP, "t"),
        P(DP, "t"),
        P(DP),
        P(DP),
        P(DP),
    )
    return jax.shard_map(
        shards,
        mesh=split,
        in_specs=placed,
        out_specs=(P(DP, None), P(DP, "t"), P(None, "t", DP), P(None, "t", DP)),
        check_vma=False,
    )
```

```python
import math

import jax
import jax.numpy as jnp
from jax import lax
from jax.experimental import pallas as pl
from jax.experimental.pallas import tpu as pltpu
from jax.sharding import Mesh
from jax.sharding import PartitionSpec as P

HD = 128
HEADS_TP = 8
GROUP = 4
COMP = 256
RANK = 64
LANES = 128
ROLLS = 2
CHIP_COUNT = 32
PIECE = 16
FIRST_ROWS = 24
QKV_ROWS = 24
KEY_ROW = ROLLS * HEADS_TP
STATE_ROW = KEY_ROW + 2 * ROLLS
GRANT = 40
SMALL_GRANT = 24
DECODE_HINT = 128

adapter_scale = 2.0
f32 = jnp.float32
bf16 = jnp.bfloat16
CHIPS = ("y", "z")
DP = ("y", "z", "c")
HIGH = lax.Precision.HIGHEST
SMEM = pltpu.SMEM
VMEM = None


def nn_dot(a, b):
    return jnp.dot(a, b, preferred_element_type=f32)


def nt_dot(a, b, precision=None):
    return lax.dot_general(
        a, b, (((1,), (1,)), ((), ())), preferred_element_type=f32, precision=precision
    )


def tn_dot(a, b):
    return lax.dot_general(a, b, (((0,), (0,)), ((), ())), preferred_element_type=f32)


def swapped(x):
    return lax.ppermute(x, "c", [(0, 1), (1, 0)])


def shift(x, by, n):
    return lax.ppermute(x, "t", [(i, (i + by) % n) for i in range(n)])


def shifts(x, n):
    return [x] + [shift(x, by, n) for by in range(1, n)]


def exchange(x, axes):
    return lax.all_to_all(x, axes, split_axis=0, concat_axis=0, tiled=True)


def to_all(x, axes):
    return exchange(jnp.broadcast_to(x, (lax.axis_size(axes), *x.shape)), axes)


def together(*xs):
    return lax.optimization_barrier(xs)


def lane_iota(shape):
    return lax.broadcasted_iota(jnp.int32, shape, len(shape) - 1)


def call(kernel, out, specs, args, scratch=(), flops=0, grant=SMALL_GRANT):
    moved = sum(a.size * a.dtype.itemsize for a in args)
    outs = out if isinstance(out, tuple) else (out,)
    moved += sum(math.prod(o.shape) * o.dtype.itemsize for o in outs)
    whole = pl.BlockSpec()
    return pl.pallas_call(
        kernel,
        out_shape=out,
        in_specs=[pl.BlockSpec(memory_space=k) if k == SMEM else whole for k in specs],
        out_specs=tuple(whole for _ in outs) if isinstance(out, tuple) else whole,
        scratch_shapes=list(scratch),
        compiler_params=pltpu.CompilerParams(vmem_limit_bytes=grant << 20),
        cost_estimate=pl.CostEstimate(flops=flops, bytes_accessed=moved, transcendentals=0),
    )(*args)


def shape(*dims, dtype=f32):
    return jax.ShapeDtypeStruct(dims, dtype)


def message_kernel(rewards, prompts, a_ref, b_ref, hidden, out):
    pieces = jnp.concatenate([a_ref[...], b_ref[...]], axis=1)
    out[:, :PIECE, :] = jnp.broadcast_to(pieces, (CHIP_COUNT, PIECE, LANES))
    lane = lane_iota((1, LANES))
    value = jnp.where(lane == 0, rewards[0], jnp.where(lane == 1, rewards[1], 0.0))
    prompt = jnp.where(lane == 0, prompts[0], jnp.where(lane == 1, prompts[1], 0)).astype(f32)
    high = value.astype(bf16).astype(f32)
    mid = (value - high).astype(bf16).astype(f32)
    low = value - high - mid
    tail = jnp.concatenate([high, mid, low, prompt, jnp.zeros((2, LANES), f32)], axis=0)
    for m in range(CHIP_COUNT):
        cut = hidden[:, m * LANES : (m + 1) * LANES].astype(f32)
        out[m, PIECE:, :] = jnp.concatenate([cut, tail], axis=0).astype(bf16)


def spread_qkv(state, gain, w, out):
    x = state * gain
    x1 = x.astype(bf16)
    rest = x - x1.astype(f32)
    x2 = rest.astype(bf16)
    x3 = (rest - x2.astype(f32)).astype(bf16)
    count = x.shape[0]
    parts = nn_dot(jnp.concatenate([x1, x2, x3], axis=0), w)
    qkv = parts[:count] + parts[count : 2 * count] + parts[2 * count :]

    def put(row, block):
        out[pl.ds(row, CHIP_COUNT, stride=QKV_ROWS), :] = block

    for b in range(ROLLS):
        mine = qkv[b * CHIP_COUNT : (b + 1) * CHIP_COUNT]
        for h in range(HEADS_TP):
            put(b * HEADS_TP + h, mine[:, h * HD : (h + 1) * HD])
        put(KEY_ROW + 2 * b, mine[:, HEADS_TP * HD : (HEADS_TP + 1) * HD])
        put(KEY_ROW + 2 * b + 1, mine[:, (HEADS_TP + 1) * HD :])
        put(STATE_ROW + b, state[b * CHIP_COUNT : (b + 1) * CHIP_COUNT])
    for row in range(STATE_ROW + ROLLS, QKV_ROWS):
        put(row, jnp.zeros((CHIP_COUNT, LANES), f32))


def first_core():
    return lax.axis_index("c") == 0


def gain_of(gain):
    m = lax.axis_index("y") * lax.axis_size("z") + lax.axis_index("z")
    start = pl.multiple_of(m * LANES, LANES)
    return gain[:, pl.ds(start, LANES)].astype(f32)


def qkv_first_kernel(arrived, gain, w_own, w_other, out, state_out, w_out, held):
    held[...] = arrived[...].astype(f32).reshape(CHIP_COUNT * FIRST_ROWS, LANES)
    state = jnp.concatenate(
        [held[pl.ds(PIECE + b, CHIP_COUNT, stride=FIRST_ROWS), :] for b in range(ROLLS)], axis=0
    )
    state_out[...] = state
    first = first_core()
    rows = w_own.shape[0]
    w_out[:rows, :] = jnp.where(first, w_own[...], w_other[...])
    w_out[rows:, :] = jnp.where(first, w_other[...], w_own[...])
    spread_qkv(state, gain_of(gain), w_out[...], out)


def qkv_later_kernel(held, gain, w, s0, s1, s2, s3, out):
    share = s0[...] + s1[...] + s2[...] + s3[...]
    low = share[:, LANES:]
    count = share.shape[0]
    now = (
        held[:count, :]
        + share[:, :LANES]
        + adapter_scale * nt_dot(low, held[count:, :], precision=HIGH)
    )
    spread_qkv(now, gain_of(gain), w[...], out)


def attend_kernel(last, lengths, came, cache, *refs):
    if last:
        before, ab, attended, owned_out = refs
    else:
        attended, kv_out = refs
    sums = jnp.sum(came[...].reshape(CHIP_COUNT, QKV_ROWS, LANES), axis=0)
    factor = 1.0 / math.sqrt(HD)
    width = CHIP_COUNT * LANES
    rows = []
    lows = []
    kvs = []
    for b in range(ROLLS):
        owned = came[pl.ds(STATE_ROW + b, CHIP_COUNT, stride=QKV_ROWS), :]
        if last:
            owned_out[b * CHIP_COUNT : (b + 1) * CHIP_COUNT, :] = owned
        total = jnp.sum(jnp.sum(owned * owned, axis=0, keepdims=True), axis=1, keepdims=True)
        scale = lax.rsqrt(total * (1.0 / width) + 1e-05)
        query = sums[b * HEADS_TP : (b + 1) * HEADS_TP] * scale
        fresh = sums[KEY_ROW + 2 * b : KEY_ROW + 2 * b + 2] * scale
        kvs.append(fresh)
        q1 = query.astype(bf16)
        rest = query - q1.astype(f32)
        q2 = rest.astype(bf16)
        q3 = (rest - q2.astype(f32)).astype(bf16)
        keys = cache[b, :, :HD]
        parts = nt_dot(jnp.concatenate([q1, q2, q3], axis=0), keys)
        scores = (parts[:HEADS_TP] + parts[HEADS_TP : 2 * HEADS_TP] + parts[2 * HEADS_TP :]) * factor
        scores = jnp.where(lane_iota(scores.shape) < lengths[b], scores, -1e30)
        newest = [(fresh[0:1], fresh[1:2])]
        if last:
            newest = [(before[2 * b : 2 * b + 1], before[2 * b + 1 : 2 * b + 2])] + newest
        extra = [jnp.sum(query * k, axis=1, keepdims=True) * factor for k, _ in newest]
        top = jnp.max(scores, axis=1, keepdims=True)
        for e in extra:
            top = jnp.maximum(top, e)
        expo = jnp.exp(scores - top)
        total = jnp.sum(expo, axis=1, keepdims=True)
        more = [jnp.exp(e - top) for e in extra]
        for e in more:
            total = total + e
        out = nn_dot((expo / total).astype(bf16), cache[b, :, HD:])
        for e, (_, v) in zip(more, newest):
            out = out + (e / total).astype(bf16).astype(f32) * v
        out = out.astype(bf16)
        rows.append(out)
        if last:
            flat = out.astype(f32)
            lows.append(
                jnp.concatenate([flat[h : h + 1] for h in range(HEADS_TP)], axis=1)
            )
    both = jnp.concatenate([r.astype(f32) for r in rows], axis=0)
    if last:
        low = jnp.concatenate(lows + [jnp.zeros((8 - ROLLS, HEADS_TP * HD), f32)], axis=0)
        low = nn_dot(low.astype(bf16), ab[...])
        attended[...] = jnp.concatenate([both, low], axis=0)
    else:
        attended[...] = jnp.broadcast_to(both.astype(bf16), attended.shape)
        kv_out[...] = jnp.concatenate(kvs + [jnp.zeros((8 - 2 * ROLLS, LANES), f32)], axis=0)


def attend(last, lengths, came, cache, *more):
    if last:
        out = (shape(24, LANES), shape(ROLLS * CHIP_COUNT, LANES))
    else:
        out = (shape(CHIP_COUNT, ROLLS * HEADS_TP, LANES, dtype=bf16), shape(8, LANES))
    args = (lengths, came, cache, *more)
    return call(
        lambda *refs: attend_kernel(last, *refs),
        out,
        [SMEM] + [VMEM] * (len(args) - 1),
        args,
        flops=2 * 32 * 2 * cache.shape[0] * cache.shape[1] * HD,
    )


def close_kernel(came, w_own, w_other, ab, out, held):
    rows = ROLLS * HEADS_TP
    held[...] = came[...].astype(f32).reshape(CHIP_COUNT * rows, LANES)
    blocks = []
    for b in range(ROLLS):
        heads = [
            held[pl.ds(b * HEADS_TP + h, CHIP_COUNT, stride=rows), :] for h in range(HEADS_TP)
        ]
        blocks.append(jnp.concatenate(heads, axis=1))
    everyone = jnp.concatenate(blocks, axis=0).astype(bf16)
    first = first_core()
    w_even = jnp.where(first, w_own[...], w_other[...])
    w_odd = jnp.where(first, w_other[...], w_own[...])
    w = jnp.concatenate([w_even, w_odd], axis=0)
    out[:, :LANES] = nt_dot(everyone, w)
    out[:, LANES:] = nn_dot(everyone, ab[...])


def adapter_kernel(
    rewards, prompts, live, own, other, rows, upstream, weighted_out, ab_out, part
):
    first = first_core()
    even = jnp.where(first, own[...], other[...])
    odd = jnp.where(first, other[...], own[...])
    ab_out[:, :PIECE, :] = even[:, :PIECE]
    ab_out[:, PIECE:, :] = odd[:, :PIECE]
    lane = lane_iota((CHIP_COUNT, LANES))
    seen = []
    for side in (own, other):
        tail = side[:, PIECE:, :].astype(f32)
        seen.append((tail[:, 2, :] + tail[:, 3, :] + tail[:, 4, :], tail[:, 5, :]))
    count = rows.shape[0]
    index = lax.broadcasted_iota(jnp.int32, (count, 1), 0)
    weight = jnp.zeros((count, 1), f32)
    for b in range(ROLLS):
        total = jnp.zeros((1, 1), f32)
        squares = jnp.zeros((1, 1), f32)
        for value, prompt in seen:
            hit = (prompt == prompts[b].astype(f32)) & (lane < ROLLS)
            value = jnp.where(hit, value, 0.0)
            total = total + jnp.sum(jnp.sum(value, axis=0, keepdims=True), axis=1, keepdims=True)
            value = value * value
            squares = squares + jnp.sum(
                jnp.sum(value, axis=0, keepdims=True), axis=1, keepdims=True
            )
        mean = total / GROUP
        std = jnp.sqrt(jnp.maximum(squares / GROUP - mean * mean, 0.09))
        per_roll = (rewards[b] - mean) / std / live[b].astype(f32)
        slot = index - b * COMP
        inside = (slot >= 0) & (slot < COMP) & (slot < live[b])
        weight = jnp.where(inside, per_roll, weight)
    weighted = (weight * upstream[...].astype(f32)).astype(bf16)
    weighted_out[...] = weighted
    ab = ab_out[...].reshape(2 * CHIP_COUNT * PIECE, LANES)
    low = nn_dot(rows[...], ab)
    back = nn_dot(weighted, ab)
    part[:count, :] = jnp.where(lane_iota((count, LANES)) < RANK, low, back)
    z = lax.axis_index("z")
    each = LANES // (2 * PIECE)
    piece = ab_out[pl.ds(z * each, each), :, :].reshape(LANES, LANES).astype(f32)
    piece = pltpu.roll(piece, RANK, 1)
    part[count:, :] = jnp.where(lane_iota((LANES, LANES)) < RANK, piece, 0.0)


def gradient_kernel(
    p0, p1, p2, p3, rows, weighted, state, low_back, joined, kept, given
):
    count = rows.shape[0]
    total = p0[:count, :] + p1[:count, :] + p2[:count, :] + p3[:count, :]
    low_back[...] = total.astype(bf16)
    turned = pltpu.roll(total, RANK, 1).astype(bf16)
    nt = lax.axis_size("t")
    from_y = lax.rem(lax.axis_index("t") - lax.axis_index("y") + nt, nt)
    piece = p0[count:, :]
    for by, p in ((1, p1), (2, p2), (3, p3)):
        piece = jnp.where(from_y == by, p[count:, :], piece)
    joined[: state.shape[0], :] = state[...]
    joined[state.shape[0] :, :] = piece
    a_side = tn_dot(rows[...], turned)
    b_side = tn_dot(weighted[...], turned)
    both = adapter_scale * jnp.where(lane_iota(a_side.shape) < RANK, a_side, b_side)
    both = both.reshape(CHIP_COUNT, 2 * PIECE, LANES)
    even, odd = both[:, :PIECE], both[:, PIECE:]
    first = first_core()
    kept[...] = jnp.where(first, even, odd)
    given[...] = jnp.where(first, odd, even)


def turned_up(b_ref):
    b = b_ref[...]
    b = jnp.where(lane_iota(b.shape) >= RANK, b, jnp.zeros_like(b))
    return pltpu.roll(b.astype(f32), RANK, 1)


def near_kernel(where_ref, own, left, right, w_ref, low, b_ref, out):
    acc = nt_dot(own[...], w_ref[where_ref[0]])
    acc = acc + nt_dot(left[...], w_ref[where_ref[1]])
    acc = acc + nt_dot(right[...], w_ref[where_ref[3]])
    out[...] = acc + adapter_scale * nt_dot(low[...], turned_up(b_ref).astype(bf16))


def near_rows(where, own, left, right, w, low, b):
    n, width, depth = w.shape
    rows = own.shape[0]
    tile = 256
    whole = lambda a: pl.BlockSpec(a.shape, lambda j, s: (0, 0))
    return pl.pallas_call(
        near_kernel,
        out_shape=shape(rows, width),
        grid_spec=pltpu.PrefetchScalarGridSpec(
            num_scalar_prefetch=1,
            grid=(width // tile,),
            in_specs=[
                whole(own),
                whole(left),
                whole(right),
                pl.BlockSpec((n, tile, depth), lambda j, s: (0, j, 0)),
                whole(low),
                pl.BlockSpec((tile, b.shape[1]), lambda j, s: (j, 0)),
            ],
            out_specs=pl.BlockSpec((rows, tile), lambda j, s: (0, j)),
        ),
        compiler_params=pltpu.CompilerParams(vmem_limit_bytes=GRANT << 20),
        cost_estimate=pl.CostEstimate(
            flops=2 * rows * width * depth * (n - 1),
            bytes_accessed=2 * (n * width * depth + n * rows * depth) + 4 * rows * width,
            transcendentals=0,
        ),
    )(where, own, left, right, w, low, b)


def last_kernel(
    where_ref, s0, s1, s2, s3, w_ref, b_ref, owned, near, far_a, far_b, out, rows_out, heads, acc
):
    sent = (s0, s1, s2, s3)
    k = pl.program_id(0)
    half = far_a.shape[0]
    mid = len(sent) // 2

    @pl.when(k == 0)
    def _():
        for i, s in enumerate(sent):
            flat = [
                jnp.concatenate(
                    [s[b * HEADS_TP + h : b * HEADS_TP + h + 1, :] for h in range(HEADS_TP)],
                    axis=1,
                )
                for b in range(ROLLS)
            ]
            flat.append(jnp.zeros((16 - ROLLS, HEADS_TP * HD), f32))
            heads[i] = jnp.concatenate(flat, axis=0).astype(bf16)
        acc[...] = jnp.zeros_like(acc)

    @pl.when(k != mid)
    def _():
        acc[...] += nt_dot(w_ref[0], heads[k])

    @pl.when(k == mid)
    def _():
        w = w_ref[0]
        acc[...] += nt_dot(w, heads[k])
        rows_out[:half, :] = near[:half, :] + nt_dot(far_a[...], w)
        rows_out[half:, :] = near[half:, :] + nt_dot(far_b[...], w)

    @pl.when(k == pl.num_programs(0) - 1)
    def _():
        top = ROLLS * HEADS_TP
        low = s0[top:, :] + s1[top:, :] + s2[top:, :] + s3[top:, :]
        got = acc[...].T[:8] + adapter_scale * nt_dot(low, turned_up(b_ref), precision=HIGH)
        out[...] = got
        out[:ROLLS, :] += owned[...]


def last_products(where, sent, w, b, owned, near, far_a, far_b):
    n, width, depth = w.shape
    whole = lambda a: pl.BlockSpec(a.shape, lambda k, s: (0, 0))
    return pl.pallas_call(
        last_kernel,
        out_shape=(shape(8, width), shape(*near.shape)),
        grid_spec=pltpu.PrefetchScalarGridSpec(
            num_scalar_prefetch=1,
            grid=(n,),
            in_specs=[
                *(whole(s) for s in sent),
                pl.BlockSpec((1, width, depth), lambda k, s: (s[k], 0, 0)),
                whole(b),
                pl.BlockSpec((ROLLS, width), lambda k, s: (0, s[0])),
                whole(near),
                whole(far_a),
                whole(far_b),
            ],
            out_specs=(
                pl.BlockSpec((8, width), lambda k, s: (0, 0)),
                whole(near),
            ),
            scratch_shapes=[
                pltpu.VMEM((n, 16, depth), bf16),
                pltpu.VMEM((width, 16), f32),
            ],
        ),
        compiler_params=pltpu.CompilerParams(vmem_limit_bytes=GRANT << 20),
        cost_estimate=pl.CostEstimate(
            flops=DECODE_HINT * 2 * 16 * width * depth * n,
            bytes_accessed=2 * n * width * depth,
            transcendentals=0,
        ),
    )(where, *sent, w, b, owned, near, far_a, far_b)


def place_kernel(c0, c1, c2, c3, out):
    width = c0.shape[1]
    nt = lax.axis_size("t")
    for k, part in enumerate((c0, c1, c2, c3)):
        block = lax.rem(lax.axis_index("t") - k + nt, nt)
        start = pl.multiple_of(block * width, width)
        out[:, pl.ds(start, width)] = part[:ROLLS, :]


def shards(
    hidden,
    attention_norm_gain,
    query_key_value_weight,
    key_value_cache,
    cache_fill_lengths,
    output_weight_frozen,
    adapter_down_transposed,
    adapter_up_matrix,
    attention_rows,
    upstream,
    rewards,
    prompt_group_index,
    completion_live_lengths,
):
    nt = lax.axis_size("t")
    t = lax.axis_index("t")
    width = hidden.shape[1]
    shard_width = width // nt
    cache = key_value_cache[:, :, 0, :]
    where = lax.rem(t - jnp.arange(nt, dtype=jnp.int32) + nt, nt)

    message = call(
        message_kernel,
        shape(CHIP_COUNT, FIRST_ROWS, LANES, dtype=bf16),
        [SMEM, SMEM, VMEM, VMEM, VMEM],
        (
            rewards,
            prompt_group_index,
            adapter_down_transposed[:, 0, :].T,
            adapter_up_matrix[:, 0, :].T,
            hidden,
        ),
    )

    w_rows = query_key_value_weight[:, 0, :]
    w_rows_other = swapped(w_rows)
    w_cols = output_weight_frozen[0].T
    w_cols_other = swapped(w_cols)

    ny = lax.axis_size("y")
    turned = lax.ppermute(
        w_cols, ("y", "t"), [(a * nt + b, b * nt + a) for a in range(ny) for b in range(nt)]
    )
    turned, message, where = together(turned, message, where)
    w_block = lax.all_gather(turned, DP, axis=0, tiled=True)
    w_block = w_block.reshape(nt, shard_width, w_cols.shape[1])


    arrived = exchange(message, CHIPS)
    gain = attention_norm_gain[None, :]
    sent, state, w_both = call(
        qkv_first_kernel,
        (
            shape(CHIP_COUNT * QKV_ROWS, LANES),
            shape(ROLLS * CHIP_COUNT, LANES),
            shape(2 * w_rows.shape[0], w_rows.shape[1], dtype=bf16),
        ),
        [VMEM] * 4,
        (arrived, gain, w_rows, w_rows_other),
        scratch=[pltpu.VMEM((CHIP_COUNT * FIRST_ROWS, LANES), f32)],
    )
    arrived_other = swapped(arrived)
    sent, arrived, arrived_other, own_rows = together(
        sent, arrived, arrived_other, attention_rows
    )
    came = exchange(sent.reshape(CHIP_COUNT, QKV_ROWS, LANES), CHIPS)

    left = shift(own_rows, 1, nt)
    right = shift(own_rows, nt - 1, nt)
    rows = attention_rows.shape[0]
    half = rows // 2
    weighted, ab, part = call(
        adapter_kernel,
        (
            shape(rows, shard_width, dtype=bf16),
            shape(CHIP_COUNT, 2 * PIECE, LANES, dtype=bf16),
            shape(rows + LANES, LANES),
        ),
        [SMEM] * 3 + [VMEM] * 4,
        (
            rewards,
            prompt_group_index,
            completion_live_lengths,
            arrived,
            arrived_other,
            attention_rows,
            upstream,
        ),
        flops=4 * rows * shard_width * LANES,
    )
    ab = ab.reshape(shard_width, LANES)
    parts = shifts(part, nt)

    attended, kv = attend(False, cache_fill_lengths, came.reshape(-1, LANES), cache)
    everyone = exchange(attended, CHIPS)

    share = call(
        close_kernel,
        shape(ROLLS * CHIP_COUNT, 2 * LANES),
        [VMEM] * 4,
        (everyone, w_cols, w_cols_other, ab),
        scratch=[pltpu.VMEM((CHIP_COUNT * ROLLS * HEADS_TP, LANES), f32)],
    )
    share, weighted = together(share, weighted)
    shares = shifts(share, nt)

    low_back, joined, kept, given = call(
        gradient_kernel,
        (
            shape(rows, LANES, dtype=bf16),
            shape(ROLLS * CHIP_COUNT + LANES, LANES),
            shape(CHIP_COUNT, PIECE, LANES),
            shape(CHIP_COUNT, PIECE, LANES),
        ),
        [VMEM] * 7,
        (*parts, attention_rows, weighted, state),
        flops=4 * rows * shard_width * LANES,
    )

    sent = call(
        qkv_later_kernel,
        shape(CHIP_COUNT * QKV_ROWS, LANES),
        [VMEM] * 7,
        (joined, gain, w_both, *shares),
    )
    sent, low_back, left_far, right_far = together(sent, low_back, left, right)
    came = exchange(sent.reshape(CHIP_COUNT, QKV_ROWS, LANES), CHIPS)

    far_a = shift(left_far[:half], 1, nt)
    far_b = shift(right_far[half:], nt - 1, nt)
    kept = kept + swapped(given)
    near = near_rows(where, attention_rows, left, right, w_block, low_back, ab)
    came, near = together(came, near)

    attended, owned = attend(True, cache_fill_lengths, came.reshape(-1, LANES), cache, kv, ab)
    attended, kept = together(attended, kept)
    summed = exchange(kept, CHIPS)
    cols, adapted = last_products(
        where, shifts(attended, nt), w_block, ab, owned.reshape(ROLLS, width), near, far_a, far_b
    )
    arriving = shifts(cols, nt)
    arriving[1], summed = together(arriving[1], summed)
    summed = summed.sum(axis=0)
    decoded = call(place_kernel, shape(ROLLS, width), [VMEM] * nt, tuple(arriving))
    grad_a = summed[:, :RANK].T[:, None, :]
    grad_b = summed[:, RANK:].T[:, None, :]
    return (decoded, adapted, grad_a, grad_b)


def solution(mesh):
    split = Mesh(mesh.devices.reshape(4, 8, 2, 4), ("y", "z", "c", "t"))
    placed = (
        P(DP, None),
        P(),
        P(DP, "t", None),
        P(DP, None, "t", None),
        P(DP),
        P("t", None, DP),
        P(None, "t", DP),
        P(None, "t", DP),
        P(DP, "t"),
        P(DP, "t"),
        P(DP),
        P(DP),
        P(DP),
    )
    return jax.shard_map(
        shards,
        mesh=split,
        in_specs=placed,
        out_specs=(P(DP, None), P(DP, "t"), P(None, "t", DP), P(None, "t", DP)),
        check_vma=False,
    )
```

```python
import math

import jax
import jax.numpy as jnp
from jax import lax
from jax.experimental import pallas as pl
from jax.experimental.pallas import tpu as pltpu
from jax.sharding import Mesh
from jax.sharding import PartitionSpec as P

HD = 128
HEADS_TP = 8
GROUP = 4
COMP = 256
RANK = 64
LANES = 128
ROLLS = 2
CHIP_COUNT = 32
PIECE = 16
FIRST_ROWS = 24
QKV_ROWS = 24
KEY_ROW = ROLLS * HEADS_TP
STATE_ROW = KEY_ROW + 2 * ROLLS
GRANT = 56
SMALL_GRANT = 24

adapter_scale = 2.0
f32 = jnp.float32
bf16 = jnp.bfloat16
CHIPS = ("y", "z")
DP = ("y", "z", "c")
HIGH = lax.Precision.HIGHEST
SMEM = pltpu.SMEM
VMEM = None


def nn_dot(a, b):
    return jnp.dot(a, b, preferred_element_type=f32)


def nt_dot(a, b, precision=None):
    return lax.dot_general(
        a, b, (((1,), (1,)), ((), ())), preferred_element_type=f32, precision=precision
    )


def tn_dot(a, b):
    return lax.dot_general(a, b, (((0,), (0,)), ((), ())), preferred_element_type=f32)


def swapped(x):
    return lax.ppermute(x, "c", [(0, 1), (1, 0)])


def shift(x, by, n):
    return lax.ppermute(x, "t", [(i, (i + by) % n) for i in range(n)])


def shifts(x, n):
    return [x] + [shift(x, by, n) for by in range(1, n)]


def exchange(x, axes):
    return lax.all_to_all(x, axes, split_axis=0, concat_axis=0, tiled=True)


def to_all(x, axes):
    return exchange(jnp.broadcast_to(x, (lax.axis_size(axes), *x.shape)), axes)


def together(*xs):
    return lax.optimization_barrier(xs)


def lane_iota(shape):
    return lax.broadcasted_iota(jnp.int32, shape, len(shape) - 1)


def call(kernel, out, specs, args, scratch=(), flops=0, grant=SMALL_GRANT):
    moved = sum(a.size * a.dtype.itemsize for a in args)
    outs = out if isinstance(out, tuple) else (out,)
    moved += sum(math.prod(o.shape) * o.dtype.itemsize for o in outs)
    whole = pl.BlockSpec()
    return pl.pallas_call(
        kernel,
        out_shape=out,
        in_specs=[pl.BlockSpec(memory_space=k) if k == SMEM else whole for k in specs],
        out_specs=tuple(whole for _ in outs) if isinstance(out, tuple) else whole,
        scratch_shapes=list(scratch),
        compiler_params=pltpu.CompilerParams(vmem_limit_bytes=grant << 20),
        cost_estimate=pl.CostEstimate(flops=flops, bytes_accessed=moved, transcendentals=0),
    )(*args)


def shape(*dims, dtype=f32):
    return jax.ShapeDtypeStruct(dims, dtype)


def message_kernel(rewards, prompts, a_ref, b_ref, hidden, out):
    pieces = jnp.concatenate([a_ref[...], b_ref[...]], axis=1)
    out[:, :PIECE, :] = jnp.broadcast_to(pieces, (CHIP_COUNT, PIECE, LANES))
    lane = lane_iota((1, LANES))
    value = jnp.where(lane == 0, rewards[0], jnp.where(lane == 1, rewards[1], 0.0))
    prompt = jnp.where(lane == 0, prompts[0], jnp.where(lane == 1, prompts[1], 0)).astype(f32)
    high = value.astype(bf16).astype(f32)
    mid = (value - high).astype(bf16).astype(f32)
    low = value - high - mid
    tail = jnp.concatenate([high, mid, low, prompt, jnp.zeros((2, LANES), f32)], axis=0)
    for m in range(CHIP_COUNT):
        cut = hidden[:, m * LANES : (m + 1) * LANES].astype(f32)
        out[m, PIECE:, :] = jnp.concatenate([cut, tail], axis=0).astype(bf16)


def spread_qkv(state, gain, w, out):
    x = state * gain
    x1 = x.astype(bf16)
    rest = x - x1.astype(f32)
    x2 = rest.astype(bf16)
    x3 = (rest - x2.astype(f32)).astype(bf16)
    count = x.shape[0]
    parts = nn_dot(jnp.concatenate([x1, x2, x3], axis=0), w)
    qkv = parts[:count] + parts[count : 2 * count] + parts[2 * count :]

    def put(row, block):
        out[pl.ds(row, CHIP_COUNT, stride=QKV_ROWS), :] = block

    for b in range(ROLLS):
        mine = qkv[b * CHIP_COUNT : (b + 1) * CHIP_COUNT]
        for h in range(HEADS_TP):
            put(b * HEADS_TP + h, mine[:, h * HD : (h + 1) * HD])
        put(KEY_ROW + 2 * b, mine[:, HEADS_TP * HD : (HEADS_TP + 1) * HD])
        put(KEY_ROW + 2 * b + 1, mine[:, (HEADS_TP + 1) * HD :])
        put(STATE_ROW + b, state[b * CHIP_COUNT : (b + 1) * CHIP_COUNT])
    for row in range(STATE_ROW + ROLLS, QKV_ROWS):
        put(row, jnp.zeros((CHIP_COUNT, LANES), f32))


def first_core():
    return lax.axis_index("c") == 0


def gain_of(gain):
    m = lax.axis_index("y") * lax.axis_size("z") + lax.axis_index("z")
    start = pl.multiple_of(m * LANES, LANES)
    return gain[:, pl.ds(start, LANES)].astype(f32)


def qkv_first_kernel(arrived, gain, w_own, w_other, out, state_out, w_out, held):
    held[...] = arrived[...].astype(f32).reshape(CHIP_COUNT * FIRST_ROWS, LANES)
    state = jnp.concatenate(
        [held[pl.ds(PIECE + b, CHIP_COUNT, stride=FIRST_ROWS), :] for b in range(ROLLS)], axis=0
    )
    state_out[...] = state
    first = first_core()
    rows = w_own.shape[0]
    w_out[:rows, :] = jnp.where(first, w_own[...], w_other[...])
    w_out[rows:, :] = jnp.where(first, w_other[...], w_own[...])
    spread_qkv(state, gain_of(gain), w_out[...], out)


def qkv_later_kernel(held, gain, w, s0, s1, s2, s3, out):
    share = s0[...] + s1[...] + s2[...] + s3[...]
    low = share[:, LANES:]
    count = share.shape[0]
    now = (
        held[:count, :]
        + share[:, :LANES]
        + adapter_scale * nt_dot(low, held[count:, :], precision=HIGH)
    )
    spread_qkv(now, gain_of(gain), w[...], out)


def attend_kernel(last, lengths, came, cache, *refs):
    if last:
        before, ab, attended, owned_out = refs
    else:
        attended, kv_out = refs
    sums = jnp.sum(came[...].reshape(CHIP_COUNT, QKV_ROWS, LANES), axis=0)
    factor = 1.0 / math.sqrt(HD)
    width = CHIP_COUNT * LANES
    rows = []
    lows = []
    kvs = []
    for b in range(ROLLS):
        owned = came[pl.ds(STATE_ROW + b, CHIP_COUNT, stride=QKV_ROWS), :]
        if last:
            owned_out[b * CHIP_COUNT : (b + 1) * CHIP_COUNT, :] = owned
        total = jnp.sum(jnp.sum(owned * owned, axis=0, keepdims=True), axis=1, keepdims=True)
        scale = lax.rsqrt(total * (1.0 / width) + 1e-05)
        query = sums[b * HEADS_TP : (b + 1) * HEADS_TP] * scale
        fresh = sums[KEY_ROW + 2 * b : KEY_ROW + 2 * b + 2] * scale
        kvs.append(fresh)
        q1 = query.astype(bf16)
        rest = query - q1.astype(f32)
        q2 = rest.astype(bf16)
        q3 = (rest - q2.astype(f32)).astype(bf16)
        keys = cache[b, :, :HD]
        parts = nt_dot(jnp.concatenate([q1, q2, q3], axis=0), keys)
        scores = (parts[:HEADS_TP] + parts[HEADS_TP : 2 * HEADS_TP] + parts[2 * HEADS_TP :]) * factor
        scores = jnp.where(lane_iota(scores.shape) < lengths[b], scores, -1e30)
        newest = [(fresh[0:1], fresh[1:2])]
        if last:
            newest = [(before[2 * b : 2 * b + 1], before[2 * b + 1 : 2 * b + 2])] + newest
        extra = [jnp.sum(query * k, axis=1, keepdims=True) * factor for k, _ in newest]
        top = jnp.max(scores, axis=1, keepdims=True)
        for e in extra:
            top = jnp.maximum(top, e)
        expo = jnp.exp(scores - top)
        total = jnp.sum(expo, axis=1, keepdims=True)
        more = [jnp.exp(e - top) for e in extra]
        for e in more:
            total = total + e
        out = nn_dot((expo / total).astype(bf16), cache[b, :, HD:])
        for e, (_, v) in zip(more, newest):
            out = out + (e / total).astype(bf16).astype(f32) * v
        out = out.astype(bf16)
        rows.append(out)
        if last:
            flat = out.astype(f32)
            lows.append(
                jnp.concatenate([flat[h : h + 1] for h in range(HEADS_TP)], axis=1)
            )
    both = jnp.concatenate([r.astype(f32) for r in rows], axis=0)
    if last:
        low = jnp.concatenate(lows + [jnp.zeros((8 - ROLLS, HEADS_TP * HD), f32)], axis=0)
        low = nn_dot(low.astype(bf16), ab[...])
        attended[...] = jnp.concatenate([both, low], axis=0)
    else:
        attended[...] = jnp.broadcast_to(both.astype(bf16), attended.shape)
        kv_out[...] = jnp.concatenate(kvs + [jnp.zeros((8 - 2 * ROLLS, LANES), f32)], axis=0)


def attend(last, lengths, came, cache, *more):
    if last:
        out = (shape(24, LANES), shape(ROLLS * CHIP_COUNT, LANES))
    else:
        out = (shape(CHIP_COUNT, ROLLS * HEADS_TP, LANES, dtype=bf16), shape(8, LANES))
    args = (lengths, came, cache, *more)
    return call(
        lambda *refs: attend_kernel(last, *refs),
        out,
        [SMEM] + [VMEM] * (len(args) - 1),
        args,
        flops=2 * 32 * 2 * cache.shape[0] * cache.shape[1] * HD,
    )


def close_kernel(came, w_own, w_other, ab, out, held):
    rows = ROLLS * HEADS_TP
    held[...] = came[...].astype(f32).reshape(CHIP_COUNT * rows, LANES)
    blocks = []
    for b in range(ROLLS):
        heads = [
            held[pl.ds(b * HEADS_TP + h, CHIP_COUNT, stride=rows), :] for h in range(HEADS_TP)
        ]
        blocks.append(jnp.concatenate(heads, axis=1))
    everyone = jnp.concatenate(blocks, axis=0).astype(bf16)
    first = first_core()
    w_even = jnp.where(first, w_own[...], w_other[...])
    w_odd = jnp.where(first, w_other[...], w_own[...])
    w = jnp.concatenate([w_even, w_odd], axis=0)
    out[:, :LANES] = nt_dot(everyone, w)
    out[:, LANES:] = nn_dot(everyone, ab[...])


def adapter_kernel(
    rewards, prompts, live, own, other, rows, upstream, weighted_out, ab_out, part
):
    first = first_core()
    even = jnp.where(first, own[...], other[...])
    odd = jnp.where(first, other[...], own[...])
    ab_out[:, :PIECE, :] = even[:, :PIECE]
    ab_out[:, PIECE:, :] = odd[:, :PIECE]
    lane = lane_iota((CHIP_COUNT, LANES))
    seen = []
    for side in (own, other):
        tail = side[:, PIECE:, :].astype(f32)
        seen.append((tail[:, 2, :] + tail[:, 3, :] + tail[:, 4, :], tail[:, 5, :]))
    count = rows.shape[0]
    index = lax.broadcasted_iota(jnp.int32, (count, 1), 0)
    weight = jnp.zeros((count, 1), f32)
    for b in range(ROLLS):
        total = jnp.zeros((1, 1), f32)
        squares = jnp.zeros((1, 1), f32)
        for value, prompt in seen:
            hit = (prompt == prompts[b].astype(f32)) & (lane < ROLLS)
            value = jnp.where(hit, value, 0.0)
            total = total + jnp.sum(jnp.sum(value, axis=0, keepdims=True), axis=1, keepdims=True)
            value = value * value
            squares = squares + jnp.sum(
                jnp.sum(value, axis=0, keepdims=True), axis=1, keepdims=True
            )
        mean = total / GROUP
        std = jnp.sqrt(jnp.maximum(squares / GROUP - mean * mean, 0.09))
        per_roll = (rewards[b] - mean) / std / live[b].astype(f32)
        slot = index - b * COMP
        inside = (slot >= 0) & (slot < COMP) & (slot < live[b])
        weight = jnp.where(inside, per_roll, weight)
    weighted = (weight * upstream[...].astype(f32)).astype(bf16)
    weighted_out[...] = weighted
    ab = ab_out[...].reshape(2 * CHIP_COUNT * PIECE, LANES)
    low = nn_dot(rows[...], ab)
    back = nn_dot(weighted, ab)
    part[:count, :] = jnp.where(lane_iota((count, LANES)) < RANK, low, back)
    z = lax.axis_index("z")
    each = LANES // (2 * PIECE)
    piece = ab_out[pl.ds(z * each, each), :, :].reshape(LANES, LANES).astype(f32)
    piece = pltpu.roll(piece, RANK, 1)
    part[count:, :] = jnp.where(lane_iota((LANES, LANES)) < RANK, piece, 0.0)


def gradient_kernel(
    p0, p1, p2, p3, rows, weighted, state, low_back, joined, kept, given
):
    count = rows.shape[0]
    total = p0[:count, :] + p1[:count, :] + p2[:count, :] + p3[:count, :]
    low_back[...] = total.astype(bf16)
    turned = pltpu.roll(total, RANK, 1).astype(bf16)
    nt = lax.axis_size("t")
    from_y = lax.rem(lax.axis_index("t") - lax.axis_index("y") + nt, nt)
    piece = p0[count:, :]
    for by, p in ((1, p1), (2, p2), (3, p3)):
        piece = jnp.where(from_y == by, p[count:, :], piece)
    joined[: state.shape[0], :] = state[...]
    joined[state.shape[0] :, :] = piece
    a_side = tn_dot(rows[...], turned)
    b_side = tn_dot(weighted[...], turned)
    both = adapter_scale * jnp.where(lane_iota(a_side.shape) < RANK, a_side, b_side)
    both = both.reshape(CHIP_COUNT, 2 * PIECE, LANES)
    even, odd = both[:, :PIECE], both[:, PIECE:]
    first = first_core()
    kept[...] = jnp.where(first, even, odd)
    given[...] = jnp.where(first, odd, even)


def turned_up(b_ref):
    b = b_ref[...]
    b = jnp.where(lane_iota(b.shape) >= RANK, b, jnp.zeros_like(b))
    return pltpu.roll(b.astype(f32), RANK, 1)


def rows_kernel(
    where_ref, own, left, right, far_a, far_b, w_ref, low, b_ref, s0, s1, s2, s3, owned, out, cols, x
):
    rows = own.shape[0]
    half = far_a.shape[0]
    sent = (s0, s1, s2, s3)

    @pl.when(pl.program_id(0) == 0)
    def _():
        x[0, :rows, :] = own[...]
        x[1, :rows, :] = left[...]
        x[2, :half, :] = far_a[...]
        x[2, half:rows, :] = far_b[...]
        x[3, :rows, :] = right[...]
        for k, s in enumerate(sent):
            flat = [
                jnp.concatenate(
                    [s[b * HEADS_TP + h : b * HEADS_TP + h + 1, :] for h in range(HEADS_TP)],
                    axis=1,
                )
                for b in range(ROLLS)
            ]
            flat.append(jnp.zeros((16 - ROLLS, HEADS_TP * HD), f32))
            x[k, rows:, :] = jnp.concatenate(flat, axis=0).astype(bf16)

    b_turned = turned_up(b_ref)
    acc = nt_dot(x[0], w_ref[where_ref[0]])
    for k in range(1, len(sent)):
        acc = acc + nt_dot(x[k], w_ref[where_ref[k]])
    out[...] = acc[:rows] + adapter_scale * nt_dot(low[...], b_turned.astype(bf16))
    top = ROLLS * HEADS_TP
    low_sum = s0[top:, :] + s1[top:, :] + s2[top:, :] + s3[top:, :]
    got = adapter_scale * nt_dot(low_sum, b_turned, precision=HIGH)
    cols[...] = got + acc[rows : rows + 8]
    cols[:ROLLS, :] += owned[...]


def output_rows(where, own, left, right, far_a, far_b, w, low, b, sent, owned):
    n, width, depth = w.shape
    rows = own.shape[0]
    tile = 256
    tiles = width // tile
    whole = lambda a: pl.BlockSpec(a.shape, lambda j, s: (0, 0))
    return pl.pallas_call(
        rows_kernel,
        out_shape=(shape(rows, width), shape(8, width)),
        grid_spec=pltpu.PrefetchScalarGridSpec(
            num_scalar_prefetch=1,
            grid=(tiles,),
            in_specs=[
                whole(own),
                whole(left),
                whole(right),
                whole(far_a),
                whole(far_b),
                pl.BlockSpec((n, tile, depth), lambda j, s: (0, j, 0)),
                whole(low),
                pl.BlockSpec((tile, b.shape[1]), lambda j, s: (j, 0)),
                *(whole(s) for s in sent),
                pl.BlockSpec((ROLLS, tile), lambda j, s: (0, s[0] * tiles + j)),
            ],
            out_specs=(
                pl.BlockSpec((rows, tile), lambda j, s: (0, j)),
                pl.BlockSpec((8, tile), lambda j, s: (0, j)),
            ),
            scratch_shapes=[pltpu.VMEM((n, rows + 16, depth), bf16)],
        ),
        compiler_params=pltpu.CompilerParams(vmem_limit_bytes=GRANT << 20),
        cost_estimate=pl.CostEstimate(
            flops=2 * rows * width * depth * n,
            bytes_accessed=2 * (n * width * depth + n * rows * depth) + 4 * rows * width,
            transcendentals=0,
        ),
    )(where, own, left, right, far_a, far_b, w, low, b, *sent, owned)


def place_kernel(c0, c1, c2, c3, out):
    width = c0.shape[1]
    nt = lax.axis_size("t")
    for k, part in enumerate((c0, c1, c2, c3)):
        block = lax.rem(lax.axis_index("t") - k + nt, nt)
        start = pl.multiple_of(block * width, width)
        out[:, pl.ds(start, width)] = part[:ROLLS, :]


def shards(
    hidden,
    attention_norm_gain,
    query_key_value_weight,
    key_value_cache,
    cache_fill_lengths,
    output_weight_frozen,
    adapter_down_transposed,
    adapter_up_matrix,
    attention_rows,
    upstream,
    rewards,
    prompt_group_index,
    completion_live_lengths,
):
    nt = lax.axis_size("t")
    t = lax.axis_index("t")
    width = hidden.shape[1]
    shard_width = width // nt
    cache = key_value_cache[:, :, 0, :]
    where = lax.rem(t - jnp.arange(nt, dtype=jnp.int32) + nt, nt)

    message = call(
        message_kernel,
        shape(CHIP_COUNT, FIRST_ROWS, LANES, dtype=bf16),
        [SMEM, SMEM, VMEM, VMEM, VMEM],
        (
            rewards,
            prompt_group_index,
            adapter_down_transposed[:, 0, :].T,
            adapter_up_matrix[:, 0, :].T,
            hidden,
        ),
    )

    w_rows = query_key_value_weight[:, 0, :]
    w_rows_other = swapped(w_rows)
    w_cols = output_weight_frozen[0].T
    w_cols_other = swapped(w_cols)

    ny = lax.axis_size("y")
    turned = lax.ppermute(
        w_cols, ("y", "t"), [(a * nt + b, b * nt + a) for a in range(ny) for b in range(nt)]
    )
    arrived = exchange(message, CHIPS)
    turned, _ = together(turned, arrived)
    w_block = lax.all_gather(turned, DP, axis=0, tiled=True)
    w_block = w_block.reshape(nt, shard_width, w_cols.shape[1])
    gain = attention_norm_gain[None, :]
    sent, state, w_both = call(
        qkv_first_kernel,
        (
            shape(CHIP_COUNT * QKV_ROWS, LANES),
            shape(ROLLS * CHIP_COUNT, LANES),
            shape(2 * w_rows.shape[0], w_rows.shape[1], dtype=bf16),
        ),
        [VMEM] * 4,
        (arrived, gain, w_rows, w_rows_other),
        scratch=[pltpu.VMEM((CHIP_COUNT * FIRST_ROWS, LANES), f32)],
    )
    arrived_other = swapped(arrived)
    sent, arrived, arrived_other, own_rows = together(
        sent, arrived, arrived_other, attention_rows
    )
    came = exchange(sent.reshape(CHIP_COUNT, QKV_ROWS, LANES), CHIPS)

    left = shift(own_rows, 1, nt)
    right = shift(own_rows, nt - 1, nt)
    rows = attention_rows.shape[0]
    half = rows // 2
    weighted, ab, part = call(
        adapter_kernel,
        (
            shape(rows, shard_width, dtype=bf16),
            shape(CHIP_COUNT, 2 * PIECE, LANES, dtype=bf16),
            shape(rows + LANES, LANES),
        ),
        [SMEM] * 3 + [VMEM] * 4,
        (
            rewards,
            prompt_group_index,
            completion_live_lengths,
            arrived,
            arrived_other,
            attention_rows,
            upstream,
        ),
        flops=4 * rows * shard_width * LANES,
    )
    ab = ab.reshape(shard_width, LANES)
    parts = shifts(part, nt)

    attended, kv = attend(False, cache_fill_lengths, came.reshape(-1, LANES), cache)
    everyone = exchange(attended, CHIPS)

    share = call(
        close_kernel,
        shape(ROLLS * CHIP_COUNT, 2 * LANES),
        [VMEM] * 4,
        (everyone, w_cols, w_cols_other, ab),
        scratch=[pltpu.VMEM((CHIP_COUNT * ROLLS * HEADS_TP, LANES), f32)],
    )
    share, weighted = together(share, weighted)
    shares = shifts(share, nt)

    low_back, joined, kept, given = call(
        gradient_kernel,
        (
            shape(rows, LANES, dtype=bf16),
            shape(ROLLS * CHIP_COUNT + LANES, LANES),
            shape(CHIP_COUNT, PIECE, LANES),
            shape(CHIP_COUNT, PIECE, LANES),
        ),
        [VMEM] * 7,
        (*parts, attention_rows, weighted, state),
        flops=4 * rows * shard_width * LANES,
    )

    sent = call(
        qkv_later_kernel,
        shape(CHIP_COUNT * QKV_ROWS, LANES),
        [VMEM] * 7,
        (joined, gain, w_both, *shares),
    )
    sent, low_back, left_far, right_far = together(sent, low_back, left, right)
    came = exchange(sent.reshape(CHIP_COUNT, QKV_ROWS, LANES), CHIPS)

    far_a = shift(left_far[:half], 1, nt)
    far_b = shift(right_far[half:], nt - 1, nt)
    kept = kept + swapped(given)

    attended, owned = attend(True, cache_fill_lengths, came.reshape(-1, LANES), cache, kv, ab)
    attended, kept = together(attended, kept)
    summed = exchange(kept, CHIPS)
    adapted, cols = output_rows(
        where,
        attention_rows,
        left,
        right,
        far_a,
        far_b,
        w_block,
        low_back,
        ab,
        shifts(attended, nt),
        owned.reshape(ROLLS, width),
    )
    arriving = shifts(cols, nt)
    arriving[1], summed = together(arriving[1], summed)
    summed = summed.sum(axis=0)
    decoded = call(place_kernel, shape(ROLLS, width), [VMEM] * nt, tuple(arriving))
    grad_a = summed[:, :RANK].T[:, None, :]
    grad_b = summed[:, RANK:].T[:, None, :]
    return (decoded, adapted, grad_a, grad_b)


def solution(mesh):
    split = Mesh(mesh.devices.reshape(4, 8, 2, 4), ("y", "z", "c", "t"))
    placed = (
        P(DP, None),
        P(),
        P(DP, "t", None),
        P(DP, None, "t", None),
        P(DP),
        P("t", None, DP),
        P(None, "t", DP),
        P(None, "t", DP),
        P(DP, "t"),
        P(DP, "t"),
        P(DP),
        P(DP),
        P(DP),
    )
    return jax.shard_map(
        shards,
        mesh=split,
        in_specs=placed,
        out_specs=(P(DP, None), P(DP, "t"), P(None, "t", DP), P(None, "t", DP)),
        check_vma=False,
    )
```

```python
import math

import jax
import jax.numpy as jnp
from jax import lax
from jax.experimental import pallas as pl
from jax.experimental.pallas import tpu as pltpu
from jax.sharding import Mesh
from jax.sharding import PartitionSpec as P

HD = 128
HEADS_TP = 8
GROUP = 4
COMP = 256
RANK = 64
LANES = 128
ROLLS = 2
CHIP_COUNT = 32
PIECE = 16
FIRST_ROWS = 24
QKV_ROWS = 24
KEY_ROW = ROLLS * HEADS_TP
STATE_ROW = KEY_ROW + 2 * ROLLS
GRANT = 56
SMALL_GRANT = 24

adapter_scale = 2.0
f32 = jnp.float32
bf16 = jnp.bfloat16
CHIPS = ("y", "z")
DP = ("y", "z", "c")
HIGH = lax.Precision.HIGHEST
SMEM = pltpu.SMEM
VMEM = None


def nn_dot(a, b):
    return jnp.dot(a, b, preferred_element_type=f32)


def nt_dot(a, b, precision=None):
    return lax.dot_general(
        a, b, (((1,), (1,)), ((), ())), preferred_element_type=f32, precision=precision
    )


def tn_dot(a, b):
    return lax.dot_general(a, b, (((0,), (0,)), ((), ())), preferred_element_type=f32)


def swapped(x):
    return lax.ppermute(x, "c", [(0, 1), (1, 0)])


def shift(x, by, n):
    return lax.ppermute(x, "t", [(i, (i + by) % n) for i in range(n)])


def shifts(x, n):
    return [x] + [shift(x, by, n) for by in range(1, n)]


def exchange(x, axes):
    return lax.all_to_all(x, axes, split_axis=0, concat_axis=0, tiled=True)


def to_all(x, axes):
    return exchange(jnp.broadcast_to(x, (lax.axis_size(axes), *x.shape)), axes)


def together(*xs):
    return lax.optimization_barrier(xs)


def lane_iota(shape):
    return lax.broadcasted_iota(jnp.int32, shape, len(shape) - 1)


def call(kernel, out, specs, args, scratch=(), flops=0, grant=SMALL_GRANT):
    moved = sum(a.size * a.dtype.itemsize for a in args)
    outs = out if isinstance(out, tuple) else (out,)
    moved += sum(math.prod(o.shape) * o.dtype.itemsize for o in outs)
    whole = pl.BlockSpec()
    return pl.pallas_call(
        kernel,
        out_shape=out,
        in_specs=[pl.BlockSpec(memory_space=k) if k == SMEM else whole for k in specs],
        out_specs=tuple(whole for _ in outs) if isinstance(out, tuple) else whole,
        scratch_shapes=list(scratch),
        compiler_params=pltpu.CompilerParams(vmem_limit_bytes=grant << 20),
        cost_estimate=pl.CostEstimate(flops=flops, bytes_accessed=moved, transcendentals=0),
    )(*args)


def shape(*dims, dtype=f32):
    return jax.ShapeDtypeStruct(dims, dtype)


def message_kernel(rewards, prompts, a_far, b_far, hidden_far, out_far, a_ref, b_ref, hidden, out, sem):
    pairs = ((a_far, a_ref), (b_far, b_ref), (hidden_far, hidden))
    copies = [pltpu.make_async_copy(p, q, sem.at[i]) for i, (p, q) in enumerate(pairs)]
    for copy in copies:
        copy.start()
    for copy in copies:
        copy.wait()
    pieces = jnp.concatenate([a_ref[...], b_ref[...]], axis=1)
    out[:, :PIECE, :] = jnp.broadcast_to(pieces, (CHIP_COUNT, PIECE, LANES))
    lane = lane_iota((1, LANES))
    value = jnp.where(lane == 0, rewards[0], jnp.where(lane == 1, rewards[1], 0.0))
    prompt = jnp.where(lane == 0, prompts[0], jnp.where(lane == 1, prompts[1], 0)).astype(f32)
    high = value.astype(bf16).astype(f32)
    mid = (value - high).astype(bf16).astype(f32)
    low = value - high - mid
    tail = jnp.concatenate([high, mid, low, prompt, jnp.zeros((2, LANES), f32)], axis=0)
    for m in range(CHIP_COUNT):
        cut = hidden[:, m * LANES : (m + 1) * LANES].astype(f32)
        out[m, PIECE:, :] = jnp.concatenate([cut, tail], axis=0).astype(bf16)
    copy = pltpu.make_async_copy(out, out_far, sem.at[len(pairs)])
    copy.start()
    copy.wait()


def first_message(rewards, prompts, a, b, hidden):
    out = shape(CHIP_COUNT, FIRST_ROWS, LANES, dtype=bf16)
    smem = pl.BlockSpec(memory_space=SMEM)
    hbm = pl.BlockSpec(memory_space=pltpu.HBM)
    return pl.pallas_call(
        message_kernel,
        out_shape=out,
        in_specs=[smem, smem, hbm, hbm, hbm],
        out_specs=hbm,
        scratch_shapes=[
            *(pltpu.VMEM(v.shape, v.dtype) for v in (a, b, hidden, out)),
            pltpu.SemaphoreType.DMA((4,)),
        ],
        compiler_params=pltpu.CompilerParams(vmem_limit_bytes=GRANT << 20),
    )(rewards, prompts, a, b, hidden)


def spread_qkv(state, gain, w, out):
    x = state * gain
    x1 = x.astype(bf16)
    rest = x - x1.astype(f32)
    x2 = rest.astype(bf16)
    x3 = (rest - x2.astype(f32)).astype(bf16)
    count = x.shape[0]
    parts = nn_dot(jnp.concatenate([x1, x2, x3], axis=0), w)
    qkv = parts[:count] + parts[count : 2 * count] + parts[2 * count :]

    def put(row, block):
        out[pl.ds(row, CHIP_COUNT, stride=QKV_ROWS), :] = block

    for b in range(ROLLS):
        mine = qkv[b * CHIP_COUNT : (b + 1) * CHIP_COUNT]
        for h in range(HEADS_TP):
            put(b * HEADS_TP + h, mine[:, h * HD : (h + 1) * HD])
        put(KEY_ROW + 2 * b, mine[:, HEADS_TP * HD : (HEADS_TP + 1) * HD])
        put(KEY_ROW + 2 * b + 1, mine[:, (HEADS_TP + 1) * HD :])
        put(STATE_ROW + b, state[b * CHIP_COUNT : (b + 1) * CHIP_COUNT])
    for row in range(STATE_ROW + ROLLS, QKV_ROWS):
        put(row, jnp.zeros((CHIP_COUNT, LANES), f32))


def first_core():
    return lax.axis_index("c") == 0


def gain_of(gain):
    m = lax.axis_index("y") * lax.axis_size("z") + lax.axis_index("z")
    start = pl.multiple_of(m * LANES, LANES)
    return gain[:, pl.ds(start, LANES)].astype(f32)


def state_of(arrived, held):
    held[...] = arrived[...].astype(f32).reshape(CHIP_COUNT * FIRST_ROWS, LANES)
    return jnp.concatenate(
        [held[pl.ds(PIECE + b, CHIP_COUNT, stride=FIRST_ROWS), :] for b in range(ROLLS)], axis=0
    )


def in_core_order(own, other):
    first = first_core()
    even = jnp.where(first, own[...], other[...])
    odd = jnp.where(first, other[...], own[...])
    return jnp.concatenate([even, odd], axis=0)


def qkv_first_kernel(arrived, gain, w_own, w_other, out, held):
    spread_qkv(state_of(arrived, held), gain_of(gain), in_core_order(w_own, w_other), out)


def qkv_later_kernel(held, gain, w, s0, s1, s2, s3, out):
    share = s0[...] + s1[...] + s2[...] + s3[...]
    low = share[:, LANES:]
    count = share.shape[0]
    now = (
        held[:count, :]
        + share[:, :LANES]
        + adapter_scale * nt_dot(low, held[count:, :], precision=HIGH)
    )
    spread_qkv(now, gain_of(gain), w[...], out)


def attend_kernel(last, lengths, came, cache, *refs):
    if last:
        before, ab, attended, owned_out = refs
    else:
        attended, kv_out = refs
    sums = jnp.sum(came[...].reshape(CHIP_COUNT, QKV_ROWS, LANES), axis=0)
    factor = 1.0 / math.sqrt(HD)
    width = CHIP_COUNT * LANES
    rows = []
    lows = []
    kvs = []
    for b in range(ROLLS):
        owned = came[pl.ds(STATE_ROW + b, CHIP_COUNT, stride=QKV_ROWS), :]
        if last:
            owned_out[b * CHIP_COUNT : (b + 1) * CHIP_COUNT, :] = owned
        total = jnp.sum(jnp.sum(owned * owned, axis=0, keepdims=True), axis=1, keepdims=True)
        scale = lax.rsqrt(total * (1.0 / width) + 1e-05)
        query = sums[b * HEADS_TP : (b + 1) * HEADS_TP] * scale
        fresh = sums[KEY_ROW + 2 * b : KEY_ROW + 2 * b + 2] * scale
        kvs.append(fresh)
        q1 = query.astype(bf16)
        rest = query - q1.astype(f32)
        q2 = rest.astype(bf16)
        q3 = (rest - q2.astype(f32)).astype(bf16)
        keys = cache[b, :, :HD]
        parts = nt_dot(jnp.concatenate([q1, q2, q3], axis=0), keys)
        scores = (parts[:HEADS_TP] + parts[HEADS_TP : 2 * HEADS_TP] + parts[2 * HEADS_TP :]) * factor
        scores = jnp.where(lane_iota(scores.shape) < lengths[b], scores, -1e30)
        newest = [(fresh[0:1], fresh[1:2])]
        if last:
            newest = [(before[2 * b : 2 * b + 1], before[2 * b + 1 : 2 * b + 2])] + newest
        extra = [jnp.sum(query * k, axis=1, keepdims=True) * factor for k, _ in newest]
        top = jnp.max(scores, axis=1, keepdims=True)
        for e in extra:
            top = jnp.maximum(top, e)
        expo = jnp.exp(scores - top)
        total = jnp.sum(expo, axis=1, keepdims=True)
        more = [jnp.exp(e - top) for e in extra]
        for e in more:
            total = total + e
        out = nn_dot((expo / total).astype(bf16), cache[b, :, HD:])
        for e, (_, v) in zip(more, newest):
            out = out + (e / total).astype(bf16).astype(f32) * v
        out = out.astype(bf16)
        rows.append(out)
        if last:
            flat = out.astype(f32)
            lows.append(
                jnp.concatenate([flat[h : h + 1] for h in range(HEADS_TP)], axis=1)
            )
    both = jnp.concatenate([r.astype(f32) for r in rows], axis=0)
    if last:
        low = jnp.concatenate(lows + [jnp.zeros((8 - ROLLS, HEADS_TP * HD), f32)], axis=0)
        low = nn_dot(low.astype(bf16), ab[...])
        attended[...] = jnp.concatenate([both, low], axis=0)
    else:
        attended[...] = jnp.broadcast_to(both.astype(bf16), attended.shape)
        kv_out[...] = jnp.concatenate(kvs + [jnp.zeros((8 - 2 * ROLLS, LANES), f32)], axis=0)


def attend(last, lengths, came, cache, *more):
    if last:
        out = (shape(24, LANES), shape(ROLLS * CHIP_COUNT, LANES))
    else:
        out = (shape(CHIP_COUNT, ROLLS * HEADS_TP, LANES, dtype=bf16), shape(8, LANES))
    args = (lengths, came, cache, *more)
    return call(
        lambda *refs: attend_kernel(last, *refs),
        out,
        [SMEM] + [VMEM] * (len(args) - 1),
        args,
        flops=2 * 32 * 2 * cache.shape[0] * cache.shape[1] * HD,
    )


def close_kernel(came, w_own, w_other, ab, out, held):
    rows = ROLLS * HEADS_TP
    held[...] = came[...].astype(f32).reshape(CHIP_COUNT * rows, LANES)
    blocks = []
    for b in range(ROLLS):
        heads = [
            held[pl.ds(b * HEADS_TP + h, CHIP_COUNT, stride=rows), :] for h in range(HEADS_TP)
        ]
        blocks.append(jnp.concatenate(heads, axis=1))
    everyone = jnp.concatenate(blocks, axis=0).astype(bf16)
    first = first_core()
    w_even = jnp.where(first, w_own[...], w_other[...])
    w_odd = jnp.where(first, w_other[...], w_own[...])
    w = jnp.concatenate([w_even, w_odd], axis=0)
    out[:, :LANES] = nt_dot(everyone, w)
    out[:, LANES:] = nn_dot(everyone, ab[...])


def adapter_kernel(
    rewards,
    prompts,
    live,
    own,
    other,
    rows,
    upstream,
    w_own,
    w_other,
    weighted_out,
    ab_out,
    part,
    state_out,
    w_out,
    held,
):
    state_out[...] = state_of(own, held)
    w_out[...] = in_core_order(w_own, w_other)
    first = first_core()
    even = jnp.where(first, own[...], other[...])
    odd = jnp.where(first, other[...], own[...])
    ab_out[:, :PIECE, :] = even[:, :PIECE]
    ab_out[:, PIECE:, :] = odd[:, :PIECE]
    lane = lane_iota((CHIP_COUNT, LANES))
    seen = []
    for side in (own, other):
        tail = side[:, PIECE:, :].astype(f32)
        seen.append((tail[:, 2, :] + tail[:, 3, :] + tail[:, 4, :], tail[:, 5, :]))
    count = rows.shape[0]
    index = lax.broadcasted_iota(jnp.int32, (count, 1), 0)
    weight = jnp.zeros((count, 1), f32)
    for b in range(ROLLS):
        total = jnp.zeros((1, 1), f32)
        squares = jnp.zeros((1, 1), f32)
        for value, prompt in seen:
            hit = (prompt == prompts[b].astype(f32)) & (lane < ROLLS)
            value = jnp.where(hit, value, 0.0)
            total = total + jnp.sum(jnp.sum(value, axis=0, keepdims=True), axis=1, keepdims=True)
            value = value * value
            squares = squares + jnp.sum(
                jnp.sum(value, axis=0, keepdims=True), axis=1, keepdims=True
            )
        mean = total / GROUP
        std = jnp.sqrt(jnp.maximum(squares / GROUP - mean * mean, 0.09))
        per_roll = (rewards[b] - mean) / std / live[b].astype(f32)
        slot = index - b * COMP
        inside = (slot >= 0) & (slot < COMP) & (slot < live[b])
        weight = jnp.where(inside, per_roll, weight)
    weighted = (weight * upstream[...].astype(f32)).astype(bf16)
    weighted_out[...] = weighted
    ab = ab_out[...].reshape(2 * CHIP_COUNT * PIECE, LANES)
    low = nn_dot(rows[...], ab)
    back = nn_dot(weighted, ab)
    part[:count, :] = jnp.where(lane_iota((count, LANES)) < RANK, low, back)
    z = lax.axis_index("z")
    each = LANES // (2 * PIECE)
    piece = ab_out[pl.ds(z * each, each), :, :].reshape(LANES, LANES).astype(f32)
    piece = pltpu.roll(piece, RANK, 1)
    part[count:, :] = jnp.where(lane_iota((LANES, LANES)) < RANK, piece, 0.0)


def gradient_kernel(
    p0, p1, p2, p3, rows, weighted, state, low_back, joined, kept, given
):
    count = rows.shape[0]
    total = p0[:count, :] + p1[:count, :] + p2[:count, :] + p3[:count, :]
    low_back[...] = total.astype(bf16)
    turned = pltpu.roll(total, RANK, 1).astype(bf16)
    nt = lax.axis_size("t")
    from_y = lax.rem(lax.axis_index("t") - lax.axis_index("y") + nt, nt)
    piece = p0[count:, :]
    for by, p in ((1, p1), (2, p2), (3, p3)):
        piece = jnp.where(from_y == by, p[count:, :], piece)
    joined[: state.shape[0], :] = state[...]
    joined[state.shape[0] :, :] = piece
    a_side = tn_dot(rows[...], turned)
    b_side = tn_dot(weighted[...], turned)
    both = adapter_scale * jnp.where(lane_iota(a_side.shape) < RANK, a_side, b_side)
    both = both.reshape(CHIP_COUNT, 2 * PIECE, LANES)
    even, odd = both[:, :PIECE], both[:, PIECE:]
    first = first_core()
    kept[...] = jnp.where(first, even, odd)
    given[...] = jnp.where(first, odd, even)


def turned_up(b_ref):
    b = b_ref[...]
    b = jnp.where(lane_iota(b.shape) >= RANK, b, jnp.zeros_like(b))
    return pltpu.roll(b.astype(f32), RANK, 1)


def rows_kernel(
    where_ref, own, left, right, far_a, far_b, w_ref, low, b_ref, s0, s1, s2, s3, owned, out, cols, x
):
    rows = own.shape[0]
    half = far_a.shape[0]
    sent = (s0, s1, s2, s3)

    @pl.when(pl.program_id(0) == 0)
    def _():
        x[0, :rows, :] = own[...]
        x[1, :rows, :] = left[...]
        x[2, :half, :] = far_a[...]
        x[2, half:rows, :] = far_b[...]
        x[3, :rows, :] = right[...]
        for k, s in enumerate(sent):
            flat = [
                jnp.concatenate(
                    [s[b * HEADS_TP + h : b * HEADS_TP + h + 1, :] for h in range(HEADS_TP)],
                    axis=1,
                )
                for b in range(ROLLS)
            ]
            flat.append(jnp.zeros((16 - ROLLS, HEADS_TP * HD), f32))
            x[k, rows:, :] = jnp.concatenate(flat, axis=0).astype(bf16)

    b_turned = turned_up(b_ref)
    acc = nt_dot(x[0], w_ref[where_ref[0]])
    for k in range(1, len(sent)):
        acc = acc + nt_dot(x[k], w_ref[where_ref[k]])
    out[...] = acc[:rows] + adapter_scale * nt_dot(low[...], b_turned.astype(bf16))
    top = ROLLS * HEADS_TP
    low_sum = s0[top:, :] + s1[top:, :] + s2[top:, :] + s3[top:, :]
    got = adapter_scale * nt_dot(low_sum, b_turned, precision=HIGH)
    cols[...] = got + acc[rows : rows + 8]
    cols[:ROLLS, :] += owned[...]


def output_rows(where, own, left, right, far_a, far_b, w, low, b, sent, owned):
    n, width, depth = w.shape
    rows = own.shape[0]
    tile = 256
    tiles = width // tile
    whole = lambda a: pl.BlockSpec(a.shape, lambda j, s: (0, 0))
    return pl.pallas_call(
        rows_kernel,
        out_shape=(shape(rows, width), shape(8, width)),
        grid_spec=pltpu.PrefetchScalarGridSpec(
            num_scalar_prefetch=1,
            grid=(tiles,),
            in_specs=[
                whole(own),
                whole(left),
                whole(right),
                whole(far_a),
                whole(far_b),
                pl.BlockSpec((n, tile, depth), lambda j, s: (0, j, 0)),
                whole(low),
                pl.BlockSpec((tile, b.shape[1]), lambda j, s: (j, 0)),
                *(whole(s) for s in sent),
                pl.BlockSpec((ROLLS, tile), lambda j, s: (0, s[0] * tiles + j)),
            ],
            out_specs=(
                pl.BlockSpec((rows, tile), lambda j, s: (0, j)),
                pl.BlockSpec((8, tile), lambda j, s: (0, j)),
            ),
            scratch_shapes=[pltpu.VMEM((n, rows + 16, depth), bf16)],
        ),
        compiler_params=pltpu.CompilerParams(vmem_limit_bytes=GRANT << 20),
        cost_estimate=pl.CostEstimate(
            flops=2 * rows * width * depth * n,
            bytes_accessed=2 * (n * width * depth + n * rows * depth) + 4 * rows * width,
            transcendentals=0,
        ),
    )(where, own, left, right, far_a, far_b, w, low, b, *sent, owned)


def place_kernel(c0, c1, c2, c3, out):
    width = c0.shape[1]
    nt = lax.axis_size("t")
    for k, part in enumerate((c0, c1, c2, c3)):
        block = lax.rem(lax.axis_index("t") - k + nt, nt)
        start = pl.multiple_of(block * width, width)
        out[:, pl.ds(start, width)] = part[:ROLLS, :]


def shards(
    hidden,
    attention_norm_gain,
    query_key_value_weight,
    key_value_cache,
    cache_fill_lengths,
    output_weight_frozen,
    adapter_down_transposed,
    adapter_up_matrix,
    attention_rows,
    upstream,
    rewards,
    prompt_group_index,
    completion_live_lengths,
):
    nt = lax.axis_size("t")
    t = lax.axis_index("t")
    width = hidden.shape[1]
    shard_width = width // nt
    cache = key_value_cache[:, :, 0, :]
    where = lax.rem(t - jnp.arange(nt, dtype=jnp.int32) + nt, nt)

    message = first_message(
        rewards,
        prompt_group_index,
        adapter_down_transposed[:, 0, :].T,
        adapter_up_matrix[:, 0, :].T,
        hidden,
    )

    w_rows = query_key_value_weight[:, 0, :]
    w_rows_other = swapped(w_rows)
    w_cols = output_weight_frozen[0].T
    w_cols_other = swapped(w_cols)

    ny = lax.axis_size("y")
    turned = lax.ppermute(
        w_cols, ("y", "t"), [(a * nt + b, b * nt + a) for a in range(ny) for b in range(nt)]
    )
    arrived = exchange(message, CHIPS)
    turned, gain, w_rows_other = together(turned, attention_norm_gain[None, :], w_rows_other)
    turned, _ = together(turned, arrived)
    w_block = lax.all_gather(turned, DP, axis=0, tiled=True)
    w_block = w_block.reshape(nt, shard_width, w_cols.shape[1])
    arrived, gain, w_rows_other = together(arrived, gain, w_rows_other)
    sent = call(
        qkv_first_kernel,
        shape(CHIP_COUNT * QKV_ROWS, LANES),
        [VMEM] * 4,
        (arrived, gain, w_rows, w_rows_other),
        scratch=[pltpu.VMEM((CHIP_COUNT * FIRST_ROWS, LANES), f32)],
    )
    arrived_other = swapped(arrived)
    sent, arrived, arrived_other, own_rows = together(
        sent, arrived, arrived_other, attention_rows
    )
    came = exchange(sent.reshape(CHIP_COUNT, QKV_ROWS, LANES), CHIPS)

    left = shift(own_rows, 1, nt)
    right = shift(own_rows, nt - 1, nt)
    rows = attention_rows.shape[0]
    half = rows // 2
    weighted, ab, part, state, w_both = call(
        adapter_kernel,
        (
            shape(rows, shard_width, dtype=bf16),
            shape(CHIP_COUNT, 2 * PIECE, LANES, dtype=bf16),
            shape(rows + LANES, LANES),
            shape(ROLLS * CHIP_COUNT, LANES),
            shape(2 * w_rows.shape[0], w_rows.shape[1], dtype=bf16),
        ),
        [SMEM] * 3 + [VMEM] * 6,
        (
            rewards,
            prompt_group_index,
            completion_live_lengths,
            arrived,
            arrived_other,
            attention_rows,
            upstream,
            w_rows,
            w_rows_other,
        ),
        scratch=[pltpu.VMEM((CHIP_COUNT * FIRST_ROWS, LANES), f32)],
        flops=4 * rows * shard_width * LANES,
    )
    ab = ab.reshape(shard_width, LANES)
    parts = shifts(part, nt)

    attended, kv = attend(False, cache_fill_lengths, came.reshape(-1, LANES), cache)
    everyone = exchange(attended, CHIPS)

    share = call(
        close_kernel,
        shape(ROLLS * CHIP_COUNT, 2 * LANES),
        [VMEM] * 4,
        (everyone, w_cols, w_cols_other, ab),
        scratch=[pltpu.VMEM((CHIP_COUNT * ROLLS * HEADS_TP, LANES), f32)],
    )
    share, weighted = together(share, weighted)
    shares = shifts(share, nt)

    low_back, joined, kept, given = call(
        gradient_kernel,
        (
            shape(rows, LANES, dtype=bf16),
            shape(ROLLS * CHIP_COUNT + LANES, LANES),
            shape(CHIP_COUNT, PIECE, LANES),
            shape(CHIP_COUNT, PIECE, LANES),
        ),
        [VMEM] * 7,
        (*parts, attention_rows, weighted, state),
        flops=4 * rows * shard_width * LANES,
    )

    sent = call(
        qkv_later_kernel,
        shape(CHIP_COUNT * QKV_ROWS, LANES),
        [VMEM] * 7,
        (joined, gain, w_both, *shares),
    )
    sent, low_back, left_far, right_far = together(sent, low_back, left, right)
    came = exchange(sent.reshape(CHIP_COUNT, QKV_ROWS, LANES), CHIPS)

    far_a = shift(left_far[:half], 1, nt)
    far_b = shift(right_far[half:], nt - 1, nt)
    kept = kept + swapped(given)

    attended, owned = attend(True, cache_fill_lengths, came.reshape(-1, LANES), cache, kv, ab)
    attended, kept = together(attended, kept)
    summed = exchange(kept, CHIPS)
    adapted, cols = output_rows(
        where,
        attention_rows,
        left,
        right,
        far_a,
        far_b,
        w_block,
        low_back,
        ab,
        shifts(attended, nt),
        owned.reshape(ROLLS, width),
    )
    arriving = shifts(cols, nt)
    arriving[1], summed = together(arriving[1], summed)
    summed = summed.sum(axis=0)
    decoded = call(place_kernel, shape(ROLLS, width), [VMEM] * nt, tuple(arriving))
    grad_a = summed[:, :RANK].T[:, None, :]
    grad_b = summed[:, RANK:].T[:, None, :]
    return (decoded, adapted, grad_a, grad_b)


def solution(mesh):
    split = Mesh(mesh.devices.reshape(4, 8, 2, 4), ("y", "z", "c", "t"))
    placed = (
        P(DP, None),
        P(),
        P(DP, "t", None),
        P(DP, None, "t", None),
        P(DP),
        P("t", None, DP),
        P(None, "t", DP),
        P(None, "t", DP),
        P(DP, "t"),
        P(DP, "t"),
        P(DP),
        P(DP),
        P(DP),
    )
    return jax.shard_map(
        shards,
        mesh=split,
        in_specs=placed,
        out_specs=(P(DP, None), P(DP, "t"), P(None, "t", DP), P(None, "t", DP)),
        check_vma=False,
    )
```

```python
import math

import jax
import jax.numpy as jnp
from jax import lax
from jax.experimental import pallas as pl
from jax.experimental.pallas import tpu as pltpu
from jax.sharding import Mesh
from jax.sharding import PartitionSpec as P

HD = 128
HEADS_TP = 8
GROUP = 4
COMP = 256
RANK = 64
LANES = 128
ROLLS = 2
CHIP_COUNT = 32
PIECE = 16
FIRST_ROWS = 24
QKV_ROWS = 24
KEY_ROW = ROLLS * HEADS_TP
STATE_ROW = KEY_ROW + 2 * ROLLS
GRANT = 56
SMALL_GRANT = 24

adapter_scale = 2.0
f32 = jnp.float32
bf16 = jnp.bfloat16
CHIPS = ("y", "z")
DP = ("y", "z", "c")
HIGH = lax.Precision.HIGHEST
SMEM = pltpu.SMEM
VMEM = None


def nn_dot(a, b):
    return jnp.dot(a, b, preferred_element_type=f32)


def nt_dot(a, b, precision=None):
    return lax.dot_general(
        a, b, (((1,), (1,)), ((), ())), preferred_element_type=f32, precision=precision
    )


def tn_dot(a, b):
    return lax.dot_general(a, b, (((0,), (0,)), ((), ())), preferred_element_type=f32)


def swapped(x):
    return lax.ppermute(x, "c", [(0, 1), (1, 0)])


def shift(x, by, n):
    return lax.ppermute(x, "t", [(i, (i + by) % n) for i in range(n)])


def shifts(x, n):
    return [x] + [shift(x, by, n) for by in range(1, n)]


def exchange(x, axes):
    return lax.all_to_all(x, axes, split_axis=0, concat_axis=0, tiled=True)


def to_all(x, axes):
    return exchange(jnp.broadcast_to(x, (lax.axis_size(axes), *x.shape)), axes)


def together(*xs):
    return lax.optimization_barrier(xs)


def lane_iota(shape):
    return lax.broadcasted_iota(jnp.int32, shape, len(shape) - 1)


def call(kernel, out, specs, args, scratch=(), flops=0, grant=SMALL_GRANT):
    moved = sum(a.size * a.dtype.itemsize for a in args)
    outs = out if isinstance(out, tuple) else (out,)
    moved += sum(math.prod(o.shape) * o.dtype.itemsize for o in outs)
    whole = pl.BlockSpec()
    return pl.pallas_call(
        kernel,
        out_shape=out,
        in_specs=[pl.BlockSpec(memory_space=k) if k == SMEM else whole for k in specs],
        out_specs=tuple(whole for _ in outs) if isinstance(out, tuple) else whole,
        scratch_shapes=list(scratch),
        compiler_params=pltpu.CompilerParams(vmem_limit_bytes=grant << 20),
        cost_estimate=pl.CostEstimate(flops=flops, bytes_accessed=moved, transcendentals=0),
    )(*args)


def shape(*dims, dtype=f32):
    return jax.ShapeDtypeStruct(dims, dtype)


def message_kernel(
    rewards, prompts, live, a_far, b_far, hidden_far, out_far, a_ref, b_ref, hidden, out, sem
):
    pairs = ((a_far, a_ref), (b_far, b_ref), (hidden_far, hidden))
    copies = [pltpu.make_async_copy(p, q, sem.at[i]) for i, (p, q) in enumerate(pairs)]
    for copy in copies:
        copy.start()
    for copy in copies:
        copy.wait()
    pieces = jnp.concatenate([a_ref[...], b_ref[...]], axis=1)
    out[:, :PIECE, :] = jnp.broadcast_to(pieces, (CHIP_COUNT, PIECE, LANES))
    lane = lane_iota((1, LANES))
    value = jnp.where(lane == 0, rewards[0], jnp.where(lane == 1, rewards[1], 0.0))
    prompt = jnp.where(lane == 0, prompts[0], jnp.where(lane == 1, prompts[1], 0)).astype(f32)
    length = jnp.where(lane == 0, live[0], jnp.where(lane == 1, live[1], 0)).astype(f32)
    high = value.astype(bf16).astype(f32)
    mid = (value - high).astype(bf16).astype(f32)
    low = value - high - mid
    tail = jnp.concatenate([high, mid, low, prompt, length, jnp.zeros((1, LANES), f32)], axis=0)
    for m in range(CHIP_COUNT):
        cut = hidden[:, m * LANES : (m + 1) * LANES].astype(f32)
        out[m, PIECE:, :] = jnp.concatenate([cut, tail], axis=0).astype(bf16)
    copy = pltpu.make_async_copy(out, out_far, sem.at[len(pairs)])
    copy.start()
    copy.wait()


def first_message(rewards, prompts, live, a, b, hidden):
    out = shape(CHIP_COUNT, FIRST_ROWS, LANES, dtype=bf16)
    smem = pl.BlockSpec(memory_space=SMEM)
    hbm = pl.BlockSpec(memory_space=pltpu.HBM)
    return pl.pallas_call(
        message_kernel,
        out_shape=out,
        in_specs=[smem, smem, smem, hbm, hbm, hbm],
        out_specs=hbm,
        scratch_shapes=[
            *(pltpu.VMEM(v.shape, v.dtype) for v in (a, b, hidden, out)),
            pltpu.SemaphoreType.DMA((4,)),
        ],
        compiler_params=pltpu.CompilerParams(vmem_limit_bytes=GRANT << 20),
    )(rewards, prompts, live, a, b, hidden)


def spread_qkv(state, gain, w, out):
    x = state * gain
    x1 = x.astype(bf16)
    rest = x - x1.astype(f32)
    x2 = rest.astype(bf16)
    x3 = (rest - x2.astype(f32)).astype(bf16)
    count = x.shape[0]
    parts = nn_dot(jnp.concatenate([x1, x2, x3], axis=0), w)
    qkv = parts[:count] + parts[count : 2 * count] + parts[2 * count :]

    def put(row, block):
        out[pl.ds(row, CHIP_COUNT, stride=QKV_ROWS), :] = block

    for b in range(ROLLS):
        mine = qkv[b * CHIP_COUNT : (b + 1) * CHIP_COUNT]
        for h in range(HEADS_TP):
            put(b * HEADS_TP + h, mine[:, h * HD : (h + 1) * HD])
        put(KEY_ROW + 2 * b, mine[:, HEADS_TP * HD : (HEADS_TP + 1) * HD])
        put(KEY_ROW + 2 * b + 1, mine[:, (HEADS_TP + 1) * HD :])
        put(STATE_ROW + b, state[b * CHIP_COUNT : (b + 1) * CHIP_COUNT])
    for row in range(STATE_ROW + ROLLS, QKV_ROWS):
        put(row, jnp.zeros((CHIP_COUNT, LANES), f32))


def first_core():
    return lax.axis_index("c") == 0


def gain_of(gain):
    m = lax.axis_index("y") * lax.axis_size("z") + lax.axis_index("z")
    start = pl.multiple_of(m * LANES, LANES)
    return gain[:, pl.ds(start, LANES)].astype(f32)


def state_of(arrived, held):
    held[...] = arrived[...].astype(f32).reshape(CHIP_COUNT * FIRST_ROWS, LANES)
    return jnp.concatenate(
        [held[pl.ds(PIECE + b, CHIP_COUNT, stride=FIRST_ROWS), :] for b in range(ROLLS)], axis=0
    )


def in_core_order(own, other):
    first = first_core()
    even = jnp.where(first, own[...], other[...])
    odd = jnp.where(first, other[...], own[...])
    return jnp.concatenate([even, odd], axis=0)


def qkv_first_kernel(arrived, gain, w_own, w_other, out, held):
    spread_qkv(state_of(arrived, held), gain_of(gain), in_core_order(w_own, w_other), out)


def qkv_later_kernel(held, gain, w, s0, s1, s2, s3, out):
    share = s0[...] + s1[...] + s2[...] + s3[...]
    low = share[:, LANES:]
    count = share.shape[0]
    now = (
        held[:count, :]
        + share[:, :LANES]
        + adapter_scale * nt_dot(low, held[count:, :], precision=HIGH)
    )
    spread_qkv(now, gain_of(gain), w[...], out)


def attend_kernel(last, lengths, came, cache, *refs):
    if last:
        before, ab, attended, owned_out = refs
    else:
        attended, kv_out = refs
    sums = jnp.sum(came[...].reshape(CHIP_COUNT, QKV_ROWS, LANES), axis=0)
    factor = 1.0 / math.sqrt(HD)
    width = CHIP_COUNT * LANES
    rows = []
    lows = []
    kvs = []
    for b in range(ROLLS):
        owned = came[pl.ds(STATE_ROW + b, CHIP_COUNT, stride=QKV_ROWS), :]
        if last:
            owned_out[b * CHIP_COUNT : (b + 1) * CHIP_COUNT, :] = owned
        total = jnp.sum(jnp.sum(owned * owned, axis=0, keepdims=True), axis=1, keepdims=True)
        scale = lax.rsqrt(total * (1.0 / width) + 1e-05)
        query = sums[b * HEADS_TP : (b + 1) * HEADS_TP] * scale
        fresh = sums[KEY_ROW + 2 * b : KEY_ROW + 2 * b + 2] * scale
        kvs.append(fresh)
        q1 = query.astype(bf16)
        rest = query - q1.astype(f32)
        q2 = rest.astype(bf16)
        q3 = (rest - q2.astype(f32)).astype(bf16)
        keys = cache[b, :, :HD]
        parts = nt_dot(jnp.concatenate([q1, q2, q3], axis=0), keys)
        scores = (parts[:HEADS_TP] + parts[HEADS_TP : 2 * HEADS_TP] + parts[2 * HEADS_TP :]) * factor
        scores = jnp.where(lane_iota(scores.shape) < lengths[b], scores, -1e30)
        newest = [(fresh[0:1], fresh[1:2])]
        if last:
            newest = [(before[2 * b : 2 * b + 1], before[2 * b + 1 : 2 * b + 2])] + newest
        extra = [jnp.sum(query * k, axis=1, keepdims=True) * factor for k, _ in newest]
        top = jnp.max(scores, axis=1, keepdims=True)
        for e in extra:
            top = jnp.maximum(top, e)
        expo = jnp.exp(scores - top)
        total = jnp.sum(expo, axis=1, keepdims=True)
        more = [jnp.exp(e - top) for e in extra]
        for e in more:
            total = total + e
        out = nn_dot((expo / total).astype(bf16), cache[b, :, HD:])
        for e, (_, v) in zip(more, newest):
            out = out + (e / total).astype(bf16).astype(f32) * v
        out = out.astype(bf16)
        rows.append(out)
        if last:
            flat = out.astype(f32)
            lows.append(
                jnp.concatenate([flat[h : h + 1] for h in range(HEADS_TP)], axis=1)
            )
    both = jnp.concatenate([r.astype(f32) for r in rows], axis=0)
    if last:
        low = jnp.concatenate(lows + [jnp.zeros((8 - ROLLS, HEADS_TP * HD), f32)], axis=0)
        low = nn_dot(low.astype(bf16), ab[...])
        attended[...] = jnp.concatenate([both, low], axis=0)
    else:
        attended[...] = jnp.broadcast_to(both.astype(bf16), attended.shape)
        kv_out[...] = jnp.concatenate(kvs + [jnp.zeros((8 - 2 * ROLLS, LANES), f32)], axis=0)


def attend(last, lengths, came, cache, *more):
    if last:
        out = (shape(24, LANES), shape(ROLLS * CHIP_COUNT, LANES))
    else:
        out = (shape(CHIP_COUNT, ROLLS * HEADS_TP, LANES, dtype=bf16), shape(8, LANES))
    args = (lengths, came, cache, *more)
    return call(
        lambda *refs: attend_kernel(last, *refs),
        out,
        [SMEM] + [VMEM] * (len(args) - 1),
        args,
        flops=2 * 32 * 2 * cache.shape[0] * cache.shape[1] * HD,
    )


def close_kernel(came, w_own, w_other, ab, out, held):
    rows = ROLLS * HEADS_TP
    held[...] = came[...].astype(f32).reshape(CHIP_COUNT * rows, LANES)
    blocks = []
    for b in range(ROLLS):
        heads = [
            held[pl.ds(b * HEADS_TP + h, CHIP_COUNT, stride=rows), :] for h in range(HEADS_TP)
        ]
        blocks.append(jnp.concatenate(heads, axis=1))
    everyone = jnp.concatenate(blocks, axis=0).astype(bf16)
    first = first_core()
    w_even = jnp.where(first, w_own[...], w_other[...])
    w_odd = jnp.where(first, w_other[...], w_own[...])
    w = jnp.concatenate([w_even, w_odd], axis=0)
    out[:, :LANES] = nt_dot(everyone, w)
    out[:, LANES:] = nn_dot(everyone, ab[...])


def adapter_kernel(
    own, other, rows, upstream, w_own, w_other, weighted_out, ab_out, part, state_out, w_out, held
):
    state_out[...] = state_of(own, held)
    w_out[...] = in_core_order(w_own, w_other)
    first = first_core()
    even = jnp.where(first, own[...], other[...])
    odd = jnp.where(first, other[...], own[...])
    ab_out[:, :PIECE, :] = even[:, :PIECE]
    ab_out[:, PIECE:, :] = odd[:, :PIECE]
    lane = lane_iota((CHIP_COUNT, LANES))
    seen = []
    for side in (own, other):
        tail = side[:, PIECE:, :].astype(f32)
        seen.append((tail[:, 2, :] + tail[:, 3, :] + tail[:, 4, :], tail[:, 5, :]))
    m = lax.axis_index("y") * lax.axis_size("z") + lax.axis_index("z")
    mine = own[pl.ds(m, 1), PIECE:, :].astype(f32).reshape(8, LANES)
    count = rows.shape[0]
    index = lax.broadcasted_iota(jnp.int32, (count, 1), 0)
    weight = jnp.zeros((count, 1), f32)
    for b in range(ROLLS):
        reward = mine[2:3, b : b + 1] + mine[3:4, b : b + 1] + mine[4:5, b : b + 1]
        live = mine[6:7, b : b + 1]
        total = jnp.zeros((1, 1), f32)
        squares = jnp.zeros((1, 1), f32)
        for value, prompt in seen:
            hit = (prompt == mine[5:6, b : b + 1]) & (lane < ROLLS)
            value = jnp.where(hit, value, 0.0)
            total = total + jnp.sum(jnp.sum(value, axis=0, keepdims=True), axis=1, keepdims=True)
            value = value * value
            squares = squares + jnp.sum(
                jnp.sum(value, axis=0, keepdims=True), axis=1, keepdims=True
            )
        mean = total / GROUP
        std = jnp.sqrt(jnp.maximum(squares / GROUP - mean * mean, 0.09))
        per_roll = (reward - mean) / std / live
        slot = index - b * COMP
        inside = (slot >= 0) & (slot < COMP) & (slot < live.astype(jnp.int32))
        weight = jnp.where(inside, per_roll, weight)
    weighted = (weight * upstream[...].astype(f32)).astype(bf16)
    weighted_out[...] = weighted
    ab = ab_out[...].reshape(2 * CHIP_COUNT * PIECE, LANES)
    low = nn_dot(rows[...], ab)
    back = nn_dot(weighted, ab)
    part[:count, :] = jnp.where(lane_iota((count, LANES)) < RANK, low, back)
    z = lax.axis_index("z")
    each = LANES // (2 * PIECE)
    piece = ab_out[pl.ds(z * each, each), :, :].reshape(LANES, LANES).astype(f32)
    piece = pltpu.roll(piece, RANK, 1)
    part[count:, :] = jnp.where(lane_iota((LANES, LANES)) < RANK, piece, 0.0)


def gradient_kernel(
    p0, p1, p2, p3, rows, weighted, state, low_back, joined, kept, given
):
    count = rows.shape[0]
    total = p0[:count, :] + p1[:count, :] + p2[:count, :] + p3[:count, :]
    low_back[...] = total.astype(bf16)
    turned = pltpu.roll(total, RANK, 1).astype(bf16)
    nt = lax.axis_size("t")
    from_y = lax.rem(lax.axis_index("t") - lax.axis_index("y") + nt, nt)
    piece = p0[count:, :]
    for by, p in ((1, p1), (2, p2), (3, p3)):
        piece = jnp.where(from_y == by, p[count:, :], piece)
    joined[: state.shape[0], :] = state[...]
    joined[state.shape[0] :, :] = piece
    a_side = tn_dot(rows[...], turned)
    b_side = tn_dot(weighted[...], turned)
    both = adapter_scale * jnp.where(lane_iota(a_side.shape) < RANK, a_side, b_side)
    both = both.reshape(CHIP_COUNT, 2 * PIECE, LANES)
    even, odd = both[:, :PIECE], both[:, PIECE:]
    first = first_core()
    kept[...] = jnp.where(first, even, odd)
    given[...] = jnp.where(first, odd, even)


def turned_up(b_ref):
    b = b_ref[...]
    b = jnp.where(lane_iota(b.shape) >= RANK, b, jnp.zeros_like(b))
    return pltpu.roll(b.astype(f32), RANK, 1)


def rows_kernel(
    where_ref, own, left, right, far_a, far_b, w_ref, low, b_ref, s0, s1, s2, s3, owned, out, cols, x
):
    rows = own.shape[0]
    half = far_a.shape[0]
    sent = (s0, s1, s2, s3)

    @pl.when(pl.program_id(0) == 0)
    def _():
        x[0, :rows, :] = own[...]
        x[1, :rows, :] = left[...]
        x[2, :half, :] = far_a[...]
        x[2, half:rows, :] = far_b[...]
        x[3, :rows, :] = right[...]
        for k, s in enumerate(sent):
            flat = [
                jnp.concatenate(
                    [s[b * HEADS_TP + h : b * HEADS_TP + h + 1, :] for h in range(HEADS_TP)],
                    axis=1,
                )
                for b in range(ROLLS)
            ]
            flat.append(jnp.zeros((16 - ROLLS, HEADS_TP * HD), f32))
            x[k, rows:, :] = jnp.concatenate(flat, axis=0).astype(bf16)

    b_turned = turned_up(b_ref)
    acc = nt_dot(x[0], w_ref[where_ref[0]])
    for k in range(1, len(sent)):
        acc = acc + nt_dot(x[k], w_ref[where_ref[k]])
    out[...] = acc[:rows] + adapter_scale * nt_dot(low[...], b_turned.astype(bf16))
    top = ROLLS * HEADS_TP
    low_sum = s0[top:, :] + s1[top:, :] + s2[top:, :] + s3[top:, :]
    got = adapter_scale * nt_dot(low_sum, b_turned, precision=HIGH)
    cols[...] = got + acc[rows : rows + 8]
    cols[:ROLLS, :] += owned[...]


def output_rows(where, own, left, right, far_a, far_b, w, low, b, sent, owned):
    n, width, depth = w.shape
    rows = own.shape[0]
    tile = 256
    tiles = width // tile
    whole = lambda a: pl.BlockSpec(a.shape, lambda j, s: (0, 0))
    return pl.pallas_call(
        rows_kernel,
        out_shape=(shape(rows, width), shape(8, width)),
        grid_spec=pltpu.PrefetchScalarGridSpec(
            num_scalar_prefetch=1,
            grid=(tiles,),
            in_specs=[
                whole(own),
                whole(left),
                whole(right),
                whole(far_a),
                whole(far_b),
                pl.BlockSpec((n, tile, depth), lambda j, s: (0, j, 0)),
                whole(low),
                pl.BlockSpec((tile, b.shape[1]), lambda j, s: (j, 0)),
                *(whole(s) for s in sent),
                pl.BlockSpec((ROLLS, tile), lambda j, s: (0, s[0] * tiles + j)),
            ],
            out_specs=(
                pl.BlockSpec((rows, tile), lambda j, s: (0, j)),
                pl.BlockSpec((8, tile), lambda j, s: (0, j)),
            ),
            scratch_shapes=[pltpu.VMEM((n, rows + 16, depth), bf16)],
        ),
        compiler_params=pltpu.CompilerParams(vmem_limit_bytes=GRANT << 20),
        cost_estimate=pl.CostEstimate(
            flops=2 * rows * width * depth * n,
            bytes_accessed=2 * (n * width * depth + n * rows * depth) + 4 * rows * width,
            transcendentals=0,
        ),
    )(where, own, left, right, far_a, far_b, w, low, b, *sent, owned)


def place_kernel(c0, c1, c2, c3, out):
    width = c0.shape[1]
    nt = lax.axis_size("t")
    for k, part in enumerate((c0, c1, c2, c3)):
        block = lax.rem(lax.axis_index("t") - k + nt, nt)
        start = pl.multiple_of(block * width, width)
        out[:, pl.ds(start, width)] = part[:ROLLS, :]


def shards(
    hidden,
    attention_norm_gain,
    query_key_value_weight,
    key_value_cache,
    cache_fill_lengths,
    output_weight_frozen,
    adapter_down_transposed,
    adapter_up_matrix,
    attention_rows,
    upstream,
    rewards,
    prompt_group_index,
    completion_live_lengths,
):
    nt = lax.axis_size("t")
    t = lax.axis_index("t")
    width = hidden.shape[1]
    shard_width = width // nt
    cache = key_value_cache[:, :, 0, :]
    where = lax.rem(t - jnp.arange(nt, dtype=jnp.int32) + nt, nt)

    message = first_message(
        rewards,
        prompt_group_index,
        completion_live_lengths,
        adapter_down_transposed[:, 0, :].T,
        adapter_up_matrix[:, 0, :].T,
        hidden,
    )

    w_rows = query_key_value_weight[:, 0, :]
    w_rows_other = swapped(w_rows)
    w_cols = output_weight_frozen[0].T
    w_cols_other = swapped(w_cols)

    ny = lax.axis_size("y")
    turned = lax.ppermute(
        w_cols, ("y", "t"), [(a * nt + b, b * nt + a) for a in range(ny) for b in range(nt)]
    )
    arrived = exchange(message, CHIPS)
    gain = attention_norm_gain[None, :]
    arrived, gain, w_rows_other = together(arrived, gain, w_rows_other)
    sent = call(
        qkv_first_kernel,
        shape(CHIP_COUNT * QKV_ROWS, LANES),
        [VMEM] * 4,
        (arrived, gain, w_rows, w_rows_other),
        scratch=[pltpu.VMEM((CHIP_COUNT * FIRST_ROWS, LANES), f32)],
    )
    turned, _ = together(turned, sent)
    w_block = lax.all_gather(turned, DP, axis=0, tiled=True)
    w_block = w_block.reshape(nt, shard_width, w_cols.shape[1])
    sent, arrived, own_rows = together(sent, arrived, attention_rows)
    arrived_other = swapped(arrived)
    came = exchange(sent.reshape(CHIP_COUNT, QKV_ROWS, LANES), CHIPS)

    left = shift(own_rows, 1, nt)
    right = shift(own_rows, nt - 1, nt)
    rows = attention_rows.shape[0]
    half = rows // 2
    weighted, ab, part, state, w_both = call(
        adapter_kernel,
        (
            shape(rows, shard_width, dtype=bf16),
            shape(CHIP_COUNT, 2 * PIECE, LANES, dtype=bf16),
            shape(rows + LANES, LANES),
            shape(ROLLS * CHIP_COUNT, LANES),
            shape(2 * w_rows.shape[0], w_rows.shape[1], dtype=bf16),
        ),
        [VMEM] * 6,
        (arrived, arrived_other, attention_rows, upstream, w_rows, w_rows_other),
        scratch=[pltpu.VMEM((CHIP_COUNT * FIRST_ROWS, LANES), f32)],
        flops=4 * rows * shard_width * LANES,
    )
    ab = ab.reshape(shard_width, LANES)
    parts = shifts(part, nt)

    attended, kv = attend(False, cache_fill_lengths, came.reshape(-1, LANES), cache)
    everyone = exchange(attended, CHIPS)

    share = call(
        close_kernel,
        shape(ROLLS * CHIP_COUNT, 2 * LANES),
        [VMEM] * 4,
        (everyone, w_cols, w_cols_other, ab),
        scratch=[pltpu.VMEM((CHIP_COUNT * ROLLS * HEADS_TP, LANES), f32)],
    )
    share, weighted = together(share, weighted)
    shares = shifts(share, nt)

    low_back, joined, kept, given = call(
        gradient_kernel,
        (
            shape(rows, LANES, dtype=bf16),
            shape(ROLLS * CHIP_COUNT + LANES, LANES),
            shape(CHIP_COUNT, PIECE, LANES),
            shape(CHIP_COUNT, PIECE, LANES),
        ),
        [VMEM] * 7,
        (*parts, attention_rows, weighted, state),
        flops=4 * rows * shard_width * LANES,
    )

    sent = call(
        qkv_later_kernel,
        shape(CHIP_COUNT * QKV_ROWS, LANES),
        [VMEM] * 7,
        (joined, gain, w_both, *shares),
    )
    sent, low_back, left_far, right_far = together(sent, low_back, left, right)
    came = exchange(sent.reshape(CHIP_COUNT, QKV_ROWS, LANES), CHIPS)

    far_a = shift(left_far[:half], 1, nt)
    far_b = shift(right_far[half:], nt - 1, nt)
    kept = kept + swapped(given)

    attended, owned = attend(True, cache_fill_lengths, came.reshape(-1, LANES), cache, kv, ab)
    attended, kept = together(attended, kept)
    summed = exchange(kept, CHIPS)
    adapted, cols = output_rows(
        where,
        attention_rows,
        left,
        right,
        far_a,
        far_b,
        w_block,
        low_back,
        ab,
        shifts(attended, nt),
        owned.reshape(ROLLS, width),
    )
    arriving = shifts(cols, nt)
    arriving[1], summed = together(arriving[1], summed)
    summed = summed.sum(axis=0)
    decoded = call(place_kernel, shape(ROLLS, width), [VMEM] * nt, tuple(arriving))
    grad_a = summed[:, :RANK].T[:, None, :]
    grad_b = summed[:, RANK:].T[:, None, :]
    return (decoded, adapted, grad_a, grad_b)


def solution(mesh):
    split = Mesh(mesh.devices.reshape(4, 8, 2, 4), ("y", "z", "c", "t"))
    placed = (
        P(DP, None),
        P(),
        P(DP, "t", None),
        P(DP, None, "t", None),
        P(DP),
        P("t", None, DP),
        P(None, "t", DP),
        P(None, "t", DP),
        P(DP, "t"),
        P(DP, "t"),
        P(DP),
        P(DP),
        P(DP),
    )
    return jax.shard_map(
        shards,
        mesh=split,
        in_specs=placed,
        out_specs=(P(DP, None), P(DP, "t"), P(None, "t", DP), P(None, "t", DP)),
        check_vma=False,
    )
```

```python
import math

import jax
import jax.numpy as jnp
from jax import lax
from jax.experimental import pallas as pl
from jax.experimental.pallas import tpu as pltpu
from jax.sharding import Mesh
from jax.sharding import PartitionSpec as P

HD = 128
HEADS_TP = 8
GROUP = 4
COMP = 256
RANK = 64
LANES = 128
ROLLS = 2
CHIP_COUNT = 32
PIECE = 16
FIRST_ROWS = 24
QKV_ROWS = 24
KEY_ROW = ROLLS * HEADS_TP
STATE_ROW = KEY_ROW + 2 * ROLLS
GRANT = 56
SMALL_GRANT = 24
HINT = 2

adapter_scale = 2.0
f32 = jnp.float32
bf16 = jnp.bfloat16
CHIPS = ("y", "z")
DP = ("y", "z", "c")
HIGH = lax.Precision.HIGHEST
SMEM = pltpu.SMEM
VMEM = None


def nn_dot(a, b):
    return jnp.dot(a, b, preferred_element_type=f32)


def nt_dot(a, b, precision=None):
    return lax.dot_general(
        a, b, (((1,), (1,)), ((), ())), preferred_element_type=f32, precision=precision
    )


def tn_dot(a, b):
    return lax.dot_general(a, b, (((0,), (0,)), ((), ())), preferred_element_type=f32)


def swapped(x):
    return lax.ppermute(x, "c", [(0, 1), (1, 0)])


def shift(x, by, n):
    return lax.ppermute(x, "t", [(i, (i + by) % n) for i in range(n)])


def shifts(x, n):
    return [x] + [shift(x, by, n) for by in range(1, n)]


def exchange(x, axes):
    return lax.all_to_all(x, axes, split_axis=0, concat_axis=0, tiled=True)


def to_all(x, axes):
    return exchange(jnp.broadcast_to(x, (lax.axis_size(axes), *x.shape)), axes)


def together(*xs):
    return lax.optimization_barrier(xs)


def lane_iota(shape):
    return lax.broadcasted_iota(jnp.int32, shape, len(shape) - 1)


def call(kernel, out, specs, args, scratch=(), flops=0, grant=SMALL_GRANT):
    moved = sum(a.size * a.dtype.itemsize for a in args)
    outs = out if isinstance(out, tuple) else (out,)
    moved += sum(math.prod(o.shape) * o.dtype.itemsize for o in outs)
    whole = pl.BlockSpec()
    return pl.pallas_call(
        kernel,
        out_shape=out,
        in_specs=[pl.BlockSpec(memory_space=k) if k == SMEM else whole for k in specs],
        out_specs=tuple(whole for _ in outs) if isinstance(out, tuple) else whole,
        scratch_shapes=list(scratch),
        compiler_params=pltpu.CompilerParams(vmem_limit_bytes=grant << 20),
        cost_estimate=pl.CostEstimate(flops=flops, bytes_accessed=moved, transcendentals=0),
    )(*args)


def shape(*dims, dtype=f32):
    return jax.ShapeDtypeStruct(dims, dtype)


def message_kernel(
    rewards, prompts, live, a_far, b_far, hidden_far, out_far, a_ref, b_ref, hidden, out, sem
):
    pairs = ((a_far, a_ref), (b_far, b_ref), (hidden_far, hidden))
    copies = [pltpu.make_async_copy(p, q, sem.at[i]) for i, (p, q) in enumerate(pairs)]
    for copy in copies:
        copy.start()
    for copy in copies:
        copy.wait()
    pieces = jnp.concatenate([a_ref[...], b_ref[...]], axis=1)
    out[:, :PIECE, :] = jnp.broadcast_to(pieces, (CHIP_COUNT, PIECE, LANES))
    lane = lane_iota((1, LANES))
    value = jnp.where(lane == 0, rewards[0], jnp.where(lane == 1, rewards[1], 0.0))
    prompt = jnp.where(lane == 0, prompts[0], jnp.where(lane == 1, prompts[1], 0)).astype(f32)
    length = jnp.where(lane == 0, live[0], jnp.where(lane == 1, live[1], 0)).astype(f32)
    high = value.astype(bf16).astype(f32)
    mid = (value - high).astype(bf16).astype(f32)
    low = value - high - mid
    tail = jnp.concatenate([high, mid, low, prompt, length, jnp.zeros((1, LANES), f32)], axis=0)
    for m in range(CHIP_COUNT):
        cut = hidden[:, m * LANES : (m + 1) * LANES].astype(f32)
        out[m, PIECE:, :] = jnp.concatenate([cut, tail], axis=0).astype(bf16)
    copy = pltpu.make_async_copy(out, out_far, sem.at[len(pairs)])
    copy.start()
    copy.wait()


def first_message(rewards, prompts, live, a, b, hidden):
    out = shape(CHIP_COUNT, FIRST_ROWS, LANES, dtype=bf16)
    smem = pl.BlockSpec(memory_space=SMEM)
    hbm = pl.BlockSpec(memory_space=pltpu.HBM)
    return pl.pallas_call(
        message_kernel,
        out_shape=out,
        in_specs=[smem, smem, smem, hbm, hbm, hbm],
        out_specs=hbm,
        scratch_shapes=[
            *(pltpu.VMEM(v.shape, v.dtype) for v in (a, b, hidden, out)),
            pltpu.SemaphoreType.DMA((4,)),
        ],
        compiler_params=pltpu.CompilerParams(vmem_limit_bytes=GRANT << 20),
    )(rewards, prompts, live, a, b, hidden)


def spread_qkv(state, gain, w, out):
    x = state * gain
    x1 = x.astype(bf16)
    rest = x - x1.astype(f32)
    x2 = rest.astype(bf16)
    x3 = (rest - x2.astype(f32)).astype(bf16)
    count = x.shape[0]
    parts = nn_dot(jnp.concatenate([x1, x2, x3], axis=0), w)
    qkv = parts[:count] + parts[count : 2 * count] + parts[2 * count :]

    def put(row, block):
        out[pl.ds(row, CHIP_COUNT, stride=QKV_ROWS), :] = block

    for b in range(ROLLS):
        mine = qkv[b * CHIP_COUNT : (b + 1) * CHIP_COUNT]
        for h in range(HEADS_TP):
            put(b * HEADS_TP + h, mine[:, h * HD : (h + 1) * HD])
        put(KEY_ROW + 2 * b, mine[:, HEADS_TP * HD : (HEADS_TP + 1) * HD])
        put(KEY_ROW + 2 * b + 1, mine[:, (HEADS_TP + 1) * HD :])
        put(STATE_ROW + b, state[b * CHIP_COUNT : (b + 1) * CHIP_COUNT])
    for row in range(STATE_ROW + ROLLS, QKV_ROWS):
        put(row, jnp.zeros((CHIP_COUNT, LANES), f32))


def first_core():
    return lax.axis_index("c") == 0


def gain_of(gain):
    m = lax.axis_index("y") * lax.axis_size("z") + lax.axis_index("z")
    start = pl.multiple_of(m * LANES, LANES)
    return gain[:, pl.ds(start, LANES)].astype(f32)


def state_of(arrived, held):
    held[...] = arrived[...].astype(f32).reshape(CHIP_COUNT * FIRST_ROWS, LANES)
    return jnp.concatenate(
        [held[pl.ds(PIECE + b, CHIP_COUNT, stride=FIRST_ROWS), :] for b in range(ROLLS)], axis=0
    )


def in_core_order(own, other):
    first = first_core()
    even = jnp.where(first, own[...], other[...])
    odd = jnp.where(first, other[...], own[...])
    return jnp.concatenate([even, odd], axis=0)


def qkv_first_kernel(arrived, gain, w_own, w_other, out, held):
    spread_qkv(state_of(arrived, held), gain_of(gain), in_core_order(w_own, w_other), out)


def qkv_later_kernel(held, gain, w, s0, s1, s2, s3, out):
    share = s0[...] + s1[...] + s2[...] + s3[...]
    low = share[:, LANES:]
    count = share.shape[0]
    now = (
        held[:count, :]
        + share[:, :LANES]
        + adapter_scale * nt_dot(low, held[count:, :], precision=HIGH)
    )
    spread_qkv(now, gain_of(gain), w[...], out)


def attend_kernel(last, lengths, came, cache, *refs):
    if last:
        before, ab, attended, owned_out = refs
    else:
        attended, kv_out = refs
    sums = jnp.sum(came[...].reshape(CHIP_COUNT, QKV_ROWS, LANES), axis=0)
    factor = 1.0 / math.sqrt(HD)
    width = CHIP_COUNT * LANES
    rows = []
    lows = []
    kvs = []
    for b in range(ROLLS):
        owned = came[pl.ds(STATE_ROW + b, CHIP_COUNT, stride=QKV_ROWS), :]
        if last:
            owned_out[b * CHIP_COUNT : (b + 1) * CHIP_COUNT, :] = owned
        total = jnp.sum(jnp.sum(owned * owned, axis=0, keepdims=True), axis=1, keepdims=True)
        scale = lax.rsqrt(total * (1.0 / width) + 1e-05)
        query = sums[b * HEADS_TP : (b + 1) * HEADS_TP] * scale
        fresh = sums[KEY_ROW + 2 * b : KEY_ROW + 2 * b + 2] * scale
        kvs.append(fresh)
        q1 = query.astype(bf16)
        rest = query - q1.astype(f32)
        q2 = rest.astype(bf16)
        q3 = (rest - q2.astype(f32)).astype(bf16)
        keys = cache[b, :, :HD]
        parts = nt_dot(jnp.concatenate([q1, q2, q3], axis=0), keys)
        scores = (parts[:HEADS_TP] + parts[HEADS_TP : 2 * HEADS_TP] + parts[2 * HEADS_TP :]) * factor
        scores = jnp.where(lane_iota(scores.shape) < lengths[b], scores, -1e30)
        newest = [(fresh[0:1], fresh[1:2])]
        if last:
            newest = [(before[2 * b : 2 * b + 1], before[2 * b + 1 : 2 * b + 2])] + newest
        extra = [jnp.sum(query * k, axis=1, keepdims=True) * factor for k, _ in newest]
        top = jnp.max(scores, axis=1, keepdims=True)
        for e in extra:
            top = jnp.maximum(top, e)
        expo = jnp.exp(scores - top)
        total = jnp.sum(expo, axis=1, keepdims=True)
        more = [jnp.exp(e - top) for e in extra]
        for e in more:
            total = total + e
        out = nn_dot((expo / total).astype(bf16), cache[b, :, HD:])
        for e, (_, v) in zip(more, newest):
            out = out + (e / total).astype(bf16).astype(f32) * v
        out = out.astype(bf16)
        rows.append(out)
        if last:
            flat = out.astype(f32)
            lows.append(
                jnp.concatenate([flat[h : h + 1] for h in range(HEADS_TP)], axis=1)
            )
    both = jnp.concatenate([r.astype(f32) for r in rows], axis=0)
    if last:
        low = jnp.concatenate(lows + [jnp.zeros((8 - ROLLS, HEADS_TP * HD), f32)], axis=0)
        low = nn_dot(low.astype(bf16), ab[...])
        attended[...] = jnp.concatenate([both, low], axis=0)
    else:
        attended[...] = jnp.broadcast_to(both.astype(bf16), attended.shape)
        kv_out[...] = jnp.concatenate(kvs + [jnp.zeros((8 - 2 * ROLLS, LANES), f32)], axis=0)


def attend(last, lengths, came, cache, *more):
    if last:
        out = (shape(24, LANES), shape(ROLLS * CHIP_COUNT, LANES))
    else:
        out = (shape(CHIP_COUNT, ROLLS * HEADS_TP, LANES, dtype=bf16), shape(8, LANES))
    args = (lengths, came, cache, *more)
    return call(
        lambda *refs: attend_kernel(last, *refs),
        out,
        [SMEM] + [VMEM] * (len(args) - 1),
        args,
        flops=2 * 32 * 2 * cache.shape[0] * cache.shape[1] * HD,
    )


def close_kernel(came, w_own, w_other, ab, out, held):
    rows = ROLLS * HEADS_TP
    held[...] = came[...].astype(f32).reshape(CHIP_COUNT * rows, LANES)
    blocks = []
    for b in range(ROLLS):
        heads = [
            held[pl.ds(b * HEADS_TP + h, CHIP_COUNT, stride=rows), :] for h in range(HEADS_TP)
        ]
        blocks.append(jnp.concatenate(heads, axis=1))
    everyone = jnp.concatenate(blocks, axis=0).astype(bf16)
    first = first_core()
    w_even = jnp.where(first, w_own[...], w_other[...])
    w_odd = jnp.where(first, w_other[...], w_own[...])
    w = jnp.concatenate([w_even, w_odd], axis=0)
    out[:, :LANES] = nt_dot(everyone, w)
    out[:, LANES:] = nn_dot(everyone, ab[...])


def adapter_kernel(
    own, other, rows, upstream, w_own, w_other, weighted_out, ab_out, part, state_out, w_out, held
):
    state_out[...] = state_of(own, held)
    w_out[...] = in_core_order(w_own, w_other)
    first = first_core()
    even = jnp.where(first, own[...], other[...])
    odd = jnp.where(first, other[...], own[...])
    ab_out[:, :PIECE, :] = even[:, :PIECE]
    ab_out[:, PIECE:, :] = odd[:, :PIECE]
    lane = lane_iota((CHIP_COUNT, LANES))
    seen = []
    for side in (own, other):
        tail = side[:, PIECE:, :].astype(f32)
        seen.append((tail[:, 2, :] + tail[:, 3, :] + tail[:, 4, :], tail[:, 5, :]))
    m = lax.axis_index("y") * lax.axis_size("z") + lax.axis_index("z")
    mine = own[pl.ds(m, 1), PIECE:, :].astype(f32).reshape(8, LANES)
    count = rows.shape[0]
    index = lax.broadcasted_iota(jnp.int32, (count, 1), 0)
    weight = jnp.zeros((count, 1), f32)
    for b in range(ROLLS):
        reward = mine[2:3, b : b + 1] + mine[3:4, b : b + 1] + mine[4:5, b : b + 1]
        live = mine[6:7, b : b + 1]
        total = jnp.zeros((1, 1), f32)
        squares = jnp.zeros((1, 1), f32)
        for value, prompt in seen:
            hit = (prompt == mine[5:6, b : b + 1]) & (lane < ROLLS)
            value = jnp.where(hit, value, 0.0)
            total = total + jnp.sum(jnp.sum(value, axis=0, keepdims=True), axis=1, keepdims=True)
            value = value * value
            squares = squares + jnp.sum(
                jnp.sum(value, axis=0, keepdims=True), axis=1, keepdims=True
            )
        mean = total / GROUP
        std = jnp.sqrt(jnp.maximum(squares / GROUP - mean * mean, 0.09))
        per_roll = (reward - mean) / std / live
        slot = index - b * COMP
        inside = (slot >= 0) & (slot < COMP) & (slot < live.astype(jnp.int32))
        weight = jnp.where(inside, per_roll, weight)
    weighted = (weight * upstream[...].astype(f32)).astype(bf16)
    weighted_out[...] = weighted
    ab = ab_out[...].reshape(2 * CHIP_COUNT * PIECE, LANES)
    low = nn_dot(rows[...], ab)
    back = nn_dot(weighted, ab)
    part[:count, :] = jnp.where(lane_iota((count, LANES)) < RANK, low, back)
    z = lax.axis_index("z")
    each = LANES // (2 * PIECE)
    piece = ab_out[pl.ds(z * each, each), :, :].reshape(LANES, LANES).astype(f32)
    piece = pltpu.roll(piece, RANK, 1)
    part[count:, :] = jnp.where(lane_iota((LANES, LANES)) < RANK, piece, 0.0)


def gradient_kernel(
    p0, p1, p2, p3, rows, weighted, state, low_back, joined, kept, given
):
    count = rows.shape[0]
    total = p0[:count, :] + p1[:count, :] + p2[:count, :] + p3[:count, :]
    low_back[...] = total.astype(bf16)
    turned = pltpu.roll(total, RANK, 1).astype(bf16)
    nt = lax.axis_size("t")
    from_y = lax.rem(lax.axis_index("t") - lax.axis_index("y") + nt, nt)
    piece = p0[count:, :]
    for by, p in ((1, p1), (2, p2), (3, p3)):
        piece = jnp.where(from_y == by, p[count:, :], piece)
    joined[: state.shape[0], :] = state[...]
    joined[state.shape[0] :, :] = piece
    a_side = tn_dot(rows[...], turned)
    b_side = tn_dot(weighted[...], turned)
    both = adapter_scale * jnp.where(lane_iota(a_side.shape) < RANK, a_side, b_side)
    both = both.reshape(CHIP_COUNT, 2 * PIECE, LANES)
    even, odd = both[:, :PIECE], both[:, PIECE:]
    first = first_core()
    kept[...] = jnp.where(first, even, odd)
    given[...] = jnp.where(first, odd, even)


def turned_up(b_ref):
    b = b_ref[...]
    b = jnp.where(lane_iota(b.shape) >= RANK, b, jnp.zeros_like(b))
    return pltpu.roll(b.astype(f32), RANK, 1)


def rows_kernel(
    where_ref, own, left, right, far_a, far_b, w_ref, low, b_ref, s0, s1, s2, s3, owned, out, cols, x
):
    rows = own.shape[0]
    half = far_a.shape[0]
    sent = (s0, s1, s2, s3)

    @pl.when(pl.program_id(0) == 0)
    def _():
        x[0, :rows, :] = own[...]
        x[1, :rows, :] = left[...]
        x[2, :half, :] = far_a[...]
        x[2, half:rows, :] = far_b[...]
        x[3, :rows, :] = right[...]
        for k, s in enumerate(sent):
            flat = [
                jnp.concatenate(
                    [s[b * HEADS_TP + h : b * HEADS_TP + h + 1, :] for h in range(HEADS_TP)],
                    axis=1,
                )
                for b in range(ROLLS)
            ]
            flat.append(jnp.zeros((16 - ROLLS, HEADS_TP * HD), f32))
            x[k, rows:, :] = jnp.concatenate(flat, axis=0).astype(bf16)

    b_turned = turned_up(b_ref)
    acc = nt_dot(x[0], w_ref[where_ref[0]])
    for k in range(1, len(sent)):
        acc = acc + nt_dot(x[k], w_ref[where_ref[k]])
    out[...] = acc[:rows] + adapter_scale * nt_dot(low[...], b_turned.astype(bf16))
    top = ROLLS * HEADS_TP
    low_sum = s0[top:, :] + s1[top:, :] + s2[top:, :] + s3[top:, :]
    got = adapter_scale * nt_dot(low_sum, b_turned, precision=HIGH)
    cols[...] = got + acc[rows : rows + 8]
    wide = cols.shape[1] // LANES
    start = (where_ref[0] * pl.num_programs(0) + pl.program_id(0)) * wide
    for b in range(ROLLS):
        for i in range(wide):
            block = owned[pl.ds(b * CHIP_COUNT + start + i, 1), :]
            cols[b : b + 1, i * LANES : (i + 1) * LANES] += block


def output_rows(where, own, left, right, far_a, far_b, w, low, b, sent, owned):
    n, width, depth = w.shape
    rows = own.shape[0]
    tile = 256
    tiles = width // tile
    whole = lambda a: pl.BlockSpec(a.shape, lambda j, s: (0, 0))
    return pl.pallas_call(
        rows_kernel,
        out_shape=(shape(rows, width), shape(8, width)),
        grid_spec=pltpu.PrefetchScalarGridSpec(
            num_scalar_prefetch=1,
            grid=(tiles,),
            in_specs=[
                whole(own),
                whole(left),
                whole(right),
                whole(far_a),
                whole(far_b),
                pl.BlockSpec((n, tile, depth), lambda j, s: (0, j, 0)),
                whole(low),
                pl.BlockSpec((tile, b.shape[1]), lambda j, s: (j, 0)),
                *(whole(s) for s in sent),
                whole(owned),
            ],
            out_specs=(
                pl.BlockSpec((rows, tile), lambda j, s: (0, j)),
                pl.BlockSpec((8, tile), lambda j, s: (0, j)),
            ),
            scratch_shapes=[pltpu.VMEM((n, rows + 16, depth), bf16)],
        ),
        compiler_params=pltpu.CompilerParams(vmem_limit_bytes=GRANT << 20),
        cost_estimate=pl.CostEstimate(
            flops=HINT * 2 * rows * width * depth * n,
            bytes_accessed=2 * (n * width * depth + n * rows * depth) + 4 * rows * width,
            transcendentals=0,
        ),
    )(where, own, left, right, far_a, far_b, w, low, b, *sent, owned)


def place_kernel(c0, c1, c2, c3, out):
    width = c0.shape[1]
    nt = lax.axis_size("t")
    for k, part in enumerate((c0, c1, c2, c3)):
        block = lax.rem(lax.axis_index("t") - k + nt, nt)
        start = pl.multiple_of(block * width, width)
        out[:, pl.ds(start, width)] = part[:ROLLS, :]


def shards(
    hidden,
    attention_norm_gain,
    query_key_value_weight,
    key_value_cache,
    cache_fill_lengths,
    output_weight_frozen,
    adapter_down_transposed,
    adapter_up_matrix,
    attention_rows,
    upstream,
    rewards,
    prompt_group_index,
    completion_live_lengths,
):
    nt = lax.axis_size("t")
    t = lax.axis_index("t")
    width = hidden.shape[1]
    shard_width = width // nt
    cache = key_value_cache[:, :, 0, :]
    where = lax.rem(t - jnp.arange(nt, dtype=jnp.int32) + nt, nt)

    message = first_message(
        rewards,
        prompt_group_index,
        completion_live_lengths,
        adapter_down_transposed[:, 0, :].T,
        adapter_up_matrix[:, 0, :].T,
        hidden,
    )

    w_rows = query_key_value_weight[:, 0, :]
    w_rows_other = swapped(w_rows)
    w_cols = output_weight_frozen[0].T
    w_cols_other = swapped(w_cols)

    ny = lax.axis_size("y")
    turned = lax.ppermute(
        w_cols, ("y", "t"), [(a * nt + b, b * nt + a) for a in range(ny) for b in range(nt)]
    )
    arrived = exchange(message, CHIPS)
    gain = attention_norm_gain[None, :]
    arrived, gain, w_rows_other, w_cols_other, where = together(
        arrived, gain, w_rows_other, w_cols_other, where
    )
    sent = call(
        qkv_first_kernel,
        shape(CHIP_COUNT * QKV_ROWS, LANES),
        [VMEM] * 4,
        (arrived, gain, w_rows, w_rows_other),
        scratch=[pltpu.VMEM((CHIP_COUNT * FIRST_ROWS, LANES), f32)],
    )
    turned, _ = together(turned, sent)
    w_block = lax.all_gather(turned, DP, axis=0, tiled=True)
    w_block = w_block.reshape(nt, shard_width, w_cols.shape[1])
    sent, arrived, own_rows = together(sent, arrived, attention_rows)
    arrived_other = swapped(arrived)
    came = exchange(sent.reshape(CHIP_COUNT, QKV_ROWS, LANES), CHIPS)

    left = shift(own_rows, 1, nt)
    right = shift(own_rows, nt - 1, nt)
    rows = attention_rows.shape[0]
    half = rows // 2
    weighted, ab, part, state, w_both = call(
        adapter_kernel,
        (
            shape(rows, shard_width, dtype=bf16),
            shape(CHIP_COUNT, 2 * PIECE, LANES, dtype=bf16),
            shape(rows + LANES, LANES),
            shape(ROLLS * CHIP_COUNT, LANES),
            shape(2 * w_rows.shape[0], w_rows.shape[1], dtype=bf16),
        ),
        [VMEM] * 6,
        (arrived, arrived_other, attention_rows, upstream, w_rows, w_rows_other),
        scratch=[pltpu.VMEM((CHIP_COUNT * FIRST_ROWS, LANES), f32)],
        flops=4 * rows * shard_width * LANES,
    )
    ab = ab.reshape(shard_width, LANES)
    parts = shifts(part, nt)

    attended, kv = attend(False, cache_fill_lengths, came.reshape(-1, LANES), cache)
    everyone = exchange(attended, CHIPS)

    share = call(
        close_kernel,
        shape(ROLLS * CHIP_COUNT, 2 * LANES),
        [VMEM] * 4,
        (everyone, w_cols, w_cols_other, ab),
        scratch=[pltpu.VMEM((CHIP_COUNT * ROLLS * HEADS_TP, LANES), f32)],
    )
    share, weighted = together(share, weighted)
    shares = shifts(share, nt)

    low_back, joined, kept, given = call(
        gradient_kernel,
        (
            shape(rows, LANES, dtype=bf16),
            shape(ROLLS * CHIP_COUNT + LANES, LANES),
            shape(CHIP_COUNT, PIECE, LANES),
            shape(CHIP_COUNT, PIECE, LANES),
        ),
        [VMEM] * 7,
        (*parts, attention_rows, weighted, state),
        flops=4 * rows * shard_width * LANES,
    )

    sent = call(
        qkv_later_kernel,
        shape(CHIP_COUNT * QKV_ROWS, LANES),
        [VMEM] * 7,
        (joined, gain, w_both, *shares),
    )
    sent, low_back, left_far, right_far = together(sent, low_back, left, right)
    came = exchange(sent.reshape(CHIP_COUNT, QKV_ROWS, LANES), CHIPS)

    far_a = shift(left_far[:half], 1, nt)
    far_b = shift(right_far[half:], nt - 1, nt)
    kept = kept + swapped(given)

    attended, owned = attend(True, cache_fill_lengths, came.reshape(-1, LANES), cache, kv, ab)
    attended, kept = together(attended, kept)
    summed = exchange(kept, CHIPS)
    adapted, cols = output_rows(
        where,
        attention_rows,
        left,
        right,
        far_a,
        far_b,
        w_block,
        low_back,
        ab,
        shifts(attended, nt),
        owned,
    )
    arriving = shifts(cols, nt)
    arriving[1], summed = together(arriving[1], summed)
    summed = summed.sum(axis=0)
    decoded = call(place_kernel, shape(ROLLS, width), [VMEM] * nt, tuple(arriving))
    grad_a = summed[:, :RANK].T[:, None, :]
    grad_b = summed[:, RANK:].T[:, None, :]
    return (decoded, adapted, grad_a, grad_b)


def solution(mesh):
    split = Mesh(mesh.devices.reshape(4, 8, 2, 4), ("y", "z", "c", "t"))
    placed = (
        P(DP, None),
        P(),
        P(DP, "t", None),
        P(DP, None, "t", None),
        P(DP),
        P("t", None, DP),
        P(None, "t", DP),
        P(None, "t", DP),
        P(DP, "t"),
        P(DP, "t"),
        P(DP),
        P(DP),
        P(DP),
    )
    return jax.shard_map(
        shards,
        mesh=split,
        in_specs=placed,
        out_specs=(P(DP, None), P(DP, "t"), P(None, "t", DP), P(None, "t", DP)),
        check_vma=False,
    )
```

```python
import math

import jax
import jax.numpy as jnp
from jax import lax
from jax.experimental import pallas as pl
from jax.experimental.pallas import tpu as pltpu
from jax.sharding import Mesh
from jax.sharding import PartitionSpec as P

HD = 128
HEADS_TP = 8
GROUP = 4
COMP = 256
RANK = 64
LANES = 128
ROLLS = 2
CHIP_COUNT = 32
PIECE = 16
FIRST_ROWS = 24
QKV_ROWS = 24
KEY_ROW = ROLLS * HEADS_TP
STATE_ROW = KEY_ROW + 2 * ROLLS
GRANT = 56
SMALL_GRANT = 24
HINT = 2

adapter_scale = 2.0
f32 = jnp.float32
bf16 = jnp.bfloat16
CHIPS = ("y", "z")
DP = ("y", "z", "c")
HIGH = lax.Precision.HIGHEST
SMEM = pltpu.SMEM
VMEM = None


def nn_dot(a, b):
    return jnp.dot(a, b, preferred_element_type=f32)


def nt_dot(a, b, precision=None):
    return lax.dot_general(
        a, b, (((1,), (1,)), ((), ())), preferred_element_type=f32, precision=precision
    )


def tn_dot(a, b):
    return lax.dot_general(a, b, (((0,), (0,)), ((), ())), preferred_element_type=f32)


def swapped(x):
    return lax.ppermute(x, "c", [(0, 1), (1, 0)])


def shift(x, by, n):
    return lax.ppermute(x, "t", [(i, (i + by) % n) for i in range(n)])


def shifts(x, n):
    return [x] + [shift(x, by, n) for by in range(1, n)]


def exchange(x, axes):
    return lax.all_to_all(x, axes, split_axis=0, concat_axis=0, tiled=True)


def to_all(x, axes):
    return exchange(jnp.broadcast_to(x, (lax.axis_size(axes), *x.shape)), axes)


def together(*xs):
    return lax.optimization_barrier(xs)


def lane_iota(shape):
    return lax.broadcasted_iota(jnp.int32, shape, len(shape) - 1)


def call(kernel, out, specs, args, scratch=(), flops=0, grant=SMALL_GRANT):
    moved = sum(a.size * a.dtype.itemsize for a in args)
    outs = out if isinstance(out, tuple) else (out,)
    moved += sum(math.prod(o.shape) * o.dtype.itemsize for o in outs)
    whole = pl.BlockSpec()
    return pl.pallas_call(
        kernel,
        out_shape=out,
        in_specs=[pl.BlockSpec(memory_space=k) if k == SMEM else whole for k in specs],
        out_specs=tuple(whole for _ in outs) if isinstance(out, tuple) else whole,
        scratch_shapes=list(scratch),
        compiler_params=pltpu.CompilerParams(vmem_limit_bytes=grant << 20),
        cost_estimate=pl.CostEstimate(flops=flops, bytes_accessed=moved, transcendentals=0),
    )(*args)


def shape(*dims, dtype=f32):
    return jax.ShapeDtypeStruct(dims, dtype)


def message_kernel(
    rewards, prompts, live, a_far, b_far, hidden_far, out_far, a_ref, b_ref, hidden, out, sem
):
    pairs = ((a_far, a_ref), (b_far, b_ref), (hidden_far, hidden))
    copies = [pltpu.make_async_copy(p, q, sem.at[i]) for i, (p, q) in enumerate(pairs)]
    for copy in copies:
        copy.start()
    for copy in copies:
        copy.wait()
    pieces = jnp.concatenate([a_ref[...], b_ref[...]], axis=1)
    out[:, :PIECE, :] = jnp.broadcast_to(pieces, (CHIP_COUNT, PIECE, LANES))
    lane = lane_iota((1, LANES))
    value = jnp.where(lane == 0, rewards[0], jnp.where(lane == 1, rewards[1], 0.0))
    prompt = jnp.where(lane == 0, prompts[0], jnp.where(lane == 1, prompts[1], 0)).astype(f32)
    length = jnp.where(lane == 0, live[0], jnp.where(lane == 1, live[1], 0)).astype(f32)
    high = value.astype(bf16).astype(f32)
    mid = (value - high).astype(bf16).astype(f32)
    low = value - high - mid
    tail = jnp.concatenate([high, mid, low, prompt, length, jnp.zeros((1, LANES), f32)], axis=0)
    for m in range(CHIP_COUNT):
        cut = hidden[:, m * LANES : (m + 1) * LANES].astype(f32)
        out[m, PIECE:, :] = jnp.concatenate([cut, tail], axis=0).astype(bf16)
    copy = pltpu.make_async_copy(out, out_far, sem.at[len(pairs)])
    copy.start()
    copy.wait()


def first_message(rewards, prompts, live, a, b, hidden):
    out = shape(CHIP_COUNT, FIRST_ROWS, LANES, dtype=bf16)
    smem = pl.BlockSpec(memory_space=SMEM)
    hbm = pl.BlockSpec(memory_space=pltpu.HBM)
    return pl.pallas_call(
        message_kernel,
        out_shape=out,
        in_specs=[smem, smem, smem, hbm, hbm, hbm],
        out_specs=hbm,
        scratch_shapes=[
            *(pltpu.VMEM(v.shape, v.dtype) for v in (a, b, hidden, out)),
            pltpu.SemaphoreType.DMA((4,)),
        ],
        compiler_params=pltpu.CompilerParams(vmem_limit_bytes=GRANT << 20),
    )(rewards, prompts, live, a, b, hidden)


def spread_qkv(state, gain, w, out):
    x = state * gain
    x1 = x.astype(bf16)
    rest = x - x1.astype(f32)
    x2 = rest.astype(bf16)
    x3 = (rest - x2.astype(f32)).astype(bf16)
    count = x.shape[0]
    parts = nn_dot(jnp.concatenate([x1, x2, x3], axis=0), w)
    qkv = parts[:count] + parts[count : 2 * count] + parts[2 * count :]

    def put(row, block):
        out[pl.ds(row, CHIP_COUNT, stride=QKV_ROWS), :] = block

    for b in range(ROLLS):
        mine = qkv[b * CHIP_COUNT : (b + 1) * CHIP_COUNT]
        for h in range(HEADS_TP):
            put(b * HEADS_TP + h, mine[:, h * HD : (h + 1) * HD])
        put(KEY_ROW + 2 * b, mine[:, HEADS_TP * HD : (HEADS_TP + 1) * HD])
        put(KEY_ROW + 2 * b + 1, mine[:, (HEADS_TP + 1) * HD :])
        put(STATE_ROW + b, state[b * CHIP_COUNT : (b + 1) * CHIP_COUNT])
    for row in range(STATE_ROW + ROLLS, QKV_ROWS):
        put(row, jnp.zeros((CHIP_COUNT, LANES), f32))


def first_core():
    return lax.axis_index("c") == 0


def gain_of(gain):
    m = lax.axis_index("y") * lax.axis_size("z") + lax.axis_index("z")
    start = pl.multiple_of(m * LANES, LANES)
    return gain[:, pl.ds(start, LANES)].astype(f32)


def state_of(arrived, held):
    held[...] = arrived[...].astype(f32).reshape(CHIP_COUNT * FIRST_ROWS, LANES)
    return jnp.concatenate(
        [held[pl.ds(PIECE + b, CHIP_COUNT, stride=FIRST_ROWS), :] for b in range(ROLLS)], axis=0
    )


def in_core_order(own, other):
    first = first_core()
    even = jnp.where(first, own[...], other[...])
    odd = jnp.where(first, other[...], own[...])
    return jnp.concatenate([even, odd], axis=0)


def qkv_first_kernel(arrived, gain, w_own, w_other, out, held):
    spread_qkv(state_of(arrived, held), gain_of(gain), in_core_order(w_own, w_other), out)


def qkv_later_kernel(held, gain, w, s0, s1, s2, s3, out):
    share = s0[...] + s1[...] + s2[...] + s3[...]
    low = share[:, LANES:]
    count = share.shape[0]
    now = (
        held[:count, :]
        + share[:, :LANES]
        + adapter_scale * nt_dot(low, held[count:, :], precision=HIGH)
    )
    spread_qkv(now, gain_of(gain), w[...], out)


def attend_kernel(last, lengths, came, cache, *refs):
    if last:
        before, ab, attended, owned_out = refs
    else:
        attended, kv_out = refs
    sums = jnp.sum(came[...].reshape(CHIP_COUNT, QKV_ROWS, LANES), axis=0)
    factor = 1.0 / math.sqrt(HD)
    width = CHIP_COUNT * LANES
    rows = []
    lows = []
    kvs = []
    for b in range(ROLLS):
        owned = came[pl.ds(STATE_ROW + b, CHIP_COUNT, stride=QKV_ROWS), :]
        if last:
            owned_out[b * CHIP_COUNT : (b + 1) * CHIP_COUNT, :] = owned
        total = jnp.sum(jnp.sum(owned * owned, axis=0, keepdims=True), axis=1, keepdims=True)
        scale = lax.rsqrt(total * (1.0 / width) + 1e-05)
        query = sums[b * HEADS_TP : (b + 1) * HEADS_TP] * scale
        fresh = sums[KEY_ROW + 2 * b : KEY_ROW + 2 * b + 2] * scale
        kvs.append(fresh)
        q1 = query.astype(bf16)
        rest = query - q1.astype(f32)
        q2 = rest.astype(bf16)
        q3 = (rest - q2.astype(f32)).astype(bf16)
        keys = cache[b, :, :HD]
        parts = nt_dot(jnp.concatenate([q1, q2, q3], axis=0), keys)
        scores = (parts[:HEADS_TP] + parts[HEADS_TP : 2 * HEADS_TP] + parts[2 * HEADS_TP :]) * factor
        scores = jnp.where(lane_iota(scores.shape) < lengths[b], scores, -1e30)
        newest = [(fresh[0:1], fresh[1:2])]
        if last:
            newest = [(before[2 * b : 2 * b + 1], before[2 * b + 1 : 2 * b + 2])] + newest
        extra = [jnp.sum(query * k, axis=1, keepdims=True) * factor for k, _ in newest]
        top = jnp.max(scores, axis=1, keepdims=True)
        for e in extra:
            top = jnp.maximum(top, e)
        expo = jnp.exp(scores - top)
        total = jnp.sum(expo, axis=1, keepdims=True)
        more = [jnp.exp(e - top) for e in extra]
        for e in more:
            total = total + e
        out = nn_dot((expo / total).astype(bf16), cache[b, :, HD:])
        for e, (_, v) in zip(more, newest):
            out = out + (e / total).astype(bf16).astype(f32) * v
        out = out.astype(bf16)
        rows.append(out)
        if last:
            flat = out.astype(f32)
            lows.append(
                jnp.concatenate([flat[h : h + 1] for h in range(HEADS_TP)], axis=1)
            )
    both = jnp.concatenate([r.astype(f32) for r in rows], axis=0)
    if last:
        low = jnp.concatenate(lows + [jnp.zeros((8 - ROLLS, HEADS_TP * HD), f32)], axis=0)
        low = nn_dot(low.astype(bf16), ab[...])
        attended[...] = jnp.concatenate([both, low], axis=0)
    else:
        attended[...] = jnp.broadcast_to(both.astype(bf16), attended.shape)
        kv_out[...] = jnp.concatenate(kvs + [jnp.zeros((8 - 2 * ROLLS, LANES), f32)], axis=0)


def attend(last, lengths, came, cache, *more):
    if last:
        out = (shape(24, LANES), shape(ROLLS * CHIP_COUNT, LANES))
    else:
        out = (shape(CHIP_COUNT, ROLLS * HEADS_TP, LANES, dtype=bf16), shape(8, LANES))
    args = (lengths, came, cache, *more)
    return call(
        lambda *refs: attend_kernel(last, *refs),
        out,
        [SMEM] + [VMEM] * (len(args) - 1),
        args,
        flops=2 * 32 * 2 * cache.shape[0] * cache.shape[1] * HD,
    )


def close_kernel(came, w_own, w_other, ab, out, held):
    rows = ROLLS * HEADS_TP
    held[...] = came[...].astype(f32).reshape(CHIP_COUNT * rows, LANES)
    blocks = []
    for b in range(ROLLS):
        heads = [
            held[pl.ds(b * HEADS_TP + h, CHIP_COUNT, stride=rows), :] for h in range(HEADS_TP)
        ]
        blocks.append(jnp.concatenate(heads, axis=1))
    everyone = jnp.concatenate(blocks, axis=0).astype(bf16)
    first = first_core()
    w_even = jnp.where(first, w_own[...], w_other[...])
    w_odd = jnp.where(first, w_other[...], w_own[...])
    w = jnp.concatenate([w_even, w_odd], axis=0)
    out[:, :LANES] = nt_dot(everyone, w)
    out[:, LANES:] = nn_dot(everyone, ab[...])


def adapter_kernel(
    own, other, rows, upstream, w_own, w_other, weighted_out, ab_out, part, state_out, w_out, held
):
    state_out[...] = state_of(own, held)
    w_out[...] = in_core_order(w_own, w_other)
    first = first_core()
    even = jnp.where(first, own[...], other[...])
    odd = jnp.where(first, other[...], own[...])
    ab_out[:, :PIECE, :] = even[:, :PIECE]
    ab_out[:, PIECE:, :] = odd[:, :PIECE]
    lane = lane_iota((CHIP_COUNT, LANES))
    seen = []
    for side in (own, other):
        tail = side[:, PIECE:, :].astype(f32)
        seen.append((tail[:, 2, :] + tail[:, 3, :] + tail[:, 4, :], tail[:, 5, :]))
    m = lax.axis_index("y") * lax.axis_size("z") + lax.axis_index("z")
    mine = own[pl.ds(m, 1), PIECE:, :].astype(f32).reshape(8, LANES)
    count = rows.shape[0]
    index = lax.broadcasted_iota(jnp.int32, (count, 1), 0)
    weight = jnp.zeros((count, 1), f32)
    for b in range(ROLLS):
        reward = mine[2:3, b : b + 1] + mine[3:4, b : b + 1] + mine[4:5, b : b + 1]
        live = mine[6:7, b : b + 1]
        total = jnp.zeros((1, 1), f32)
        squares = jnp.zeros((1, 1), f32)
        for value, prompt in seen:
            hit = (prompt == mine[5:6, b : b + 1]) & (lane < ROLLS)
            value = jnp.where(hit, value, 0.0)
            total = total + jnp.sum(jnp.sum(value, axis=0, keepdims=True), axis=1, keepdims=True)
            value = value * value
            squares = squares + jnp.sum(
                jnp.sum(value, axis=0, keepdims=True), axis=1, keepdims=True
            )
        mean = total / GROUP
        std = jnp.sqrt(jnp.maximum(squares / GROUP - mean * mean, 0.09))
        per_roll = (reward - mean) / std / live
        slot = index - b * COMP
        inside = (slot >= 0) & (slot < COMP) & (slot < live.astype(jnp.int32))
        weight = jnp.where(inside, per_roll, weight)
    weighted = (weight * upstream[...].astype(f32)).astype(bf16)
    weighted_out[...] = weighted
    ab = ab_out[...].reshape(2 * CHIP_COUNT * PIECE, LANES)
    low = nn_dot(rows[...], ab)
    back = nn_dot(weighted, ab)
    part[:count, :] = jnp.where(lane_iota((count, LANES)) < RANK, low, back)
    z = lax.axis_index("z")
    each = LANES // (2 * PIECE)
    piece = ab_out[pl.ds(z * each, each), :, :].reshape(LANES, LANES).astype(f32)
    piece = pltpu.roll(piece, RANK, 1)
    part[count:, :] = jnp.where(lane_iota((LANES, LANES)) < RANK, piece, 0.0)


def gradient_kernel(
    p0, p1, p2, p3, rows, weighted, state, low_back, joined, kept, given
):
    count = rows.shape[0]
    total = p0[:count, :] + p1[:count, :] + p2[:count, :] + p3[:count, :]
    low_back[...] = total.astype(bf16)
    turned = pltpu.roll(total, RANK, 1).astype(bf16)
    nt = lax.axis_size("t")
    from_y = lax.rem(lax.axis_index("t") - lax.axis_index("y") + nt, nt)
    piece = p0[count:, :]
    for by, p in ((1, p1), (2, p2), (3, p3)):
        piece = jnp.where(from_y == by, p[count:, :], piece)
    joined[: state.shape[0], :] = state[...]
    joined[state.shape[0] :, :] = piece
    a_side = tn_dot(rows[...], turned)
    b_side = tn_dot(weighted[...], turned)
    both = adapter_scale * jnp.where(lane_iota(a_side.shape) < RANK, a_side, b_side)
    both = both.reshape(CHIP_COUNT, 2 * PIECE, LANES)
    even, odd = both[:, :PIECE], both[:, PIECE:]
    first = first_core()
    kept[...] = jnp.where(first, even, odd)
    given[...] = jnp.where(first, odd, even)


def turned_up(b_ref):
    b = b_ref[...]
    b = jnp.where(lane_iota(b.shape) >= RANK, b, jnp.zeros_like(b))
    return pltpu.roll(b.astype(f32), RANK, 1)


def rows_kernel(
    where_ref, own, left, right, far_a, far_b, w_ref, low, b_ref, s0, s1, s2, s3, owned, out, cols, x
):
    rows = own.shape[0]
    half = far_a.shape[0]
    sent = (s0, s1, s2, s3)

    @pl.when(pl.program_id(0) == 0)
    def _():
        x[0, :rows, :] = own[...]
        x[1, :rows, :] = left[...]
        x[2, :half, :] = far_a[...]
        x[2, half:rows, :] = far_b[...]
        x[3, :rows, :] = right[...]
        for k, s in enumerate(sent):
            flat = [
                jnp.concatenate(
                    [s[b * HEADS_TP + h : b * HEADS_TP + h + 1, :] for h in range(HEADS_TP)],
                    axis=1,
                )
                for b in range(ROLLS)
            ]
            flat.append(jnp.zeros((16 - ROLLS, HEADS_TP * HD), f32))
            x[k, rows:, :] = jnp.concatenate(flat, axis=0).astype(bf16)

    b_turned = turned_up(b_ref)
    acc = nt_dot(x[0], w_ref[where_ref[0]])
    for k in range(1, len(sent)):
        acc = acc + nt_dot(x[k], w_ref[where_ref[k]])
    out[...] = acc[:rows] + adapter_scale * nt_dot(low[...], b_turned.astype(bf16))
    top = ROLLS * HEADS_TP
    low_sum = s0[top:, :] + s1[top:, :] + s2[top:, :] + s3[top:, :]
    got = adapter_scale * nt_dot(low_sum, b_turned, precision=HIGH)
    cols[...] = got + acc[rows : rows + 8]
    wide = cols.shape[1] // LANES
    start = (where_ref[0] * pl.num_programs(0) + pl.program_id(0)) * wide
    for b in range(ROLLS):
        for i in range(wide):
            block = owned[pl.ds(b * CHIP_COUNT + start + i, 1), :]
            cols[b : b + 1, i * LANES : (i + 1) * LANES] += block


def output_rows(where, own, left, right, far_a, far_b, w, low, b, sent, owned):
    n, width, depth = w.shape
    rows = own.shape[0]
    tile = 256
    tiles = width // tile
    whole = lambda a: pl.BlockSpec(a.shape, lambda j, s: (0, 0))
    return pl.pallas_call(
        rows_kernel,
        out_shape=(shape(rows, width), shape(8, width)),
        grid_spec=pltpu.PrefetchScalarGridSpec(
            num_scalar_prefetch=1,
            grid=(tiles,),
            in_specs=[
                whole(own),
                whole(left),
                whole(right),
                whole(far_a),
                whole(far_b),
                pl.BlockSpec((n, tile, depth), lambda j, s: (0, j, 0)),
                whole(low),
                pl.BlockSpec((tile, b.shape[1]), lambda j, s: (j, 0)),
                *(whole(s) for s in sent),
                whole(owned),
            ],
            out_specs=(
                pl.BlockSpec((rows, tile), lambda j, s: (0, j)),
                pl.BlockSpec((8, tile), lambda j, s: (0, j)),
            ),
            scratch_shapes=[pltpu.VMEM((n, rows + 16, depth), bf16)],
        ),
        compiler_params=pltpu.CompilerParams(vmem_limit_bytes=GRANT << 20),
        cost_estimate=pl.CostEstimate(
            flops=HINT * 2 * rows * width * depth * n,
            bytes_accessed=2 * (n * width * depth + n * rows * depth) + 4 * rows * width,
            transcendentals=0,
        ),
    )(where, own, left, right, far_a, far_b, w, low, b, *sent, owned)


def place_kernel(c0, c1, c2, c3, out):
    width = c0.shape[1]
    nt = lax.axis_size("t")
    for k, part in enumerate((c0, c1, c2, c3)):
        block = lax.rem(lax.axis_index("t") - k + nt, nt)
        start = pl.multiple_of(block * width, width)
        out[:, pl.ds(start, width)] = part[:ROLLS, :]


def shards(
    hidden,
    attention_norm_gain,
    query_key_value_weight,
    key_value_cache,
    cache_fill_lengths,
    output_weight_frozen,
    adapter_down_transposed,
    adapter_up_matrix,
    attention_rows,
    upstream,
    rewards,
    prompt_group_index,
    completion_live_lengths,
):
    nt = lax.axis_size("t")
    t = lax.axis_index("t")
    width = hidden.shape[1]
    shard_width = width // nt
    cache = key_value_cache[:, :, 0, :]
    where = lax.rem(t - jnp.arange(nt, dtype=jnp.int32) + nt, nt)

    message = first_message(
        rewards,
        prompt_group_index,
        completion_live_lengths,
        adapter_down_transposed[:, 0, :].T,
        adapter_up_matrix[:, 0, :].T,
        hidden,
    )

    w_rows = query_key_value_weight[:, 0, :]
    w_rows_other = swapped(w_rows)
    w_cols = output_weight_frozen[0].T
    w_cols_other = swapped(w_cols)

    ny = lax.axis_size("y")
    turned = lax.ppermute(
        w_cols, ("y", "t"), [(a * nt + b, b * nt + a) for a in range(ny) for b in range(nt)]
    )
    arrived = exchange(message, CHIPS)
    gain = attention_norm_gain[None, :]
    lengths = jnp.maximum(cache_fill_lengths, 0)
    arrived, gain, w_rows_other, w_cols_other, where, lengths = together(
        arrived, gain, w_rows_other, w_cols_other, where, lengths
    )
    sent = call(
        qkv_first_kernel,
        shape(CHIP_COUNT * QKV_ROWS, LANES),
        [VMEM] * 4,
        (arrived, gain, w_rows, w_rows_other),
        scratch=[pltpu.VMEM((CHIP_COUNT * FIRST_ROWS, LANES), f32)],
    )
    turned, _ = together(turned, sent)
    w_block = lax.all_gather(turned, DP, axis=0, tiled=True)
    w_block = w_block.reshape(nt, shard_width, w_cols.shape[1])
    sent, arrived, own_rows = together(sent, arrived, attention_rows)
    arrived_other = swapped(arrived)
    came = exchange(sent.reshape(CHIP_COUNT, QKV_ROWS, LANES), CHIPS)

    left = shift(own_rows, 1, nt)
    right = shift(own_rows, nt - 1, nt)
    rows = attention_rows.shape[0]
    half = rows // 2
    weighted, ab, part, state, w_both = call(
        adapter_kernel,
        (
            shape(rows, shard_width, dtype=bf16),
            shape(CHIP_COUNT, 2 * PIECE, LANES, dtype=bf16),
            shape(rows + LANES, LANES),
            shape(ROLLS * CHIP_COUNT, LANES),
            shape(2 * w_rows.shape[0], w_rows.shape[1], dtype=bf16),
        ),
        [VMEM] * 6,
        (arrived, arrived_other, attention_rows, upstream, w_rows, w_rows_other),
        scratch=[pltpu.VMEM((CHIP_COUNT * FIRST_ROWS, LANES), f32)],
        flops=4 * rows * shard_width * LANES,
    )
    ab = ab.reshape(shard_width, LANES)
    parts = shifts(part, nt)

    attended, kv = attend(False, lengths, came.reshape(-1, LANES), cache)
    everyone = exchange(attended, CHIPS)

    share = call(
        close_kernel,
        shape(ROLLS * CHIP_COUNT, 2 * LANES),
        [VMEM] * 4,
        (everyone, w_cols, w_cols_other, ab),
        scratch=[pltpu.VMEM((CHIP_COUNT * ROLLS * HEADS_TP, LANES), f32)],
    )
    share, weighted = together(share, weighted)
    shares = shifts(share, nt)

    low_back, joined, kept, given = call(
        gradient_kernel,
        (
            shape(rows, LANES, dtype=bf16),
            shape(ROLLS * CHIP_COUNT + LANES, LANES),
            shape(CHIP_COUNT, PIECE, LANES),
            shape(CHIP_COUNT, PIECE, LANES),
        ),
        [VMEM] * 7,
        (*parts, attention_rows, weighted, state),
        flops=4 * rows * shard_width * LANES,
    )

    sent = call(
        qkv_later_kernel,
        shape(CHIP_COUNT * QKV_ROWS, LANES),
        [VMEM] * 7,
        (joined, gain, w_both, *shares),
    )
    sent, low_back, left_far, right_far = together(sent, low_back, left, right)
    came = exchange(sent.reshape(CHIP_COUNT, QKV_ROWS, LANES), CHIPS)

    far_a = shift(left_far[:half], 1, nt)
    far_b = shift(right_far[half:], nt - 1, nt)
    kept = kept + swapped(given)

    attended, owned = attend(True, lengths, came.reshape(-1, LANES), cache, kv, ab)
    attended, kept = together(attended, kept)
    summed = exchange(kept, CHIPS)
    adapted, cols = output_rows(
        where,
        attention_rows,
        left,
        right,
        far_a,
        far_b,
        w_block,
        low_back,
        ab,
        shifts(attended, nt),
        owned,
    )
    arriving = shifts(cols, nt)
    arriving[1], summed = together(arriving[1], summed)
    summed = summed.sum(axis=0)
    decoded = call(place_kernel, shape(ROLLS, width), [VMEM] * nt, tuple(arriving))
    grad_a = summed[:, :RANK].T[:, None, :]
    grad_b = summed[:, RANK:].T[:, None, :]
    return (decoded, adapted, grad_a, grad_b)


def solution(mesh):
    split = Mesh(mesh.devices.reshape(4, 8, 2, 4), ("y", "z", "c", "t"))
    placed = (
        P(DP, None),
        P(),
        P(DP, "t", None),
        P(DP, None, "t", None),
        P(DP),
        P("t", None, DP),
        P(None, "t", DP),
        P(None, "t", DP),
        P(DP, "t"),
        P(DP, "t"),
        P(DP),
        P(DP),
        P(DP),
    )
    return jax.shard_map(
        shards,
        mesh=split,
        in_specs=placed,
        out_specs=(P(DP, None), P(DP, "t"), P(None, "t", DP), P(None, "t", DP)),
        check_vma=False,
    )
```
